32 devices in a mesh: dp: 8 (over z, y), ctx: 2 (over x), tensor: 2 (over core).
Axes of the slice: x: 2, y: 2, z: 4, core: 2. Of those that a mesh axis runs over, the one named last changes fastest.
Arguments:
- block_input: bfloat16 [8, 384, 1024], P('dp', 'ctx'), may hold values from -6 to 6
- attn_gain: float32 [1024], replicated, may hold values from 0.1 to 1.9
- query_weight: bfloat16 [1024, 2048], P('dp', 'tensor'), may hold values from -0.1875 to 0.1875
- key_weight: bfloat16 [1024, 1024], P('dp', 'tensor'), may hold values from -0.1875 to 0.1875
- value_weight: bfloat16 [1024, 1024], P('dp', 'tensor'), may hold values from -0.1875 to 0.1875
- query_gain: float32 [128], replicated, may hold values from 0.5 to 12
- key_gain: float32 [128], replicated, may hold values from 0.5 to 12
- output_weight: bfloat16 [2048, 1024], P('tensor', 'dp'), may hold values from -1 to 1
- mlp_gain: float32 [1024], replicated, may hold values from 0.1 to 1.9
- gate_weight: bfloat16 [1024, 3072], P('dp', 'tensor'), may hold values from -0.1875 to 0.1875
- up_weight: bfloat16 [1024, 3072], P('dp', 'tensor'), may hold values from -0.1875 to 0.1875
- down_weight: bfloat16 [3072, 1024], P('tensor', 'dp'), may hold values from -0.109375 to 0.109375
- cotangent: bfloat16 [8, 384, 1024], P('dp', 'ctx'), may hold values from -6 to 6
Outputs:
- block_output: bfloat16 [8, 384, 1024], P('dp', 'ctx')
- input_grad: bfloat16 [8, 384, 1024], P('dp', 'ctx')
- attn_gain_grad: float32 [1024], P('dp')
- query_weight_grad: float32 [1024, 2048], P('dp', 'tensor')
- key_weight_grad: float32 [1024, 1024], P('dp', 'tensor')
- value_weight_grad: float32 [1024, 1024], P('dp', 'tensor')
- query_gain_grad: float32 [128], P('dp')
- key_gain_grad: float32 [128], P('dp')
- output_weight_grad: float32 [2048, 1024], P('tensor', 'dp')
- mlp_gain_grad: float32 [1024], P('dp')
- gate_weight_grad: float32 [1024, 3072], P('dp', 'tensor')
- up_weight_grad: float32 [1024, 3072], P('dp', 'tensor')
- down_weight_grad: float32 [3072, 1024], P('tensor', 'dp')
The draws below stay inside these ranges and needn't reach their ends.
All inputs are finite; a program needn't handle non-finite values.
Results may differ from the reference program's by a relative error of at most 0.015.
The reference program's roundings to bfloat16 on the way count: a program that leaves them out, or rounds other values in their place, can miss the bound.
Values may be sent and summed in bfloat16 or wider, within the bound.
A program may use at most 128 MiB of HBM per device.

```python
import math
import jax
import jax.numpy as jnp
from jax import lax

D = 1024
HEADS = 16
KVH = 8
HD = 128
FF = 3072
BLK = 192
LEN = 384
SEQS = 8
N_CTX = 2


def spread_gain(key, salt):
    level = jax.random.uniform(jax.random.fold_in(key, salt), (HD,), jnp.float32, -0.6931, 0.6931)
    return jnp.exp(level)


def draw_query_gain(key, part):
    values = spread_gain(key, 1)
    return values


def draw_key_gain(key, part):
    values = spread_gain(key, 3)
    return values


def steps_of(key, dims, cuts, low, largest):
    level, own = 1.0, jax.random.fold_in(key, 6)
    for axis_at, parts in cuts:
        steps = jnp.exp(jax.random.uniform(jax.random.fold_in(own, axis_at), (parts,), jnp.float32, low / len(cuts), largest / len(cuts)))
        level = level * jnp.repeat(steps, dims[axis_at] // parts).reshape([-1 if axis == axis_at else 1 for axis in range(len(dims))])
    return level


def scatter_about(key, dims, spread, reach, cuts=(), kind=jnp.bfloat16):
    values = jax.random.normal(key, dims, jnp.float32) * spread
    if len(cuts) > 0:
        values = steps_of(key, dims, cuts, -0.22, 0.18) * values
    return jnp.clip(values, min=-reach, max=reach).astype(kind)


def setup_inputs(seed: int = 0) -> dict:
    key_list = jax.random.split(jax.random.key(seed), 14)
    return {
        "block_input": scatter_about(key_list[0], (SEQS, LEN, D), 1.0, 6.0, ((0, 8), (1, 2))),
        "attn_gain": jnp.clip(1.0 + 0.18 * jax.random.normal(key_list[1], (D,), jnp.float32), 0.1, 1.9),
        "query_weight": scatter_about(key_list[2], (D, HEADS * HD), D ** -0.5, 0.1875, ((0, 8), (1, 2))),
        "key_weight": scatter_about(key_list[3], (D, KVH * HD), D ** -0.5, 0.1875, ((0, 8), (1, 2))),
        "value_weight": scatter_about(key_list[4], (D, KVH * HD), D ** -0.5, 0.1875, ((0, 8), (1, 2))),
        "query_gain": draw_query_gain(jax.random.fold_in(key_list[13], 71), 0),
        "key_gain": draw_key_gain(jax.random.fold_in(key_list[13], 71), 0),
        "output_weight": scatter_about(key_list[7], (HEADS * HD, D), (max(1, 6 * HEADS * HD // (BLK * N_CTX))) ** -0.5, 1.0, ((0, 2), (1, 8))),
        "mlp_gain": jnp.clip(1.0 + 0.18 * jax.random.normal(key_list[8], (D,), jnp.float32), 0.1, 1.9),
        "gate_weight": scatter_about(key_list[9], (D, FF), D ** -0.5, 0.1875, ((0, 8), (1, 2))),
        "up_weight": scatter_about(key_list[10], (D, FF), D ** -0.5, 0.1875, ((0, 8), (1, 2))),
        "down_weight": scatter_about(key_list[11], (FF, D), FF ** -0.5, 0.109375, ((0, 2), (1, 8))),
        "cotangent": scatter_about(key_list[12], (SEQS, LEN, D), 1.0, 6.0, ((0, 8), (1, 2))),
    }


EPS = 1e-06
THETA = 1000000.0
F32 = jnp.float32
BF16 = jnp.bfloat16

def rounded(value):
    return lax.optimization_barrier(value.astype(BF16)).astype(F32)

def rms_inverse(value):
    return lax.rsqrt(lax.optimization_barrier(jnp.mean(value * value, axis=-1, keepdims=True)) + EPS)

def norm_back(grad, unit, inverse, gain):
    scaled = grad * gain
    return inverse * (scaled - unit * lax.optimization_barrier(jnp.mean(scaled * unit, axis=-1, keepdims=True)))

def rotate(value):
    half_width = value.shape[-1] // 2
    return jnp.concatenate([-value[..., half_width:], value[..., :half_width]], axis=-1)

def rotate_back(value):
    half_width = value.shape[-1] // 2
    return jnp.concatenate([value[..., half_width:], -value[..., :half_width]], axis=-1)

def rope_tables(positions, width):
    half_width = width // 2
    exponent = jnp.arange(half_width).astype(F32) * (2.0 / width)
    frequency = jnp.power(THETA, -exponent)
    angle = positions.astype(F32)[:, None] * frequency[None, :]
    angle = jnp.concatenate([angle, angle], axis=-1)
    return (jnp.cos(angle), jnp.sin(angle))

def one_sequence(x_seq, dy_seq, params):
    attn_gain, w_query, w_key, w_value, query_gain, key_gain, w_out, mlp_gain, w_gate, w_up, w_down = params
    length = x_seq.shape[0]
    group_size = HEADS // KVH
    score_scale = 1.0 / math.sqrt(HD)
    positions = jnp.arange(length).astype(jnp.int32)
    cos_table, sin_table = rope_tables(positions, HD)
    cos_heads = cos_table[:, None, :]
    sin_heads = sin_table[:, None, :]
    tokens = x_seq.astype(F32)
    inv_one = rms_inverse(tokens)
    unit_one = tokens * inv_one
    normed_one = (unit_one * attn_gain).astype(BF16)
    query = jnp.dot(normed_one, w_query, preferred_element_type=F32).reshape(length, HEADS, HD)
    key_raw = jnp.dot(normed_one, w_key, preferred_element_type=F32).reshape(length, KVH, HD)
    value = jnp.dot(normed_one, w_value, preferred_element_type=F32).astype(BF16).reshape(length, KVH, HD)
    query_inv = rms_inverse(query)
    query_unit = query * query_inv
    query_scaled = query_unit * query_gain
    query_rot = (query_scaled * cos_heads + rotate(query_scaled) * sin_heads).astype(BF16)
    key_inv = rms_inverse(key_raw)
    key_unit = key_raw * key_inv
    key_scaled = key_unit * key_gain
    key_rot = (key_scaled * cos_heads + rotate(key_scaled) * sin_heads).astype(BF16)
    q_heads = query_rot.reshape(length, KVH, group_size, HD).transpose(1, 2, 0, 3)
    k_heads = key_rot.transpose(1, 0, 2)
    v_heads = value.transpose(1, 0, 2)
    allowed = positions[:, None] >= positions[None, :]

    def head_scores(q_one, k_one):
        raw_scores = jnp.einsum('gqd,nd->gqn', q_one.astype(F32), k_one.astype(F32)) * score_scale
        return jnp.where(allowed[None], raw_scores, -jnp.inf)

    def head_forward(item):
        q_one, k_one, v_one = item
        scores = head_scores(q_one, k_one)
        row_peak = lax.optimization_barrier(jnp.max(scores, axis=-1))
        expo = jnp.exp(scores - row_peak[..., None])
        row_total = lax.optimization_barrier(jnp.sum(expo, axis=-1))
        mixed = jnp.einsum('gqn,nd->gqd', rounded(expo), v_one.astype(F32)) / row_total[..., None]
        return (mixed.astype(BF16), row_peak + jnp.log(row_total))
    attn_heads, log_total = lax.map(head_forward, (q_heads, k_heads, v_heads))
    attn = attn_heads.transpose(2, 0, 1, 3).reshape(length, HEADS * HD)
    resid = tokens + jnp.dot(attn, w_out, preferred_element_type=F32)
    inv_two = rms_inverse(resid)
    unit_two = resid * inv_two
    normed_two = (unit_two * mlp_gain).astype(BF16)
    gate = jnp.dot(normed_two, w_gate, preferred_element_type=F32)
    up_proj = jnp.dot(normed_two, w_up, preferred_element_type=F32)
    sigma = jax.nn.sigmoid(gate)
    silu_gate = gate * sigma
    hidden = (silu_gate * up_proj).astype(BF16)
    output = (resid + jnp.dot(hidden, w_down, preferred_element_type=F32)).astype(BF16)
    d_hidden = jnp.dot(dy_seq, w_down.T, preferred_element_type=F32)
    grad_down = jnp.dot(hidden.T, dy_seq, preferred_element_type=F32)
    d_gate = (d_hidden * up_proj * sigma * (1.0 + gate * (1.0 - sigma))).astype(BF16)
    d_up = (d_hidden * silu_gate).astype(BF16)
    grad_gate = jnp.dot(normed_two.T, d_gate, preferred_element_type=F32)
    grad_up = jnp.dot(normed_two.T, d_up, preferred_element_type=F32)
    d_normed_two = jnp.dot(d_gate, w_gate.T, preferred_element_type=F32) + jnp.dot(d_up, w_up.T, preferred_element_type=F32)
    grad_mlp_gain = lax.optimization_barrier(jnp.sum(d_normed_two * unit_two, axis=0))
    d_resid = dy_seq.astype(F32) + norm_back(d_normed_two, unit_two, inv_two, mlp_gain)
    d_resid_b = d_resid.astype(BF16)
    grad_out = jnp.dot(attn.T, d_resid_b, preferred_element_type=F32)
    d_attn = jnp.dot(d_resid_b, w_out.T, preferred_element_type=F32).astype(BF16)
    delta = lax.optimization_barrier(jnp.sum(d_attn.astype(F32).reshape(length, HEADS, HD) * attn.astype(F32).reshape(length, HEADS, HD), axis=-1))
    da_heads = d_attn.reshape(length, KVH, group_size, HD).transpose(1, 2, 0, 3)
    delta_heads = delta.reshape(length, KVH, group_size).transpose(1, 2, 0)

    def head_backward(item):
        q_one, k_one, v_one, da_one, lse_one, delta_one = item
        scores = head_scores(q_one, k_one)
        probs = jnp.exp(scores - lse_one[..., None])
        d_probs = jnp.einsum('gqd,nd->gqn', da_one.astype(F32), v_one.astype(F32))
        d_scores = rounded(probs * (d_probs - delta_one[..., None]) * score_scale)
        d_q = jnp.einsum('gqn,nd->gqd', d_scores, k_one.astype(F32))
        d_k = jnp.einsum('gqn,gqd->nd', d_scores, q_one.astype(F32))
        d_v = jnp.einsum('gqn,gqd->nd', rounded(probs), da_one.astype(F32))
        return (d_q, d_k, d_v)
    dq_heads, dk_heads, dv_heads = lax.map(head_backward, (q_heads, k_heads, v_heads, da_heads, log_total, delta_heads))
    d_query_rot = dq_heads.transpose(2, 0, 1, 3).reshape(length, HEADS, HD)
    d_key_rot = dk_heads.transpose(1, 0, 2)
    d_value = dv_heads.transpose(1, 0, 2).reshape(length, KVH * HD).astype(BF16)
    d_query_scaled = d_query_rot * cos_heads + rotate_back(d_query_rot * sin_heads)
    d_key_scaled = d_key_rot * cos_heads + rotate_back(d_key_rot * sin_heads)
    grad_query_gain = lax.optimization_barrier(jnp.sum(d_query_scaled * query_unit, axis=(0, 1)))
    grad_key_gain = lax.optimization_barrier(jnp.sum(d_key_scaled * key_unit, axis=(0, 1)))
    d_query = norm_back(d_query_scaled, query_unit, query_inv, query_gain).astype(BF16).reshape(length, HEADS * HD)
    d_key = norm_back(d_key_scaled, key_unit, key_inv, key_gain).astype(BF16).reshape(length, KVH * HD)
    grad_query = jnp.dot(normed_one.T, d_query, preferred_element_type=F32)
    grad_key = jnp.dot(normed_one.T, d_key, preferred_element_type=F32)
    grad_value = jnp.dot(normed_one.T, d_value, preferred_element_type=F32)
    d_normed_one = jnp.dot(d_query, w_query.T, preferred_element_type=F32)
    d_normed_one = d_normed_one + jnp.dot(d_key, w_key.T, preferred_element_type=F32)
    d_normed_one = d_normed_one + jnp.dot(d_value, w_value.T, preferred_element_type=F32)
    grad_attn_gain = lax.optimization_barrier(jnp.sum(d_normed_one * unit_one, axis=0))
    d_input = (d_resid + norm_back(d_normed_one, unit_one, inv_one, attn_gain)).astype(BF16)
    grads = (grad_attn_gain, grad_query, grad_key, grad_value, grad_query_gain, grad_key_gain, grad_out, grad_mlp_gain, grad_gate, grad_up, grad_down)
    return (output, d_input, grads)

def zeros_like_float(weight):
    return jnp.zeros(weight.shape, F32)

def reference(block_input, attn_gain, query_weight, key_weight, value_weight, query_gain, key_gain, output_weight, mlp_gain, gate_weight, up_weight, down_weight, cotangent):
    params = (attn_gain, query_weight, key_weight, value_weight, query_gain, key_gain, output_weight, mlp_gain, gate_weight, up_weight, down_weight)
    start_grads = jax.tree.map(zeros_like_float, params)

    def step_sequence(carry, item):
        x_seq, dy_seq = item
        output, d_input, grads = one_sequence(x_seq, dy_seq, params)
        return (jax.tree.map(jnp.add, carry, grads), (output, d_input))
    totals, stacked = lax.scan(step_sequence, start_grads, (block_input, cotangent))
    outputs, d_inputs = stacked
    return (outputs, d_inputs, totals[0], totals[1], totals[2], totals[3], totals[4], totals[5], totals[6], totals[7], totals[8], totals[9], totals[10])
```

```python
import functools
import math

import jax
import jax.numpy as jnp
from jax import lax
from jax.sharding import PartitionSpec as P

HD = 128


EPS = 1e-06
THETA = 1000000.0
F32 = jnp.float32
BF16 = jnp.bfloat16


def rms_inverse(value):
    return lax.rsqrt(jnp.mean(value * value, axis=-1, keepdims=True) + EPS)


def norm_back(grad, unit, inverse, gain):
    scaled = grad * gain
    return inverse * (scaled - unit * jnp.mean(scaled * unit, axis=-1, keepdims=True))


def rotate(value):
    half_width = value.shape[-1] // 2
    return jnp.concatenate([-value[..., half_width:], value[..., :half_width]], axis=-1)


def rotate_back(value):
    half_width = value.shape[-1] // 2
    return jnp.concatenate([value[..., half_width:], -value[..., :half_width]], axis=-1)


def rope_tables(positions, width):
    half_width = width // 2
    exponent = jnp.arange(half_width).astype(F32) * (2.0 / width)
    frequency = jnp.power(THETA, -exponent)
    angle = positions.astype(F32)[:, None] * frequency[None, :]
    angle = jnp.concatenate([angle, angle], axis=-1)
    return (jnp.cos(angle), jnp.sin(angle))


def over_heads(partial_value):
    return lax.psum(partial_value, "tensor")


def per_device(
    block_input,
    attn_gain,
    query_weight,
    key_weight,
    value_weight,
    query_gain,
    key_gain,
    output_weight,
    mlp_gain,
    gate_weight,
    up_weight,
    down_weight,
    cotangent,
):
    tokens = block_input[0].astype(F32)
    row_count = tokens.shape[0]
    score_scale = 1.0 / math.sqrt(HD)
    positions = lax.axis_index("ctx") * row_count + jnp.arange(row_count, dtype=jnp.int32)
    cos_table, sin_table = rope_tables(positions, HD)
    cos_heads = cos_table[:, None, :]
    sin_heads = sin_table[:, None, :]
    w_query, w_key, w_value, w_out, w_gate, w_up, w_down = (
        lax.all_gather(query_weight, "dp", axis=0, tiled=True),
        lax.all_gather(key_weight, "dp", axis=0, tiled=True),
        lax.all_gather(value_weight, "dp", axis=0, tiled=True),
        lax.all_gather(output_weight, "dp", axis=1, tiled=True),
        lax.all_gather(gate_weight, "dp", axis=0, tiled=True),
        lax.all_gather(up_weight, "dp", axis=0, tiled=True),
        lax.all_gather(down_weight, "dp", axis=1, tiled=True),
    )
    q_heads = w_query.shape[1] // HD
    kv_heads = w_key.shape[1] // HD
    group_size = q_heads // kv_heads
    inv_one = rms_inverse(tokens)
    unit_one = tokens * inv_one
    normed_one = (unit_one * attn_gain).astype(BF16)
    query = jnp.dot(normed_one, w_query, preferred_element_type=F32).reshape(row_count, q_heads, HD)
    key_raw = jnp.dot(normed_one, w_key, preferred_element_type=F32).reshape(
        row_count, kv_heads, HD
    )
    value = (
        jnp.dot(normed_one, w_value, preferred_element_type=F32)
        .astype(BF16)
        .reshape(row_count, kv_heads, HD)
    )
    query_inv = rms_inverse(query)
    query_unit = query * query_inv
    query_scaled = query_unit * query_gain
    query_rot = (query_scaled * cos_heads + rotate(query_scaled) * sin_heads).astype(BF16)
    key_inv = rms_inverse(key_raw)
    key_unit = key_raw * key_inv
    key_scaled = key_unit * key_gain
    key_rot = (key_scaled * cos_heads + rotate(key_scaled) * sin_heads).astype(BF16)
    grouped_query = query_rot.reshape(row_count, kv_heads, group_size, HD)

    def piece_scores(piece_keys):
        piece_rows = piece_keys.shape[0]
        key_positions = jnp.arange(piece_rows, dtype=jnp.int32)
        allowed = key_positions[None, :] <= positions[:, None]
        scores = (
            jnp.einsum("qkgd,nkd->kgqn", grouped_query, piece_keys, preferred_element_type=F32)
            * score_scale
        )
        return jnp.where(allowed, scores, -jnp.inf)

    peak_old = jnp.full((kv_heads, group_size, row_count), -1e30, F32)
    piece_keys = lax.all_gather(key_rot, "ctx", axis=0, tiled=True)
    piece_values = lax.all_gather(value, "ctx", axis=0, tiled=True)
    scores = piece_scores(piece_keys)
    peak_new = jnp.maximum(peak_old, jnp.max(scores, axis=-1))
    expo = jnp.exp(scores - peak_new[..., None])
    total_new = jnp.sum(expo, axis=-1)
    accum_new = jnp.einsum(
        "kgqn,nkd->kgqd", expo.astype(BF16), piece_values, preferred_element_type=F32
    )
    log_total = peak_new + jnp.log(total_new)
    attn = (
        (accum_new / total_new[..., None])
        .astype(BF16)
        .transpose(2, 0, 1, 3)
        .reshape(row_count, q_heads * HD)
    )
    resid = tokens + over_heads(jnp.dot(attn, w_out, preferred_element_type=F32))
    inv_two = rms_inverse(resid)
    unit_two = resid * inv_two
    normed_two = (unit_two * mlp_gain).astype(BF16)
    gate = jnp.dot(normed_two, w_gate, preferred_element_type=F32)
    up_proj = jnp.dot(normed_two, w_up, preferred_element_type=F32)
    sigma = jax.nn.sigmoid(gate)
    silu_gate = gate * sigma
    hidden = (silu_gate * up_proj).astype(BF16)
    output = (resid + over_heads(jnp.dot(hidden, w_down, preferred_element_type=F32))).astype(BF16)
    w_query, w_key, w_value, w_out, w_gate, w_up, w_down = (
        lax.all_gather(query_weight, "dp", axis=0, tiled=True),
        lax.all_gather(key_weight, "dp", axis=0, tiled=True),
        lax.all_gather(value_weight, "dp", axis=0, tiled=True),
        lax.all_gather(output_weight, "dp", axis=1, tiled=True),
        lax.all_gather(gate_weight, "dp", axis=0, tiled=True),
        lax.all_gather(up_weight, "dp", axis=0, tiled=True),
        lax.all_gather(down_weight, "dp", axis=1, tiled=True),
    )
    d_output = cotangent[0]
    d_hidden = jnp.einsum("td,fd->tf", d_output, w_down, preferred_element_type=F32)
    grad_down = jnp.einsum("tf,td->fd", hidden, d_output, preferred_element_type=F32)
    d_gate = (d_hidden * up_proj * sigma * (1.0 + gate * (1.0 - sigma))).astype(BF16)
    d_up = (d_hidden * silu_gate).astype(BF16)
    grad_gate = jnp.einsum("td,tf->df", normed_two, d_gate, preferred_element_type=F32)
    grad_up = jnp.einsum("td,tf->df", normed_two, d_up, preferred_element_type=F32)
    partial_two = jnp.einsum("tf,df->td", d_gate, w_gate, preferred_element_type=F32) + jnp.einsum(
        "tf,df->td", d_up, w_up, preferred_element_type=F32
    )
    d_normed_two = lax.psum(partial_two, "tensor")
    grad_mlp_gain = jnp.sum(d_normed_two * unit_two, axis=0)
    d_resid = d_output.astype(F32) + norm_back(d_normed_two, unit_two, inv_two, mlp_gain)
    d_resid_b = d_resid.astype(BF16)
    grad_out = jnp.einsum("th,td->hd", attn, d_resid_b, preferred_element_type=F32)
    d_attn = jnp.einsum("td,hd->th", d_resid_b, w_out, preferred_element_type=F32).astype(BF16)
    delta = jnp.sum(
        d_attn.astype(F32).reshape(row_count, q_heads, HD)
        * attn.astype(F32).reshape(row_count, q_heads, HD),
        axis=-1,
    )
    delta_heads = delta.reshape(row_count, kv_heads, group_size).transpose(1, 2, 0)
    grouped_grad = d_attn.reshape(row_count, kv_heads, group_size, HD)
    piece_keys = lax.all_gather(key_rot, "ctx", axis=0, tiled=True)
    piece_values = lax.all_gather(value, "ctx", axis=0, tiled=True)
    piece_rows = piece_keys.shape[0]
    scores = piece_scores(piece_keys)
    probs = jnp.exp(scores - log_total[..., None])
    d_probs = jnp.einsum("qkgd,nkd->kgqn", grouped_grad, piece_values, preferred_element_type=F32)
    d_scores = (probs * (d_probs - delta_heads[..., None]) * score_scale).astype(BF16)
    d_query_acc = jnp.einsum("kgqn,nkd->kgqd", d_scores, piece_keys, preferred_element_type=F32)
    d_key_piece = jnp.einsum("kgqn,qkgd->nkd", d_scores, grouped_query, preferred_element_type=F32)
    d_value_piece = jnp.einsum(
        "kgqn,qkgd->nkd", probs.astype(BF16), grouped_grad, preferred_element_type=F32
    )
    update = jnp.stack([d_key_piece, d_value_piece])
    d_kv_home = lax.psum_scatter(update, "ctx", scatter_dimension=1, tiled=True)
    d_query_rot = d_query_acc.transpose(2, 0, 1, 3).reshape(row_count, q_heads, HD)
    d_key_rot = d_kv_home[0]
    d_value = d_kv_home[1].astype(BF16).reshape(row_count, kv_heads * HD)
    d_query_scaled = d_query_rot * cos_heads + rotate_back(d_query_rot * sin_heads)
    d_key_scaled = d_key_rot * cos_heads + rotate_back(d_key_rot * sin_heads)
    query_gain_part = jnp.sum(d_query_scaled * query_unit, axis=(0, 1))
    key_gain_part = jnp.sum(d_key_scaled * key_unit, axis=(0, 1))
    d_query = (
        norm_back(d_query_scaled, query_unit, query_inv, query_gain)
        .astype(BF16)
        .reshape(row_count, q_heads * HD)
    )
    d_key = (
        norm_back(d_key_scaled, key_unit, key_inv, key_gain)
        .astype(BF16)
        .reshape(row_count, kv_heads * HD)
    )
    grad_query = jnp.einsum("td,th->dh", normed_one, d_query, preferred_element_type=F32)
    grad_key = jnp.einsum("td,th->dh", normed_one, d_key, preferred_element_type=F32)
    grad_value = jnp.einsum("td,th->dh", normed_one, d_value, preferred_element_type=F32)
    partial_one = jnp.einsum("th,dh->td", d_query, w_query, preferred_element_type=F32)
    partial_one = partial_one + jnp.einsum("th,dh->td", d_key, w_key, preferred_element_type=F32)
    partial_one = partial_one + jnp.einsum(
        "th,dh->td", d_value, w_value, preferred_element_type=F32
    )
    d_normed_one, query_gain_heads, key_gain_heads = lax.psum(
        (partial_one, query_gain_part, key_gain_part), "tensor"
    )
    grad_attn_gain = jnp.sum(d_normed_one * unit_one, axis=0)
    d_input = (d_resid + norm_back(d_normed_one, unit_one, inv_one, attn_gain)).astype(BF16)
    (
        share_a,
        share_q,
        share_k,
        share_v,
        share_qg,
        share_kg,
        share_o,
        share_m,
        share_g,
        share_u,
        share_d,
    ) = (
        lax.psum_scatter(grad_attn_gain, "dp", scatter_dimension=0, tiled=True),
        lax.psum_scatter(grad_query, "dp", scatter_dimension=0, tiled=True),
        lax.psum_scatter(grad_key, "dp", scatter_dimension=0, tiled=True),
        lax.psum_scatter(grad_value, "dp", scatter_dimension=0, tiled=True),
        lax.psum_scatter(query_gain_heads, "dp", scatter_dimension=0, tiled=True),
        lax.psum_scatter(key_gain_heads, "dp", scatter_dimension=0, tiled=True),
        lax.psum_scatter(grad_out, "dp", scatter_dimension=1, tiled=True),
        lax.psum_scatter(grad_mlp_gain, "dp", scatter_dimension=0, tiled=True),
        lax.psum_scatter(grad_gate, "dp", scatter_dimension=0, tiled=True),
        lax.psum_scatter(grad_up, "dp", scatter_dimension=0, tiled=True),
        lax.psum_scatter(grad_down, "dp", scatter_dimension=1, tiled=True),
    )
    finals = lax.psum(
        (
            share_a,
            share_q,
            share_k,
            share_v,
            share_qg,
            share_kg,
            share_o,
            share_m,
            share_g,
            share_u,
            share_d,
        ),
        "ctx",
    )
    return (
        output[None],
        d_input[None],
        finals[0],
        finals[1],
        finals[2],
        finals[3],
        finals[4],
        finals[5],
        finals[6],
        finals[7],
        finals[8],
        finals[9],
        finals[10],
    )


def tree_exchange(value, axis_name, axis_size):
    return lax.ppermute(value, axis_name, [(i, i ^ 1) for i in range(axis_size)])


def plane_device(
    dp_size,
    block_input,
    attn_gain,
    query_weight,
    key_weight,
    value_weight,
    query_gain,
    key_gain,
    output_weight,
    mlp_gain,
    gate_weight,
    up_weight,
    down_weight,
    cotangent,
):
    line = dp_size // 2
    line_groups = [[2 * j + side for j in range(line)] for side in range(2)]
    side = lax.axis_index("dp") % 2
    block = lax.axis_index("ctx")
    core = lax.axis_index("tensor")
    owned = query_weight.shape[0]
    width = owned * dp_size
    mine = 2 * block + side
    rows = block_input.shape[1]
    half = width // 2
    score_scale = 1.0 / math.sqrt(HD)

    def to_ctx(value):
        return tree_exchange(value, "ctx", 2)

    def to_pair(value):
        return tree_exchange(value, "dp", dp_size)

    def to_core(value):
        return tree_exchange(value, "tensor", 2)

    def to_diagonal(value):
        steps = [(i, i ^ 3) for i in range(2 * dp_size)]
        return lax.ppermute(value, ("dp", "ctx"), steps)

    def core_half(value):
        return lax.dynamic_slice_in_dim(value, core * half, half, axis=-1)

    def both_halves(own, other):
        return jnp.where(
            core == 0,
            jnp.concatenate([own, other], axis=-1),
            jnp.concatenate([other, own], axis=-1),
        )

    def gather_tokens(value):
        own = core_half(value)
        parts = jnp.concatenate([to_ctx(own), to_pair(own), to_diagonal(own)], axis=0)
        parts = both_halves(parts, to_core(parts))
        return jnp.concatenate([value, parts], axis=0)

    def scatter_tokens(partial_value):
        own = core_half(partial_value)
        other = lax.dynamic_slice_in_dim(partial_value, (1 - core) * half, half, axis=-1)
        own = (own + to_core(other)).reshape(4, rows, half)
        total = own[0] + to_ctx(own[1]) + to_pair(own[2]) + to_diagonal(own[3])
        return both_halves(total, to_core(total))

    def quarter(weight, which):
        part = weight.shape[1] // 4
        return lax.dynamic_slice_in_dim(weight, which * part, part, axis=1)

    def gather_weights(weights):
        keep = jnp.concatenate([quarter(w, mine) for w in weights], axis=1)
        send = jnp.concatenate([quarter(w, 2 * block + 1 - side) for w in weights], axis=1)
        found = to_pair(send)
        both = jnp.where(
            side == 0,
            jnp.concatenate([keep, found], axis=0),
            jnp.concatenate([found, keep], axis=0),
        )
        return lax.all_gather(both, "dp", axis_index_groups=line_groups, axis=0, tiled=True)

    def weight_share(features, columns):
        part = jnp.einsum("td,tf->df", features, columns, preferred_element_type=F32)
        share = lax.psum_scatter(
            part, "dp", axis_index_groups=line_groups, scatter_dimension=0, tiled=True
        )
        return share

    def spread(share):
        own = lax.dynamic_slice_in_dim(share, side * owned, owned, axis=0)
        far = lax.dynamic_slice_in_dim(share, (1 - side) * owned, owned, axis=0)
        pieces = [own, to_pair(far), to_ctx(own), to_diagonal(far)]
        return pieces

    def whole(pieces, low, high):
        own, pair, ctx, diagonal = [piece[:, low:high] for piece in pieces]
        near = jnp.where(
            side == 0,
            jnp.concatenate([own, pair], axis=1),
            jnp.concatenate([pair, own], axis=1),
        )
        away = jnp.where(
            side == 0,
            jnp.concatenate([ctx, diagonal], axis=1),
            jnp.concatenate([diagonal, ctx], axis=1),
        )
        return jnp.where(
            block == 0,
            jnp.concatenate([near, away], axis=1),
            jnp.concatenate([away, near], axis=1),
        )

    def mul_t(value, weight):
        return jnp.einsum("tf,df->td", value, weight, preferred_element_type=F32)

    w_one = gather_weights([query_weight, key_weight, value_weight, output_weight.T])
    w_two = gather_weights([gate_weight, up_weight])
    w_down_t = gather_weights([down_weight.T])
    cut_q = query_weight.shape[1] // 4
    cut_k = cut_q + key_weight.shape[1] // 4
    cut_v = cut_k + value_weight.shape[1] // 4
    units = gate_weight.shape[1] // 4
    w_qkv, w_out_t = w_one[:, :cut_v], w_one[:, cut_v:]

    tokens = block_input[0].astype(F32)
    inv_one = rms_inverse(tokens)
    unit_one = tokens * inv_one
    normed_one = gather_tokens((unit_one * attn_gain).astype(BF16))
    d_output = cotangent[0]
    d_output_all = gather_tokens(d_output)

    group = query_weight.shape[1] // key_weight.shape[1]
    kv_heads = (cut_k - cut_q) // HD
    length = 2 * rows
    index = jnp.arange(rows, dtype=jnp.int32)
    positions = jnp.concatenate([block * rows + index, (1 - block) * rows + index])
    cos_table, sin_table = rope_tables(positions, HD)
    cos_q = jnp.concatenate([cos_table] * group, axis=0)
    sin_q = jnp.concatenate([sin_table] * group, axis=0)
    positions_q = jnp.concatenate([positions] * group)
    allowed = positions[None, :] <= positions_q[:, None]

    def split_heads(value):
        g = value.shape[1] // (kv_heads * HD)
        value = value.reshape(2, length, kv_heads, g, HD).transpose(0, 2, 3, 1, 4)
        return value.reshape(2 * kv_heads, g * length, HD)

    def join_heads(value):
        g = value.shape[1] // length
        value = value.reshape(2, kv_heads, g, length, HD).transpose(0, 3, 1, 2, 4)
        return value.reshape(2 * length, kv_heads * g * HD)

    qkv = jnp.dot(normed_one, w_qkv, preferred_element_type=F32)
    query = split_heads(qkv[:, :cut_q])
    key_raw = split_heads(qkv[:, cut_q:cut_k])
    value = split_heads(qkv[:, cut_k:].astype(BF16))
    query_inv = rms_inverse(query)
    query_unit = query * query_inv
    query_scaled = query_unit * query_gain
    query_rot = (query_scaled * cos_q + rotate(query_scaled) * sin_q).astype(BF16)
    key_inv = rms_inverse(key_raw)
    key_unit = key_raw * key_inv
    key_scaled = key_unit * key_gain
    key_rot = (key_scaled * cos_table + rotate(key_scaled) * sin_table).astype(BF16)
    scores = jnp.einsum("sqd,snd->sqn", query_rot, key_rot, preferred_element_type=F32)
    scores = jnp.where(allowed, scores * score_scale, -jnp.inf)
    peak = jnp.max(scores, axis=-1, keepdims=True)
    expo = jnp.exp(scores - peak)
    total = jnp.sum(expo, axis=-1, keepdims=True)
    accum = jnp.einsum("sqn,snd->sqd", expo.astype(BF16), value, preferred_element_type=F32)
    log_total = peak + jnp.log(total)
    attn_heads = (accum / total).astype(BF16)
    attn = join_heads(attn_heads)
    resid = tokens + scatter_tokens(mul_t(attn, w_out_t))
    inv_two = rms_inverse(resid)
    unit_two = resid * inv_two
    normed_two = gather_tokens((unit_two * mlp_gain).astype(BF16))
    gate_up = jnp.dot(normed_two, w_two, preferred_element_type=F32)
    gate, up_proj = gate_up[:, :units], gate_up[:, units:]
    sigma = jax.nn.sigmoid(gate)
    silu_gate = gate * sigma
    hidden = (silu_gate * up_proj).astype(BF16)

    share_down = weight_share(d_output_all, hidden)
    d_hidden = jnp.dot(d_output_all, w_down_t, preferred_element_type=F32)
    d_gate = (d_hidden * up_proj * sigma * (1.0 + gate * (1.0 - sigma))).astype(BF16)
    d_up = (d_hidden * silu_gate).astype(BF16)
    d_gate_up = jnp.concatenate([d_gate, d_up], axis=1)
    d_normed_two = scatter_tokens(mul_t(d_gate_up, w_two))
    share_mlp = weight_share(normed_two, d_gate_up)
    output = (resid + scatter_tokens(mul_t(hidden, w_down_t))).astype(BF16)
    grad_mlp_gain = jnp.sum(d_normed_two * unit_two, axis=0)
    d_resid = d_output.astype(F32) + norm_back(d_normed_two, unit_two, inv_two, mlp_gain)
    d_resid_all = gather_tokens(d_resid.astype(BF16))
    share_out = weight_share(d_resid_all, attn)
    d_attn = split_heads(jnp.dot(d_resid_all, w_out_t, preferred_element_type=F32).astype(BF16))
    delta = jnp.sum(d_attn.astype(F32) * attn_heads.astype(F32), axis=-1, keepdims=True)
    probs = jnp.exp(scores - log_total)
    d_probs = jnp.einsum("sqd,snd->sqn", d_attn, value, preferred_element_type=F32)
    d_scores = (probs * (d_probs - delta) * score_scale).astype(BF16)
    d_query_rot = jnp.einsum("sqn,snd->sqd", d_scores, key_rot, preferred_element_type=F32)
    d_key_rot = jnp.einsum("sqn,sqd->snd", d_scores, query_rot, preferred_element_type=F32)
    d_value = jnp.einsum("sqn,sqd->snd", probs.astype(BF16), d_attn, preferred_element_type=F32)
    d_query_scaled = d_query_rot * cos_q + rotate_back(d_query_rot * sin_q)
    d_key_scaled = d_key_rot * cos_table + rotate_back(d_key_rot * sin_table)
    query_gain_part = jnp.sum(d_query_scaled * query_unit, axis=(0, 1))
    key_gain_part = jnp.sum(d_key_scaled * key_unit, axis=(0, 1))
    d_query = norm_back(d_query_scaled, query_unit, query_inv, query_gain).astype(BF16)
    d_key = norm_back(d_key_scaled, key_unit, key_inv, key_gain).astype(BF16)
    d_qkv = jnp.concatenate(
        [join_heads(d_query), join_heads(d_key), join_heads(d_value.astype(BF16))], axis=1
    )
    share_qkv = weight_share(normed_one, d_qkv)
    d_normed_one = scatter_tokens(mul_t(d_qkv, w_qkv))
    grad_attn_gain = jnp.sum(d_normed_one * unit_one, axis=0)
    d_input = (d_resid + norm_back(d_normed_one, unit_one, inv_one, attn_gain)).astype(BF16)

    gains = jnp.concatenate(
        [0.5 * grad_attn_gain, 0.5 * grad_mlp_gain, query_gain_part, key_gain_part]
    )
    gains = gains + to_core(gains)
    gains = gains + to_ctx(gains)
    stride = 1
    while stride < dp_size:
        gains = gains + lax.ppermute(gains, "dp", [(i, i ^ stride) for i in range(dp_size)])
        stride *= 2
    owner = lax.axis_index("dp")

    def owned_gain(start, size):
        part = size // dp_size
        return lax.dynamic_slice_in_dim(gains, start + owner * part, part)

    down_pieces = spread(share_down)
    mlp_pieces = spread(share_mlp)
    out_pieces = spread(share_out)
    qkv_pieces = spread(share_qkv)
    return (
        output[None],
        d_input[None],
        owned_gain(0, width),
        whole(qkv_pieces, 0, cut_q),
        whole(qkv_pieces, cut_q, cut_k),
        whole(qkv_pieces, cut_k, cut_v),
        owned_gain(2 * width, HD),
        owned_gain(2 * width + HD, HD),
        whole(out_pieces, 0, share_out.shape[1]).T,
        owned_gain(width, width),
        whole(mlp_pieces, 0, units),
        whole(mlp_pieces, units, 2 * units),
        whole(down_pieces, 0, units).T,
    )


def solution(mesh):
    sizes = dict(mesh.shape)
    body = per_device
    if sizes["ctx"] == 2 and sizes["tensor"] == 2 and sizes["dp"] in (2, 4, 8, 16):
        body = functools.partial(plane_device, sizes["dp"])
    return jax.shard_map(
        body,
        mesh=mesh,
        in_specs=(
            P("dp", "ctx", None),
            P(),
            P("dp", "tensor"),
            P("dp", "tensor"),
            P("dp", "tensor"),
            P(),
            P(),
            P("tensor", "dp"),
            P(),
            P("dp", "tensor"),
            P("dp", "tensor"),
            P("tensor", "dp"),
            P("dp", "ctx", None),
        ),
        out_specs=(
            P("dp", "ctx", None),
            P("dp", "ctx", None),
            P("dp"),
            P("dp", "tensor"),
            P("dp", "tensor"),
            P("dp", "tensor"),
            P("dp"),
            P("dp"),
            P("tensor", "dp"),
            P("dp"),
            P("dp", "tensor"),
            P("dp", "tensor"),
            P("tensor", "dp"),
        ),
        check_vma=False,
    )
```

```python
import functools
import math

import jax
import jax.numpy as jnp
from jax import lax
from jax.experimental import pallas as pl
from jax.experimental.pallas import tpu as pltpu
from jax.sharding import PartitionSpec as P

HD = 128


EPS = 1e-06
THETA = 1000000.0
F32 = jnp.float32
BF16 = jnp.bfloat16


def rms_inverse(value):
    return lax.rsqrt(jnp.mean(value * value, axis=-1, keepdims=True) + EPS)


def norm_back(grad, unit, inverse, gain):
    scaled = grad * gain
    return inverse * (scaled - unit * jnp.mean(scaled * unit, axis=-1, keepdims=True))


def rotate(value):
    half_width = value.shape[-1] // 2
    return jnp.concatenate([-value[..., half_width:], value[..., :half_width]], axis=-1)


def rotate_back(value):
    half_width = value.shape[-1] // 2
    return jnp.concatenate([value[..., half_width:], -value[..., :half_width]], axis=-1)


def rope_tables(positions, width):
    half_width = width // 2
    exponent = jnp.arange(half_width).astype(F32) * (2.0 / width)
    frequency = jnp.power(THETA, -exponent)
    angle = positions.astype(F32)[:, None] * frequency[None, :]
    angle = jnp.concatenate([angle, angle], axis=-1)
    return (jnp.cos(angle), jnp.sin(angle))


def over_heads(partial_value):
    return lax.psum(partial_value, "tensor")


def per_device(
    block_input,
    attn_gain,
    query_weight,
    key_weight,
    value_weight,
    query_gain,
    key_gain,
    output_weight,
    mlp_gain,
    gate_weight,
    up_weight,
    down_weight,
    cotangent,
):
    tokens = block_input[0].astype(F32)
    row_count = tokens.shape[0]
    score_scale = 1.0 / math.sqrt(HD)
    positions = lax.axis_index("ctx") * row_count + jnp.arange(row_count, dtype=jnp.int32)
    cos_table, sin_table = rope_tables(positions, HD)
    cos_heads = cos_table[:, None, :]
    sin_heads = sin_table[:, None, :]
    w_query, w_key, w_value, w_out, w_gate, w_up, w_down = (
        lax.all_gather(query_weight, "dp", axis=0, tiled=True),
        lax.all_gather(key_weight, "dp", axis=0, tiled=True),
        lax.all_gather(value_weight, "dp", axis=0, tiled=True),
        lax.all_gather(output_weight, "dp", axis=1, tiled=True),
        lax.all_gather(gate_weight, "dp", axis=0, tiled=True),
        lax.all_gather(up_weight, "dp", axis=0, tiled=True),
        lax.all_gather(down_weight, "dp", axis=1, tiled=True),
    )
    q_heads = w_query.shape[1] // HD
    kv_heads = w_key.shape[1] // HD
    group_size = q_heads // kv_heads
    inv_one = rms_inverse(tokens)
    unit_one = tokens * inv_one
    normed_one = (unit_one * attn_gain).astype(BF16)
    query = jnp.dot(normed_one, w_query, preferred_element_type=F32).reshape(row_count, q_heads, HD)
    key_raw = jnp.dot(normed_one, w_key, preferred_element_type=F32).reshape(
        row_count, kv_heads, HD
    )
    value = (
        jnp.dot(normed_one, w_value, preferred_element_type=F32)
        .astype(BF16)
        .reshape(row_count, kv_heads, HD)
    )
    query_inv = rms_inverse(query)
    query_unit = query * query_inv
    query_scaled = query_unit * query_gain
    query_rot = (query_scaled * cos_heads + rotate(query_scaled) * sin_heads).astype(BF16)
    key_inv = rms_inverse(key_raw)
    key_unit = key_raw * key_inv
    key_scaled = key_unit * key_gain
    key_rot = (key_scaled * cos_heads + rotate(key_scaled) * sin_heads).astype(BF16)
    grouped_query = query_rot.reshape(row_count, kv_heads, group_size, HD)

    def piece_scores(piece_keys):
        piece_rows = piece_keys.shape[0]
        key_positions = jnp.arange(piece_rows, dtype=jnp.int32)
        allowed = key_positions[None, :] <= positions[:, None]
        scores = (
            jnp.einsum("qkgd,nkd->kgqn", grouped_query, piece_keys, preferred_element_type=F32)
            * score_scale
        )
        return jnp.where(allowed, scores, -jnp.inf)

    peak_old = jnp.full((kv_heads, group_size, row_count), -1e30, F32)
    piece_keys = lax.all_gather(key_rot, "ctx", axis=0, tiled=True)
    piece_values = lax.all_gather(value, "ctx", axis=0, tiled=True)
    scores = piece_scores(piece_keys)
    peak_new = jnp.maximum(peak_old, jnp.max(scores, axis=-1))
    expo = jnp.exp(scores - peak_new[..., None])
    total_new = jnp.sum(expo, axis=-1)
    accum_new = jnp.einsum(
        "kgqn,nkd->kgqd", expo.astype(BF16), piece_values, preferred_element_type=F32
    )
    log_total = peak_new + jnp.log(total_new)
    attn = (
        (accum_new / total_new[..., None])
        .astype(BF16)
        .transpose(2, 0, 1, 3)
        .reshape(row_count, q_heads * HD)
    )
    resid = tokens + over_heads(jnp.dot(attn, w_out, preferred_element_type=F32))
    inv_two = rms_inverse(resid)
    unit_two = resid * inv_two
    normed_two = (unit_two * mlp_gain).astype(BF16)
    gate = jnp.dot(normed_two, w_gate, preferred_element_type=F32)
    up_proj = jnp.dot(normed_two, w_up, preferred_element_type=F32)
    sigma = jax.nn.sigmoid(gate)
    silu_gate = gate * sigma
    hidden = (silu_gate * up_proj).astype(BF16)
    output = (resid + over_heads(jnp.dot(hidden, w_down, preferred_element_type=F32))).astype(BF16)
    w_query, w_key, w_value, w_out, w_gate, w_up, w_down = (
        lax.all_gather(query_weight, "dp", axis=0, tiled=True),
        lax.all_gather(key_weight, "dp", axis=0, tiled=True),
        lax.all_gather(value_weight, "dp", axis=0, tiled=True),
        lax.all_gather(output_weight, "dp", axis=1, tiled=True),
        lax.all_gather(gate_weight, "dp", axis=0, tiled=True),
        lax.all_gather(up_weight, "dp", axis=0, tiled=True),
        lax.all_gather(down_weight, "dp", axis=1, tiled=True),
    )
    d_output = cotangent[0]
    d_hidden = jnp.einsum("td,fd->tf", d_output, w_down, preferred_element_type=F32)
    grad_down = jnp.einsum("tf,td->fd", hidden, d_output, preferred_element_type=F32)
    d_gate = (d_hidden * up_proj * sigma * (1.0 + gate * (1.0 - sigma))).astype(BF16)
    d_up = (d_hidden * silu_gate).astype(BF16)
    grad_gate = jnp.einsum("td,tf->df", normed_two, d_gate, preferred_element_type=F32)
    grad_up = jnp.einsum("td,tf->df", normed_two, d_up, preferred_element_type=F32)
    partial_two = jnp.einsum("tf,df->td", d_gate, w_gate, preferred_element_type=F32) + jnp.einsum(
        "tf,df->td", d_up, w_up, preferred_element_type=F32
    )
    d_normed_two = lax.psum(partial_two, "tensor")
    grad_mlp_gain = jnp.sum(d_normed_two * unit_two, axis=0)
    d_resid = d_output.astype(F32) + norm_back(d_normed_two, unit_two, inv_two, mlp_gain)
    d_resid_b = d_resid.astype(BF16)
    grad_out = jnp.einsum("th,td->hd", attn, d_resid_b, preferred_element_type=F32)
    d_attn = jnp.einsum("td,hd->th", d_resid_b, w_out, preferred_element_type=F32).astype(BF16)
    delta = jnp.sum(
        d_attn.astype(F32).reshape(row_count, q_heads, HD)
        * attn.astype(F32).reshape(row_count, q_heads, HD),
        axis=-1,
    )
    delta_heads = delta.reshape(row_count, kv_heads, group_size).transpose(1, 2, 0)
    grouped_grad = d_attn.reshape(row_count, kv_heads, group_size, HD)
    piece_keys = lax.all_gather(key_rot, "ctx", axis=0, tiled=True)
    piece_values = lax.all_gather(value, "ctx", axis=0, tiled=True)
    piece_rows = piece_keys.shape[0]
    scores = piece_scores(piece_keys)
    probs = jnp.exp(scores - log_total[..., None])
    d_probs = jnp.einsum("qkgd,nkd->kgqn", grouped_grad, piece_values, preferred_element_type=F32)
    d_scores = (probs * (d_probs - delta_heads[..., None]) * score_scale).astype(BF16)
    d_query_acc = jnp.einsum("kgqn,nkd->kgqd", d_scores, piece_keys, preferred_element_type=F32)
    d_key_piece = jnp.einsum("kgqn,qkgd->nkd", d_scores, grouped_query, preferred_element_type=F32)
    d_value_piece = jnp.einsum(
        "kgqn,qkgd->nkd", probs.astype(BF16), grouped_grad, preferred_element_type=F32
    )
    update = jnp.stack([d_key_piece, d_value_piece])
    d_kv_home = lax.psum_scatter(update, "ctx", scatter_dimension=1, tiled=True)
    d_query_rot = d_query_acc.transpose(2, 0, 1, 3).reshape(row_count, q_heads, HD)
    d_key_rot = d_kv_home[0]
    d_value = d_kv_home[1].astype(BF16).reshape(row_count, kv_heads * HD)
    d_query_scaled = d_query_rot * cos_heads + rotate_back(d_query_rot * sin_heads)
    d_key_scaled = d_key_rot * cos_heads + rotate_back(d_key_rot * sin_heads)
    query_gain_part = jnp.sum(d_query_scaled * query_unit, axis=(0, 1))
    key_gain_part = jnp.sum(d_key_scaled * key_unit, axis=(0, 1))
    d_query = (
        norm_back(d_query_scaled, query_unit, query_inv, query_gain)
        .astype(BF16)
        .reshape(row_count, q_heads * HD)
    )
    d_key = (
        norm_back(d_key_scaled, key_unit, key_inv, key_gain)
        .astype(BF16)
        .reshape(row_count, kv_heads * HD)
    )
    grad_query = jnp.einsum("td,th->dh", normed_one, d_query, preferred_element_type=F32)
    grad_key = jnp.einsum("td,th->dh", normed_one, d_key, preferred_element_type=F32)
    grad_value = jnp.einsum("td,th->dh", normed_one, d_value, preferred_element_type=F32)
    partial_one = jnp.einsum("th,dh->td", d_query, w_query, preferred_element_type=F32)
    partial_one = partial_one + jnp.einsum("th,dh->td", d_key, w_key, preferred_element_type=F32)
    partial_one = partial_one + jnp.einsum(
        "th,dh->td", d_value, w_value, preferred_element_type=F32
    )
    d_normed_one, query_gain_heads, key_gain_heads = lax.psum(
        (partial_one, query_gain_part, key_gain_part), "tensor"
    )
    grad_attn_gain = jnp.sum(d_normed_one * unit_one, axis=0)
    d_input = (d_resid + norm_back(d_normed_one, unit_one, inv_one, attn_gain)).astype(BF16)
    (
        share_a,
        share_q,
        share_k,
        share_v,
        share_qg,
        share_kg,
        share_o,
        share_m,
        share_g,
        share_u,
        share_d,
    ) = (
        lax.psum_scatter(grad_attn_gain, "dp", scatter_dimension=0, tiled=True),
        lax.psum_scatter(grad_query, "dp", scatter_dimension=0, tiled=True),
        lax.psum_scatter(grad_key, "dp", scatter_dimension=0, tiled=True),
        lax.psum_scatter(grad_value, "dp", scatter_dimension=0, tiled=True),
        lax.psum_scatter(query_gain_heads, "dp", scatter_dimension=0, tiled=True),
        lax.psum_scatter(key_gain_heads, "dp", scatter_dimension=0, tiled=True),
        lax.psum_scatter(grad_out, "dp", scatter_dimension=1, tiled=True),
        lax.psum_scatter(grad_mlp_gain, "dp", scatter_dimension=0, tiled=True),
        lax.psum_scatter(grad_gate, "dp", scatter_dimension=0, tiled=True),
        lax.psum_scatter(grad_up, "dp", scatter_dimension=0, tiled=True),
        lax.psum_scatter(grad_down, "dp", scatter_dimension=1, tiled=True),
    )
    finals = lax.psum(
        (
            share_a,
            share_q,
            share_k,
            share_v,
            share_qg,
            share_kg,
            share_o,
            share_m,
            share_g,
            share_u,
            share_d,
        ),
        "ctx",
    )
    return (
        output[None],
        d_input[None],
        finals[0],
        finals[1],
        finals[2],
        finals[3],
        finals[4],
        finals[5],
        finals[6],
        finals[7],
        finals[8],
        finals[9],
        finals[10],
    )


MESH = pl.DeviceIdType.MESH


def mm(a, b):
    return lax.dot_general(a, b, (((1,), (0,)), ((), ())), preferred_element_type=F32)


def mm_nt(a, b):
    return lax.dot_general(a, b, (((1,), (1,)), ((), ())), preferred_element_type=F32)


def mm_tn(a, b):
    return lax.dot_general(a, b, (((0,), (0,)), ((), ())), preferred_element_type=F32)


def layer_kernel(
    sizes,
    x_ref,
    dy_ref,
    attn_gain_ref,
    mlp_gain_ref,
    query_gain_ref,
    key_gain_ref,
    cos_ref,
    sin_ref,
    q_in,
    k_in,
    v_in,
    o_in,
    g_in,
    u_in,
    d_in,
    out_ref,
    d_input_ref,
    gains_ref,
    q_out,
    k_out,
    v_out,
    o_out,
    g_out,
    u_out,
    d_out,
    wq,
    wk,
    wv,
    wo,
    wg,
    wu,
    wd,
    gq,
    gk,
    gv,
    go,
    gg,
    gu,
    gd,
    lands,
    h1,
    dy_all,
    h2,
    drb,
    uq,
    uk,
    invq,
    invk,
    qr,
    kr,
    vr,
    attn,
    lse,
    hidden,
    d_gate,
    d_up,
    d_attn,
    d_qkv,
    partial,
    landing,
    acc,
    arrived,
    resid,
    d_resid,
    stat,
    stat_in,
    gains,
    gains_in,
    send_sem,
    recv_sem,
    local_sem,
):
    dp_size, rows, width, part_q, part_k, part_f = sizes
    owned = width // dp_size
    half = width // 2
    length = 2 * rows
    group = part_q // part_k
    score_scale = 1.0 / math.sqrt(HD)
    dp = lax.axis_index("dp")
    block = lax.axis_index("ctx")
    core = lax.axis_index("tensor")
    side = lax.rem(dp, 2)
    line = dp // 2
    lines = dp_size // 2
    mine = 2 * block + side

    def flip(value, bits):
        result = value
        bit = 1
        while bit <= bits:
            if bits & bit:
                result = result + bit * (1 - 2 * lax.rem(value // bit, 2))
            bit *= 2
        return result

    def at_dp(bits):
        return {"dp": flip(dp, bits), "ctx": block, "tensor": core}

    to_core = {"dp": dp, "ctx": block, "tensor": 1 - core}
    to_ctx = {"dp": dp, "ctx": 1 - block, "tensor": core}
    to_pair = at_dp(1)
    to_diagonal = {"dp": flip(dp, 1), "ctx": 1 - block, "tensor": core}
    slots = {1: to_ctx, 2: to_pair, 3: to_diagonal}

    barrier = pltpu.get_barrier_semaphore()
    peers = [to_core, to_ctx, to_diagonal] + [at_dp(bits) for bits in range(1, dp_size)]
    for peer in peers:
        pl.semaphore_signal(barrier, inc=1, device_id=peer, device_id_type=MESH)
    pl.semaphore_wait(barrier, len(peers))

    count = {"remote": 0, "local": 0}
    unsent = []
    own_copies = []

    def remote(src, dst, device):
        i = count["remote"]
        count["remote"] += 1
        copy = pltpu.make_async_remote_copy(
            src_ref=src,
            dst_ref=dst,
            send_sem=send_sem.at[i],
            recv_sem=recv_sem.at[i],
            device_id=device,
            device_id_type=MESH,
        )
        copy.start()
        unsent.append(copy)
        return copy

    def wait_sent(copy):
        copy.wait_send()
        unsent[:] = [other for other in unsent if other is not copy]

    def local(src, dst):
        i = count["local"]
        count["local"] += 1
        copy = pltpu.make_async_copy(src, dst, local_sem.at[i])
        copy.start()
        return copy

    def lanes(start, size):
        return pl.ds(pl.multiple_of(start, 128), size)

    def lines_of(start, size):
        return pl.ds(pl.multiple_of(start, 128), size)

    mine_half = lanes(core * half, half)
    other_half = lanes((1 - core) * half, half)

    def rows_of(slot):
        return pl.ds(slot * rows, rows)

    def shard_part(shard, by_rows, part, which):
        if by_rows:
            return shard.at[lines_of(which * part, part), :]
        return shard.at[:, lanes(which * part, part)]

    def owner_block(whole, by_rows, owner):
        if by_rows:
            return whole.at[:, lanes(owner * owned, owned)]
        return whole.at[lines_of(owner * owned, owned), :]

    def send_weight(shard, whole, by_rows, part):
        own = local(
            shard_part(shard, by_rows, part, mine), owner_block(whole, by_rows, dp)
        )
        found = []
        for bits in range(1, dp_size):
            which = 2 * block + (side if bits % 2 == 0 else 1 - side)
            copy = remote(
                shard_part(shard, by_rows, part, which),
                owner_block(whole, by_rows, dp),
                at_dp(bits),
            )
            found.append(copy)
        return own, found

    def wait_weight(handles):
        own, found = handles
        own.wait()
        for copy in found:
            copy.wait_recv()

    def gather_start(buffer, with_core):
        own = buffer.at[rows_of(0), mine_half]
        first = remote(own, own, to_core) if with_core else None
        parts = {
            slot: remote(own, buffer.at[rows_of(slot), mine_half], slots[slot])
            for slot in (1, 2, 3)
        }
        return buffer, first, parts

    def gather_end(handles):
        buffer, first, parts = handles
        forwards = []
        for slot in (1, 2, 3):
            parts[slot].wait_recv()
            place = buffer.at[rows_of(slot), mine_half]
            forwards.append(remote(place, place, to_core))
        if first is not None:
            first.wait_recv()
        for copy in forwards:
            copy.wait_recv()

    order = (3, 1, 2, 0)

    def scatter_start(which, compute):
        copies = {}
        for slot in order:
            partial[which, rows_of(slot), :] = compute(rows_of(slot))
            copies[slot] = remote(
                partial.at[which, rows_of(slot), other_half],
                landing.at[which, rows_of(slot), :],
                to_core,
            )
        return copies

    def scatter_middle(which, copies):
        sent = {}
        for slot in order:
            copies[slot].wait_recv()
            acc[which, rows_of(slot), :] = (
                partial[which, rows_of(slot), mine_half] + landing[which, rows_of(slot), :]
            )
            if slot > 0:
                sent[slot] = remote(
                    acc.at[which, rows_of(slot), :],
                    arrived.at[which, slot - 1],
                    slots[slot],
                )
        return copies, sent

    def scatter_end(which, handles):
        copies, sent = handles
        for slot in (1, 2, 3):
            sent[slot].wait_recv()
        total = acc[which, rows_of(0), :] + arrived[which, 0]
        total = total + (arrived[which, 1] + arrived[which, 2])
        for copy in list(copies.values()) + list(sent.values()):
            wait_sent(copy)
        return total

    def core_sum(which, value):
        stat[which] = jnp.broadcast_to(value, stat.shape[1:])
        copy = remote(stat.at[which], stat_in.at[which], to_core)
        copy.wait_recv()
        return value + stat_in[which][:, :1]

    weight_q = send_weight(q_in, wq, False, part_q)
    weight_k = send_weight(k_in, wk, False, part_k)
    weight_v = send_weight(v_in, wv, False, part_k)
    tokens = x_ref[...].astype(F32)
    inv_one = lax.rsqrt(jnp.mean(tokens * tokens, axis=-1, keepdims=True) + EPS)
    h1[rows_of(0), :] = (tokens * inv_one * attn_gain_ref[...]).astype(BF16)
    gather_one = gather_start(h1, False)
    weight_o = send_weight(o_in, wo, True, part_q)
    weight_g = send_weight(g_in, wg, False, part_f)
    weight_u = send_weight(u_in, wu, False, part_f)
    dy_all[rows_of(0), :] = dy_ref[...]
    gather_dy = gather_start(dy_all, False)
    weight_d = send_weight(d_in, wd, True, part_f)
    gains[...] = jnp.zeros_like(gains)
    gather_end(gather_one)
    for handles in (weight_q, weight_k, weight_v):
        wait_weight(handles)

    def project(slot, carry):
        here = pl.ds(pl.multiple_of(slot * rows, rows), rows)
        table = pl.ds(pl.multiple_of(lax.rem(slot, 2) * rows, rows), rows)
        cos, sin = cos_ref[table, :], sin_ref[table, :]
        normed = h1[here, :]

        def head(raw, gain, unit_ref, inverse_ref, rot_ref, at):
            inverse = lax.rsqrt(jnp.mean(raw * raw, axis=-1, keepdims=True) + EPS)
            unit = raw * inverse
            scaled = unit * gain
            turned = scaled * cos + pltpu.roll(scaled, HD // 2, 1) * sin
            unit_ref[here, at * HD : (at + 1) * HD] = unit
            inverse_ref[at, here, :] = inverse
            rot_ref[here, at * HD : (at + 1) * HD] = turned.astype(BF16)

        query = mm(normed, wq[...])
        for at in range(group):
            raw = query[:, at * HD : (at + 1) * HD]
            head(raw, query_gain_ref[...], uq, invq, qr, at)
        head(mm(normed, wk[...]), key_gain_ref[...], uk, invk, kr, 0)
        vr[here, :] = mm(normed, wv[...]).astype(BF16)
        return carry

    lax.fori_loop(0, 4, project, 0)

    def masked_scores(query, key):
        at_row = lax.broadcasted_iota(jnp.int32, (length, length), 0)
        at_column = lax.broadcasted_iota(jnp.int32, (length, length), 1)
        shift = block * rows
        row = jnp.where(at_row < rows, at_row + shift, at_row - shift)
        column = jnp.where(at_column < rows, at_column + shift, at_column - shift)
        return jnp.where(column <= row, mm_nt(query, key) * score_scale, -jnp.inf)

    def attend(seq, carry):
        here = pl.ds(pl.multiple_of(seq * length, length), length)
        key, value = kr[here, :], vr[here, :]
        for at in range(group):
            columns = slice(at * HD, (at + 1) * HD)
            scores = masked_scores(qr[here, columns], key)
            peak = jnp.max(scores, axis=-1, keepdims=True)
            expo = jnp.exp(scores - peak)
            total = jnp.sum(expo, axis=-1, keepdims=True)
            mixed = mm(expo.astype(BF16), value) / total
            attn[here, columns] = mixed.astype(BF16)
            lse[at, here, :] = peak + jnp.log(total)
        return carry

    lax.fori_loop(0, 2, attend, 0)
    wait_weight(weight_o)
    first = scatter_start(0, lambda here: mm(attn[here, :], wo[...]))
    middle = scatter_middle(0, first)
    gather_end(gather_dy)
    resid_half = x_ref[:, mine_half].astype(F32) + scatter_end(0, middle)
    resid[...] = resid_half
    square = core_sum(0, jnp.sum(resid_half * resid_half, axis=-1, keepdims=True))
    inv_two = lax.rsqrt(square / width + EPS)
    unit_two = resid_half * inv_two
    h2[rows_of(0), mine_half] = (unit_two * mlp_gain_ref[:, mine_half]).astype(BF16)
    gather_two = gather_start(h2, True)
    wait_weight(weight_g)
    wait_weight(weight_u)
    gather_end(gather_two)
    wait_weight(weight_d)

    def feed(slot, carry):
        here = pl.ds(pl.multiple_of(slot * rows, rows), rows)
        normed = h2[here, :]
        gated, raised = mm(normed, wg[...]), mm(normed, wu[...])
        d_hidden = mm_nt(dy_all[here, :], wd[...])
        sigma = jax.nn.sigmoid(gated)
        silu_gate = gated * sigma
        hidden[here, :] = (silu_gate * raised).astype(BF16)
        d_gate[here, :] = (d_hidden * raised * sigma * (1.0 + gated * (1.0 - sigma))).astype(BF16)
        d_up[here, :] = (d_hidden * silu_gate).astype(BF16)
        return carry

    lax.fori_loop(0, 4, feed, 0)
    first = scatter_start(
        0, lambda here: mm_nt(d_gate[here, :], wg[...]) + mm_nt(d_up[here, :], wu[...])
    )
    middle = scatter_middle(0, first)

    span = 2 * owned

    def line_block(grad, by_rows, at):
        if by_rows:
            return grad.at[:, lanes(at * span, span)]
        return grad.at[lines_of(at * span, span), :]

    def feature_grads(grad, by_rows, features, columns):
        def step(i, carry):
            place = lanes(i * span, span)
            if by_rows:
                grad[:, place] = mm_tn(columns[...], features[:, place])
            else:
                grad[place, :] = mm_tn(features[:, place], columns[...])
            return carry

        lax.fori_loop(0, lines, step, 0)

    def line_first(entry):
        grad, by_rows, land, out, part = entry
        far = near = None
        if lines > 2:
            far = remote(line_block(grad, by_rows, flip(line, 3)), land.at[0], at_dp(2))
        if lines > 1:
            near = remote(line_block(grad, by_rows, flip(line, 1)), land.at[1], at_dp(2))
        return entry, far, near

    def line_second(handles):
        entry, far, near = handles
        grad, by_rows, land, out, part = entry
        cross = None
        if far is not None:
            far.wait_recv()
            place = line_block(grad, by_rows, flip(line, 2))
            place[...] = place[...] + land[0]
            cross = remote(place, land.at[2], at_dp(4))
        return entry, near, cross

    def line_third(handles):
        entry, near, cross = handles
        grad, by_rows, land, out, part = entry
        place = line_block(grad, by_rows, line)
        if cross is not None:
            near.wait_recv()
            cross.wait_recv()
            place[...] = place[...] + (land[1] + land[2])
        elif near is not None:
            near.wait_recv()
            place[...] = place[...] + land[1]
        own = owner_block(grad, by_rows, dp)
        away = owner_block(grad, by_rows, flip(dp, 1))
        target = shard_part(out, by_rows, part, mine)
        own_copies.append(local(own, target))
        return [
            remote(own, target, to_ctx),
            remote(away, target, to_pair),
            remote(away, target, to_diagonal),
        ]

    land_q, land_k, land_v, land_o, land_g, land_u, land_d = lands
    feature_grads(gd, True, dy_all, hidden)
    line_d = line_first((gd, True, land_d, d_out, part_f))
    feature_grads(gg, False, h2, d_gate)
    line_g = line_first((gg, False, land_g, g_out, part_f))
    feature_grads(gu, False, h2, d_up)
    line_u = line_first((gu, False, land_u, u_out, part_f))

    d_normed = scatter_end(0, middle)
    unit_two = resid[...] * inv_two
    gains[1:2, mine_half] = jnp.sum(d_normed * unit_two, axis=0, keepdims=True)
    scaled = d_normed * mlp_gain_ref[:, mine_half]
    dot = core_sum(1, jnp.sum(scaled * unit_two, axis=-1, keepdims=True))
    d_resid_half = dy_ref[:, mine_half].astype(F32) + inv_two * (scaled - unit_two * (dot / width))
    d_resid[...] = d_resid_half
    drb[rows_of(0), mine_half] = d_resid_half.astype(BF16)
    gather_drb = gather_start(drb, True)
    output_first = scatter_start(1, lambda here: mm(hidden[here, :], wd[...]))
    line_d = line_second(line_d)
    gather_end(gather_drb)
    output_middle = scatter_middle(1, output_first)

    def d_attend(slot, carry):
        here = pl.ds(pl.multiple_of(slot * rows, rows), rows)
        d_attn[here, :] = mm_nt(drb[here, :], wo[...]).astype(BF16)
        return carry

    lax.fori_loop(0, 4, d_attend, 0)

    def attend_back(seq, carry):
        here = pl.ds(pl.multiple_of(seq * length, length), length)
        key, value = kr[here, :], vr[here, :]
        cos, sin = cos_ref[...], sin_ref[...]

        def unturn(d_rot):
            return d_rot * cos - pltpu.roll(d_rot, HD // 2, 1) * sin

        def norm_head(d_scaled, unit, inverse, gain):
            gained = d_scaled * gain
            mean = jnp.mean(gained * unit, axis=-1, keepdims=True)
            return (inverse * (gained - unit * mean)).astype(BF16)

        d_key = jnp.zeros((length, HD), F32)
        d_value = jnp.zeros((length, HD), F32)
        query_part, key_part = carry
        for at in range(group):
            columns = slice(at * HD, (at + 1) * HD)
            query, d_mixed = qr[here, columns], d_attn[here, columns]
            delta = jnp.sum(
                d_mixed.astype(F32) * attn[here, columns].astype(F32), axis=-1, keepdims=True
            )
            probs = jnp.exp(masked_scores(query, key) - lse[at, here, :])
            d_scores = (probs * (mm_nt(d_mixed, value) - delta) * score_scale).astype(BF16)
            d_scaled = unturn(mm(d_scores, key))
            unit = uq[here, columns]
            query_part = query_part + jnp.sum(d_scaled * unit, axis=0, keepdims=True)
            d_qkv[here, columns] = norm_head(
                d_scaled, unit, invq[at, here, :], query_gain_ref[...]
            )
            d_key = d_key + mm_tn(d_scores, query)
            d_value = d_value + mm_tn(probs.astype(BF16), d_mixed)
        d_scaled = unturn(d_key)
        unit = uk[here, :]
        key_part = key_part + jnp.sum(d_scaled * unit, axis=0, keepdims=True)
        d_qkv[here, part_q : part_q + part_k] = norm_head(
            d_scaled, unit, invk[0, here, :], key_gain_ref[...]
        )
        d_qkv[here, part_q + part_k : part_q + 2 * part_k] = d_value.astype(BF16)
        return query_part, key_part

    empty = jnp.zeros((1, HD), F32)
    query_part, key_part = lax.fori_loop(0, 2, attend_back, (empty, empty))
    gains[2:3, 0:HD] = query_part
    gains[3:4, 0:HD] = key_part

    def columns_of(start, size):
        return d_qkv.at[:, start : start + size]

    feature_grads(gq, False, h1, columns_of(0, part_q))
    line_q = line_first((gq, False, land_q, q_out, part_q))
    feature_grads(gk, False, h1, columns_of(part_q, part_k))
    line_k = line_first((gk, False, land_k, k_out, part_k))
    feature_grads(gv, False, h1, columns_of(part_q + part_k, part_k))
    line_v = line_first((gv, False, land_v, v_out, part_k))

    def d_project(here):
        d_query = d_qkv[here, 0:part_q]
        d_key = d_qkv[here, part_q : part_q + part_k]
        d_value = d_qkv[here, part_q + part_k : part_q + 2 * part_k]
        return mm_nt(d_query, wq[...]) + mm_nt(d_key, wk[...]) + mm_nt(d_value, wv[...])

    first = scatter_start(0, d_project)
    middle = scatter_middle(0, first)
    feature_grads(go, True, drb, attn)
    line_o = line_first((go, True, land_o, o_out, part_q))
    line_g = line_second(line_g)
    line_u = line_second(line_u)

    out_half = (resid[...] + scatter_end(1, output_middle)).astype(BF16)
    out_ref[:, mine_half] = out_half
    out_copy = remote(out_ref.at[:, mine_half], out_ref.at[:, mine_half], to_core)

    d_normed = scatter_end(0, middle)
    tokens_half = x_ref[:, mine_half].astype(F32)
    unit_one = tokens_half * inv_one
    gains[0:1, mine_half] = jnp.sum(d_normed * unit_one, axis=0, keepdims=True)
    scaled = d_normed * attn_gain_ref[:, mine_half]
    dot = core_sum(2, jnp.sum(scaled * unit_one, axis=-1, keepdims=True))
    d_input_half = d_resid[...] + inv_one * (scaled - unit_one * (dot / width))
    d_input_ref[:, mine_half] = d_input_half.astype(BF16)
    in_copy = remote(d_input_ref.at[:, mine_half], d_input_ref.at[:, mine_half], to_core)

    spread = []
    spread += line_third(line_d)
    line_q = line_second(line_q)
    line_k = line_second(line_k)
    line_v = line_second(line_v)
    line_o = line_second(line_o)

    rounds = [to_core, to_ctx]
    stride = 1
    while stride < dp_size:
        rounds.append(at_dp(stride))
        stride *= 2
    for i, device in enumerate(rounds):
        copy = remote(gains, gains_in.at[i], device)
        copy.wait_recv()
        wait_sent(copy)
        gains[...] = gains[...] + gains_in[i]
    gains_ref[...] = gains[...]

    for handles in (line_g, line_u, line_q, line_k, line_v, line_o):
        spread += line_third(handles)
    for copy in spread + [out_copy, in_copy]:
        copy.wait_recv()
    for copy in own_copies:
        copy.wait()
    for copy in unsent:
        copy.wait_send()


def fused_device(
    dp_size,
    block_input,
    attn_gain,
    query_weight,
    key_weight,
    value_weight,
    query_gain,
    key_gain,
    output_weight,
    mlp_gain,
    gate_weight,
    up_weight,
    down_weight,
    cotangent,
):
    rows, width = block_input.shape[1:]
    block = lax.axis_index("ctx")
    half = width // 2
    owned = width // dp_size
    part_q = query_weight.shape[1] // 4
    part_k = key_weight.shape[1] // 4
    part_f = gate_weight.shape[1] // 4
    span = 2 * owned
    tokens = 4 * rows
    index = jnp.arange(rows, dtype=jnp.int32)
    positions = jnp.concatenate([block * rows + index, (1 - block) * rows + index])
    cos_table, sin_table = rope_tables(positions, HD)
    sin_table = jnp.concatenate([-sin_table[:, : HD // 2], sin_table[:, HD // 2 :]], axis=1)
    vmem = pl.BlockSpec(memory_space=pltpu.VMEM)
    hbm = pl.BlockSpec(memory_space=pl.ANY)

    def shape(dims, kind):
        return jax.ShapeDtypeStruct(dims, kind)

    def land(by_rows, part):
        return pltpu.VMEM((3, part, span) if by_rows else (3, span, part), F32)

    weights = (
        query_weight,
        key_weight,
        value_weight,
        output_weight,
        gate_weight,
        up_weight,
        down_weight,
    )
    group = part_q // part_k
    sizes = (dp_size, rows, width, part_q, part_k, part_f)
    copies = 7 * (dp_size - 1) + 4 * 7 + 4 * 7 + 3 + 7 * 6 + 2 + 8
    results = pl.pallas_call(
        functools.partial(layer_kernel, sizes),
        out_shape=(
            shape((rows, width), BF16),
            shape((rows, width), BF16),
            shape((8, width), F32),
        )
        + tuple(shape(weight.shape, F32) for weight in weights),
        in_specs=[vmem] * 8 + [hbm] * 7,
        out_specs=(vmem,) * 3 + (hbm,) * 7,
        scratch_shapes=[
            pltpu.VMEM((width, part_q), BF16),
            pltpu.VMEM((width, part_k), BF16),
            pltpu.VMEM((width, part_k), BF16),
            pltpu.VMEM((part_q, width), BF16),
            pltpu.VMEM((width, part_f), BF16),
            pltpu.VMEM((width, part_f), BF16),
            pltpu.VMEM((part_f, width), BF16),
            pltpu.VMEM((width, part_q), F32),
            pltpu.VMEM((width, part_k), F32),
            pltpu.VMEM((width, part_k), F32),
            pltpu.VMEM((part_q, width), F32),
            pltpu.VMEM((width, part_f), F32),
            pltpu.VMEM((width, part_f), F32),
            pltpu.VMEM((part_f, width), F32),
            [
                land(False, part_q),
                land(False, part_k),
                land(False, part_k),
                land(True, part_q),
                land(False, part_f),
                land(False, part_f),
                land(True, part_f),
            ],
            pltpu.VMEM((tokens, width), BF16),
            pltpu.VMEM((tokens, width), BF16),
            pltpu.VMEM((tokens, width), BF16),
            pltpu.VMEM((tokens, width), BF16),
            pltpu.VMEM((tokens, part_q), F32),
            pltpu.VMEM((tokens, part_k), F32),
            pltpu.VMEM((group, tokens, 1), F32),
            pltpu.VMEM((1, tokens, 1), F32),
            pltpu.VMEM((tokens, part_q), BF16),
            pltpu.VMEM((tokens, part_k), BF16),
            pltpu.VMEM((tokens, part_k), BF16),
            pltpu.VMEM((tokens, part_q), BF16),
            pltpu.VMEM((group, tokens, 1), F32),
            pltpu.VMEM((tokens, part_f), BF16),
            pltpu.VMEM((tokens, part_f), BF16),
            pltpu.VMEM((tokens, part_f), BF16),
            pltpu.VMEM((tokens, part_q), BF16),
            pltpu.VMEM((tokens, part_q + 2 * part_k), BF16),
            pltpu.VMEM((2, tokens, width), F32),
            pltpu.VMEM((2, tokens, half), F32),
            pltpu.VMEM((2, tokens, half), F32),
            pltpu.VMEM((2, 3, rows, half), F32),
            pltpu.VMEM((rows, half), F32),
            pltpu.VMEM((rows, half), F32),
            pltpu.VMEM((3, rows, HD), F32),
            pltpu.VMEM((3, rows, HD), F32),
            pltpu.VMEM((8, width), F32),
            pltpu.VMEM((8, 8, width), F32),
            pltpu.SemaphoreType.DMA((copies,)),
            pltpu.SemaphoreType.DMA((copies,)),
            pltpu.SemaphoreType.DMA((14,)),
        ],
        compiler_params=pltpu.CompilerParams(
            collective_id=0, has_side_effects=True, vmem_limit_bytes=63 * 1024 * 1024
        ),
        cost_estimate=pl.CostEstimate(
            flops=24 * tokens * width * (part_q + part_k + part_f),
            bytes_accessed=8 * width * width,
            transcendentals=0,
        ),
    )(
        block_input[0],
        cotangent[0],
        attn_gain[None],
        mlp_gain[None],
        query_gain[None],
        key_gain[None],
        cos_table,
        sin_table,
        *weights,
    )
    output, d_input, gains, grad_q, grad_k, grad_v, grad_o, grad_g, grad_u, grad_d = results
    owner = lax.axis_index("dp")
    share = HD // dp_size

    def owned_gain(row, size):
        return lax.dynamic_slice_in_dim(gains[row], owner * size, size)

    return (
        output[None],
        d_input[None],
        owned_gain(0, owned),
        grad_q,
        grad_k,
        grad_v,
        owned_gain(2, share),
        owned_gain(3, share),
        grad_o,
        owned_gain(1, owned),
        grad_g,
        grad_u,
        grad_d,
    )


def solution(mesh):
    sizes = dict(mesh.shape)
    body = per_device
    if sizes["ctx"] == 2 and sizes["tensor"] == 2 and sizes["dp"] in (2, 4, 8):
        body = functools.partial(fused_device, sizes["dp"])
    return jax.shard_map(
        body,
        mesh=mesh,
        in_specs=(
            P("dp", "ctx", None),
            P(),
            P("dp", "tensor"),
            P("dp", "tensor"),
            P("dp", "tensor"),
            P(),
            P(),
            P("tensor", "dp"),
            P(),
            P("dp", "tensor"),
            P("dp", "tensor"),
            P("tensor", "dp"),
            P("dp", "ctx", None),
        ),
        out_specs=(
            P("dp", "ctx", None),
            P("dp", "ctx", None),
            P("dp"),
            P("dp", "tensor"),
            P("dp", "tensor"),
            P("dp", "tensor"),
            P("dp"),
            P("dp"),
            P("tensor", "dp"),
            P("dp"),
            P("dp", "tensor"),
            P("dp", "tensor"),
            P("tensor", "dp"),
        ),
        check_vma=False,
    )
```

```python
import functools
import math

import jax
import jax.numpy as jnp
from jax import lax
from jax.experimental import pallas as pl
from jax.experimental.pallas import tpu as pltpu
from jax.sharding import PartitionSpec as P

HD = 128


EPS = 1e-06
THETA = 1000000.0
F32 = jnp.float32
BF16 = jnp.bfloat16


def rms_inverse(value):
    return lax.rsqrt(jnp.mean(value * value, axis=-1, keepdims=True) + EPS)


def norm_back(grad, unit, inverse, gain):
    scaled = grad * gain
    return inverse * (scaled - unit * jnp.mean(scaled * unit, axis=-1, keepdims=True))


def rotate(value):
    half_width = value.shape[-1] // 2
    return jnp.concatenate([-value[..., half_width:], value[..., :half_width]], axis=-1)


def rotate_back(value):
    half_width = value.shape[-1] // 2
    return jnp.concatenate([value[..., half_width:], -value[..., :half_width]], axis=-1)


def rope_tables(positions, width):
    half_width = width // 2
    exponent = jnp.arange(half_width).astype(F32) * (2.0 / width)
    frequency = jnp.power(THETA, -exponent)
    angle = positions.astype(F32)[:, None] * frequency[None, :]
    angle = jnp.concatenate([angle, angle], axis=-1)
    return (jnp.cos(angle), jnp.sin(angle))


def over_heads(partial_value):
    return lax.psum(partial_value, "tensor")


def per_device(
    block_input,
    attn_gain,
    query_weight,
    key_weight,
    value_weight,
    query_gain,
    key_gain,
    output_weight,
    mlp_gain,
    gate_weight,
    up_weight,
    down_weight,
    cotangent,
):
    tokens = block_input[0].astype(F32)
    row_count = tokens.shape[0]
    score_scale = 1.0 / math.sqrt(HD)
    positions = lax.axis_index("ctx") * row_count + jnp.arange(row_count, dtype=jnp.int32)
    cos_table, sin_table = rope_tables(positions, HD)
    cos_heads = cos_table[:, None, :]
    sin_heads = sin_table[:, None, :]
    w_query, w_key, w_value, w_out, w_gate, w_up, w_down = (
        lax.all_gather(query_weight, "dp", axis=0, tiled=True),
        lax.all_gather(key_weight, "dp", axis=0, tiled=True),
        lax.all_gather(value_weight, "dp", axis=0, tiled=True),
        lax.all_gather(output_weight, "dp", axis=1, tiled=True),
        lax.all_gather(gate_weight, "dp", axis=0, tiled=True),
        lax.all_gather(up_weight, "dp", axis=0, tiled=True),
        lax.all_gather(down_weight, "dp", axis=1, tiled=True),
    )
    q_heads = w_query.shape[1] // HD
    kv_heads = w_key.shape[1] // HD
    group_size = q_heads // kv_heads
    inv_one = rms_inverse(tokens)
    unit_one = tokens * inv_one
    normed_one = (unit_one * attn_gain).astype(BF16)
    query = jnp.dot(normed_one, w_query, preferred_element_type=F32).reshape(row_count, q_heads, HD)
    key_raw = jnp.dot(normed_one, w_key, preferred_element_type=F32).reshape(
        row_count, kv_heads, HD
    )
    value = (
        jnp.dot(normed_one, w_value, preferred_element_type=F32)
        .astype(BF16)
        .reshape(row_count, kv_heads, HD)
    )
    query_inv = rms_inverse(query)
    query_unit = query * query_inv
    query_scaled = query_unit * query_gain
    query_rot = (query_scaled * cos_heads + rotate(query_scaled) * sin_heads).astype(BF16)
    key_inv = rms_inverse(key_raw)
    key_unit = key_raw * key_inv
    key_scaled = key_unit * key_gain
    key_rot = (key_scaled * cos_heads + rotate(key_scaled) * sin_heads).astype(BF16)
    grouped_query = query_rot.reshape(row_count, kv_heads, group_size, HD)

    def piece_scores(piece_keys):
        piece_rows = piece_keys.shape[0]
        key_positions = jnp.arange(piece_rows, dtype=jnp.int32)
        allowed = key_positions[None, :] <= positions[:, None]
        scores = (
            jnp.einsum("qkgd,nkd->kgqn", grouped_query, piece_keys, preferred_element_type=F32)
            * score_scale
        )
        return jnp.where(allowed, scores, -jnp.inf)

    peak_old = jnp.full((kv_heads, group_size, row_count), -1e30, F32)
    piece_keys = lax.all_gather(key_rot, "ctx", axis=0, tiled=True)
    piece_values = lax.all_gather(value, "ctx", axis=0, tiled=True)
    scores = piece_scores(piece_keys)
    peak_new = jnp.maximum(peak_old, jnp.max(scores, axis=-1))
    expo = jnp.exp(scores - peak_new[..., None])
    total_new = jnp.sum(expo, axis=-1)
    accum_new = jnp.einsum(
        "kgqn,nkd->kgqd", expo.astype(BF16), piece_values, preferred_element_type=F32
    )
    log_total = peak_new + jnp.log(total_new)
    attn = (
        (accum_new / total_new[..., None])
        .astype(BF16)
        .transpose(2, 0, 1, 3)
        .reshape(row_count, q_heads * HD)
    )
    resid = tokens + over_heads(jnp.dot(attn, w_out, preferred_element_type=F32))
    inv_two = rms_inverse(resid)
    unit_two = resid * inv_two
    normed_two = (unit_two * mlp_gain).astype(BF16)
    gate = jnp.dot(normed_two, w_gate, preferred_element_type=F32)
    up_proj = jnp.dot(normed_two, w_up, preferred_element_type=F32)
    sigma = jax.nn.sigmoid(gate)
    silu_gate = gate * sigma
    hidden = (silu_gate * up_proj).astype(BF16)
    output = (resid + over_heads(jnp.dot(hidden, w_down, preferred_element_type=F32))).astype(BF16)
    w_query, w_key, w_value, w_out, w_gate, w_up, w_down = (
        lax.all_gather(query_weight, "dp", axis=0, tiled=True),
        lax.all_gather(key_weight, "dp", axis=0, tiled=True),
        lax.all_gather(value_weight, "dp", axis=0, tiled=True),
        lax.all_gather(output_weight, "dp", axis=1, tiled=True),
        lax.all_gather(gate_weight, "dp", axis=0, tiled=True),
        lax.all_gather(up_weight, "dp", axis=0, tiled=True),
        lax.all_gather(down_weight, "dp", axis=1, tiled=True),
    )
    d_output = cotangent[0]
    d_hidden = jnp.einsum("td,fd->tf", d_output, w_down, preferred_element_type=F32)
    grad_down = jnp.einsum("tf,td->fd", hidden, d_output, preferred_element_type=F32)
    d_gate = (d_hidden * up_proj * sigma * (1.0 + gate * (1.0 - sigma))).astype(BF16)
    d_up = (d_hidden * silu_gate).astype(BF16)
    grad_gate = jnp.einsum("td,tf->df", normed_two, d_gate, preferred_element_type=F32)
    grad_up = jnp.einsum("td,tf->df", normed_two, d_up, preferred_element_type=F32)
    partial_two = jnp.einsum("tf,df->td", d_gate, w_gate, preferred_element_type=F32) + jnp.einsum(
        "tf,df->td", d_up, w_up, preferred_element_type=F32
    )
    d_normed_two = lax.psum(partial_two, "tensor")
    grad_mlp_gain = jnp.sum(d_normed_two * unit_two, axis=0)
    d_resid = d_output.astype(F32) + norm_back(d_normed_two, unit_two, inv_two, mlp_gain)
    d_resid_b = d_resid.astype(BF16)
    grad_out = jnp.einsum("th,td->hd", attn, d_resid_b, preferred_element_type=F32)
    d_attn = jnp.einsum("td,hd->th", d_resid_b, w_out, preferred_element_type=F32).astype(BF16)
    delta = jnp.sum(
        d_attn.astype(F32).reshape(row_count, q_heads, HD)
        * attn.astype(F32).reshape(row_count, q_heads, HD),
        axis=-1,
    )
    delta_heads = delta.reshape(row_count, kv_heads, group_size).transpose(1, 2, 0)
    grouped_grad = d_attn.reshape(row_count, kv_heads, group_size, HD)
    piece_keys = lax.all_gather(key_rot, "ctx", axis=0, tiled=True)
    piece_values = lax.all_gather(value, "ctx", axis=0, tiled=True)
    piece_rows = piece_keys.shape[0]
    scores = piece_scores(piece_keys)
    probs = jnp.exp(scores - log_total[..., None])
    d_probs = jnp.einsum("qkgd,nkd->kgqn", grouped_grad, piece_values, preferred_element_type=F32)
    d_scores = (probs * (d_probs - delta_heads[..., None]) * score_scale).astype(BF16)
    d_query_acc = jnp.einsum("kgqn,nkd->kgqd", d_scores, piece_keys, preferred_element_type=F32)
    d_key_piece = jnp.einsum("kgqn,qkgd->nkd", d_scores, grouped_query, preferred_element_type=F32)
    d_value_piece = jnp.einsum(
        "kgqn,qkgd->nkd", probs.astype(BF16), grouped_grad, preferred_element_type=F32
    )
    update = jnp.stack([d_key_piece, d_value_piece])
    d_kv_home = lax.psum_scatter(update, "ctx", scatter_dimension=1, tiled=True)
    d_query_rot = d_query_acc.transpose(2, 0, 1, 3).reshape(row_count, q_heads, HD)
    d_key_rot = d_kv_home[0]
    d_value = d_kv_home[1].astype(BF16).reshape(row_count, kv_heads * HD)
    d_query_scaled = d_query_rot * cos_heads + rotate_back(d_query_rot * sin_heads)
    d_key_scaled = d_key_rot * cos_heads + rotate_back(d_key_rot * sin_heads)
    query_gain_part = jnp.sum(d_query_scaled * query_unit, axis=(0, 1))
    key_gain_part = jnp.sum(d_key_scaled * key_unit, axis=(0, 1))
    d_query = (
        norm_back(d_query_scaled, query_unit, query_inv, query_gain)
        .astype(BF16)
        .reshape(row_count, q_heads * HD)
    )
    d_key = (
        norm_back(d_key_scaled, key_unit, key_inv, key_gain)
        .astype(BF16)
        .reshape(row_count, kv_heads * HD)
    )
    grad_query = jnp.einsum("td,th->dh", normed_one, d_query, preferred_element_type=F32)
    grad_key = jnp.einsum("td,th->dh", normed_one, d_key, preferred_element_type=F32)
    grad_value = jnp.einsum("td,th->dh", normed_one, d_value, preferred_element_type=F32)
    partial_one = jnp.einsum("th,dh->td", d_query, w_query, preferred_element_type=F32)
    partial_one = partial_one + jnp.einsum("th,dh->td", d_key, w_key, preferred_element_type=F32)
    partial_one = partial_one + jnp.einsum(
        "th,dh->td", d_value, w_value, preferred_element_type=F32
    )
    d_normed_one, query_gain_heads, key_gain_heads = lax.psum(
        (partial_one, query_gain_part, key_gain_part), "tensor"
    )
    grad_attn_gain = jnp.sum(d_normed_one * unit_one, axis=0)
    d_input = (d_resid + norm_back(d_normed_one, unit_one, inv_one, attn_gain)).astype(BF16)
    (
        share_a,
        share_q,
        share_k,
        share_v,
        share_qg,
        share_kg,
        share_o,
        share_m,
        share_g,
        share_u,
        share_d,
    ) = (
        lax.psum_scatter(grad_attn_gain, "dp", scatter_dimension=0, tiled=True),
        lax.psum_scatter(grad_query, "dp", scatter_dimension=0, tiled=True),
        lax.psum_scatter(grad_key, "dp", scatter_dimension=0, tiled=True),
        lax.psum_scatter(grad_value, "dp", scatter_dimension=0, tiled=True),
        lax.psum_scatter(query_gain_heads, "dp", scatter_dimension=0, tiled=True),
        lax.psum_scatter(key_gain_heads, "dp", scatter_dimension=0, tiled=True),
        lax.psum_scatter(grad_out, "dp", scatter_dimension=1, tiled=True),
        lax.psum_scatter(grad_mlp_gain, "dp", scatter_dimension=0, tiled=True),
        lax.psum_scatter(grad_gate, "dp", scatter_dimension=0, tiled=True),
        lax.psum_scatter(grad_up, "dp", scatter_dimension=0, tiled=True),
        lax.psum_scatter(grad_down, "dp", scatter_dimension=1, tiled=True),
    )
    finals = lax.psum(
        (
            share_a,
            share_q,
            share_k,
            share_v,
            share_qg,
            share_kg,
            share_o,
            share_m,
            share_g,
            share_u,
            share_d,
        ),
        "ctx",
    )
    return (
        output[None],
        d_input[None],
        finals[0],
        finals[1],
        finals[2],
        finals[3],
        finals[4],
        finals[5],
        finals[6],
        finals[7],
        finals[8],
        finals[9],
        finals[10],
    )


MESH = pl.DeviceIdType.MESH


def mm(a, b):
    return lax.dot_general(a, b, (((1,), (0,)), ((), ())), preferred_element_type=F32)


def mm_nt(a, b):
    return lax.dot_general(a, b, (((1,), (1,)), ((), ())), preferred_element_type=F32)


def mm_tn(a, b):
    return lax.dot_general(a, b, (((0,), (0,)), ((), ())), preferred_element_type=F32)


def layer_kernel(
    sizes,
    x_ref,
    dy_ref,
    attn_gain_ref,
    mlp_gain_ref,
    query_gain_ref,
    key_gain_ref,
    cos_ref,
    sin_ref,
    q_in,
    k_in,
    v_in,
    o_in,
    g_in,
    u_in,
    d_in,
    out_ref,
    d_input_ref,
    gains_ref,
    q_out,
    k_out,
    v_out,
    o_out,
    g_out,
    u_out,
    d_out,
    wq,
    wk,
    wv,
    wo,
    wg,
    wu,
    wd,
    grads,
    h1,
    dy_all,
    h2,
    drb,
    uq,
    uk,
    invq,
    invk,
    qr,
    kr,
    vr,
    attn,
    lse,
    hidden,
    d_gate,
    d_up,
    d_attn,
    d_qkv,
    partial,
    landing,
    acc,
    arrived,
    resid,
    d_resid,
    stat,
    stat_in,
    gains,
    gains_in,
    send_sem,
    recv_sem,
    local_sem,
):
    dp_size, rows, width, part_q, part_k, part_f = sizes
    owned = width // dp_size
    half = width // 2
    length = 2 * rows
    group = part_q // part_k
    score_scale = 1.0 / math.sqrt(HD)
    dp = lax.axis_index("dp")
    block = lax.axis_index("ctx")
    core = lax.axis_index("tensor")
    side = lax.rem(dp, 2)
    line = dp // 2
    lines = dp_size // 2
    mine = 2 * block + side

    def flip(value, bits):
        result = value
        bit = 1
        while bit <= bits:
            if bits & bit:
                result = result + bit * (1 - 2 * lax.rem(value // bit, 2))
            bit *= 2
        return result

    def at_dp(bits):
        return {"dp": flip(dp, bits), "ctx": block, "tensor": core}

    to_core = {"dp": dp, "ctx": block, "tensor": 1 - core}
    to_ctx = {"dp": dp, "ctx": 1 - block, "tensor": core}
    to_pair = at_dp(1)
    to_diagonal = {"dp": flip(dp, 1), "ctx": 1 - block, "tensor": core}
    slots = {1: to_ctx, 2: to_pair, 3: to_diagonal}

    barrier = pltpu.get_barrier_semaphore()
    peers = [to_core, to_ctx, to_diagonal] + [at_dp(bits) for bits in range(1, dp_size)]
    for peer in peers:
        pl.semaphore_signal(barrier, inc=1, device_id=peer, device_id_type=MESH)
    pl.semaphore_wait(barrier, len(peers))

    count = {"remote": 0, "local": 0}
    unsent = []
    own_copies = []

    def remote(src, dst, device):
        i = count["remote"]
        count["remote"] += 1
        copy = pltpu.make_async_remote_copy(
            src_ref=src,
            dst_ref=dst,
            send_sem=send_sem.at[i],
            recv_sem=recv_sem.at[i],
            device_id=device,
            device_id_type=MESH,
        )
        copy.start()
        unsent.append(copy)
        return copy

    def wait_sent(copy):
        copy.wait_send()
        unsent[:] = [other for other in unsent if other is not copy]

    def local(src, dst):
        i = count["local"]
        count["local"] += 1
        copy = pltpu.make_async_copy(src, dst, local_sem.at[i])
        copy.start()
        return copy

    def lanes(start, size):
        return pl.ds(pl.multiple_of(start, 128), size)

    def lines_of(start, size):
        return pl.ds(pl.multiple_of(start, 128), size)

    mine_half = lanes(core * half, half)
    other_half = lanes((1 - core) * half, half)

    def rows_of(slot):
        return pl.ds(slot * rows, rows)

    def shard_part(shard, by_rows, part, which):
        if by_rows:
            return shard.at[lines_of(which * part, part), :]
        return shard.at[:, lanes(which * part, part)]

    def owner_block(whole, by_rows, owner):
        if by_rows:
            return whole.at[:, lanes(owner * owned, owned)]
        return whole.at[lines_of(owner * owned, owned), :]

    def send_weight(shard, whole, by_rows, part):
        own = local(
            shard_part(shard, by_rows, part, mine), owner_block(whole, by_rows, dp)
        )
        found = []
        for bits in range(1, dp_size):
            which = 2 * block + (side if bits % 2 == 0 else 1 - side)
            copy = remote(
                shard_part(shard, by_rows, part, which),
                owner_block(whole, by_rows, dp),
                at_dp(bits),
            )
            found.append(copy)
        return own, found

    def wait_weight(handles):
        own, found = handles
        own.wait()
        for copy in found:
            copy.wait_recv()

    span = 2 * owned

    def line_block(whole, by_rows, at):
        if by_rows:
            return whole.at[:, lanes(at * span, span)]
        return whole.at[lines_of(at * span, span), :]

    def weight_pair(shard, whole, by_rows, part):
        place = owner_block(whole, by_rows, dp)
        own = local(shard_part(shard, by_rows, part, mine), place)
        pair = remote(shard_part(shard, by_rows, part, 2 * block + 1 - side), place, to_pair)
        return whole, by_rows, own, pair

    def weight_first(handles):
        whole, by_rows, own, pair = handles
        own.wait()
        pair.wait_recv()
        place = line_block(whole, by_rows, line)
        cross = remote(place, place, at_dp(4)) if lines > 2 else None
        near = remote(place, place, at_dp(2)) if lines > 1 else None
        return whole, by_rows, near, cross

    def weight_second(handles):
        whole, by_rows, near, cross = handles
        found = [near] if lines > 1 else []
        if cross is not None:
            cross.wait_recv()
            place = line_block(whole, by_rows, flip(line, 2))
            found.append(remote(place, place, at_dp(2)))
        return found

    def weight_end(found):
        for copy in found:
            copy.wait_recv()

    def gather_start(buffer, with_core):
        own = buffer.at[rows_of(0), mine_half]
        first = remote(own, own, to_core) if with_core else None
        parts = {
            slot: remote(own, buffer.at[rows_of(slot), mine_half], slots[slot])
            for slot in (1, 2, 3)
        }
        return buffer, first, parts

    def gather_near(handles):
        buffer, first, parts = handles
        if first is not None:
            first.wait_recv()

    def gather_pass(handles, slot):
        buffer, first, parts = handles
        parts[slot].wait_recv()
        place = buffer.at[rows_of(slot), mine_half]
        return remote(place, place, to_core)

    def gather_end(handles):
        gather_near(handles)
        for copy in [gather_pass(handles, slot) for slot in (1, 2, 3)]:
            copy.wait_recv()

    order = (3, 2, 1, 0)

    def scatter_start(which, compute, copies, some=order):
        for slot in some:
            partial[which, rows_of(slot), :] = compute(rows_of(slot))
            copies[slot] = remote(
                partial.at[which, rows_of(slot), other_half],
                landing.at[which, rows_of(slot), :],
                to_core,
            )
        return copies

    quad = half // 2
    low, high = slice(0, quad), slice(quad, half)

    def scatter_middle(which, copies):
        def near_sum(slot):
            copies[slot].wait_recv()
            acc[which, rows_of(slot), :] = (
                partial[which, rows_of(slot), mine_half] + landing[which, rows_of(slot), :]
            )

        def forward(slot, part, place, device):
            return remote(acc.at[which, rows_of(slot), part], arrived.at[which, place], device)

        near_sum(3)
        relay_low = forward(3, low, 0, to_ctx)
        relay_high = forward(3, high, 1, to_pair)
        near_sum(2)
        sent = [forward(2, high, 3, to_pair)]
        near_sum(1)
        sent.append(forward(1, low, 2, to_ctx))
        near_sum(0)
        return copies, relay_low, relay_high, sent, forward

    def scatter_relay(which, handles):
        copies, relay_low, relay_high, sent, forward = handles
        relay_low.wait_recv()
        acc[which, rows_of(2), low] = acc[which, rows_of(2), low] + arrived[which, 0]
        sent.append(forward(2, low, 4, to_pair))
        relay_high.wait_recv()
        acc[which, rows_of(1), high] = acc[which, rows_of(1), high] + arrived[which, 1]
        sent.append(forward(1, high, 5, to_ctx))
        return list(copies.values()) + [relay_low, relay_high] + sent, sent

    def scatter_end(which, handles):
        copies, sent = handles
        for copy in sent:
            copy.wait_recv()
        own = acc[which, rows_of(0), :]
        total = jnp.concatenate(
            [
                own[:, low] + (arrived[which, 2] + arrived[which, 4]),
                own[:, high] + (arrived[which, 3] + arrived[which, 5]),
            ],
            axis=1,
        )
        for copy in copies:
            wait_sent(copy)
        return total

    def core_sum(which, value):
        stat[which] = jnp.broadcast_to(value, stat.shape[1:])
        copy = remote(stat.at[which], stat_in.at[which], to_core)
        copy.wait_recv()
        return value + stat_in[which][:, :1]

    weight_q = send_weight(q_in, wq, False, part_q)
    weight_k = send_weight(k_in, wk, False, part_k)
    weight_v = send_weight(v_in, wv, False, part_k)
    tokens = x_ref[...].astype(F32)
    inv_one = lax.rsqrt(jnp.mean(tokens * tokens, axis=-1, keepdims=True) + EPS)
    h1[rows_of(0), :] = (tokens * inv_one * attn_gain_ref[...]).astype(BF16)
    gather_one = gather_start(h1, False)
    weight_o = weight_pair(o_in, wo, True, part_q)
    weight_g = weight_pair(g_in, wg, False, part_f)
    weight_u = weight_pair(u_in, wu, False, part_f)
    weight_d = weight_pair(d_in, wd, True, part_f)
    dy_all[rows_of(0), :] = dy_ref[...]
    gather_dy = gather_start(dy_all, False)
    gains[...] = jnp.zeros_like(gains)
    gather_end(gather_one)
    for handles in (weight_q, weight_k, weight_v):
        wait_weight(handles)
    weight_o = weight_first(weight_o)
    weight_g = weight_first(weight_g)
    weight_u = weight_first(weight_u)
    weight_d = weight_first(weight_d)

    def project(slot, carry):
        here = pl.ds(pl.multiple_of(slot * rows, rows), rows)
        table = pl.ds(pl.multiple_of(lax.rem(slot, 2) * rows, rows), rows)
        cos, sin = cos_ref[table, :], sin_ref[table, :]
        normed = h1[here, :]

        def head(raw, gain, unit_ref, inverse_ref, rot_ref, at):
            inverse = lax.rsqrt(jnp.mean(raw * raw, axis=-1, keepdims=True) + EPS)
            unit = raw * inverse
            scaled = unit * gain
            turned = scaled * cos + pltpu.roll(scaled, HD // 2, 1) * sin
            unit_ref[here, at * HD : (at + 1) * HD] = unit
            inverse_ref[at, here, :] = inverse
            rot_ref[here, at * HD : (at + 1) * HD] = turned.astype(BF16)

        query = mm(normed, wq[...])
        for at in range(group):
            raw = query[:, at * HD : (at + 1) * HD]
            head(raw, query_gain_ref[...], uq, invq, qr, at)
        head(mm(normed, wk[...]), key_gain_ref[...], uk, invk, kr, 0)
        vr[here, :] = mm(normed, wv[...]).astype(BF16)
        return carry

    lax.fori_loop(0, 4, project, 0)
    weight_o = weight_second(weight_o)

    def masked_scores(query, key):
        at_row = lax.broadcasted_iota(jnp.int32, (length, length), 0)
        at_column = lax.broadcasted_iota(jnp.int32, (length, length), 1)
        shift = block * rows
        row = jnp.where(at_row < rows, at_row + shift, at_row - shift)
        column = jnp.where(at_column < rows, at_column + shift, at_column - shift)
        return jnp.where(column <= row, mm_nt(query, key) * score_scale, -jnp.inf)

    def attend(seq, carry):
        here = pl.ds(pl.multiple_of(seq * length, length), length)
        key, value = kr[here, :], vr[here, :]
        for at in range(group):
            columns = slice(at * HD, (at + 1) * HD)
            scores = masked_scores(qr[here, columns], key)
            peak = jnp.max(scores, axis=-1, keepdims=True)
            expo = jnp.exp(scores - peak)
            total = jnp.sum(expo, axis=-1, keepdims=True)
            mixed = mm(expo.astype(BF16), value) / total
            attn[here, columns] = mixed.astype(BF16)
            lse[at, here, :] = peak + jnp.log(total)
        return carry

    def attend_once(seq):
        lax.fori_loop(seq, seq + 1, attend, 0)

    attend_once(1)
    weight_end(weight_o)
    def project_out(here):
        return mm(attn[here, :], wo[...])

    first = scatter_start(0, project_out, {}, (3, 2))
    attend_once(0)
    first = scatter_start(0, project_out, first, (1, 0))
    middle = scatter_middle(0, first)
    weight_g = weight_second(weight_g)
    gather_end(gather_dy)
    middle = scatter_relay(0, middle)
    weight_u = weight_second(weight_u)
    resid_half = x_ref[:, mine_half].astype(F32) + scatter_end(0, middle)
    resid[...] = resid_half
    square = core_sum(0, jnp.sum(resid_half * resid_half, axis=-1, keepdims=True))
    inv_two = lax.rsqrt(square / width + EPS)
    unit_two = resid_half * inv_two
    h2[rows_of(0), mine_half] = (unit_two * mlp_gain_ref[:, mine_half]).astype(BF16)
    gather_two = gather_start(h2, True)
    weight_d = weight_second(weight_d)
    weight_end(weight_g)
    weight_end(weight_u)
    weight_end(weight_d)

    def feed(slot):
        here = rows_of(slot)
        normed = h2[here, :]
        gated, raised = mm(normed, wg[...]), mm(normed, wu[...])
        d_hidden = mm_nt(dy_all[here, :], wd[...])
        sigma = jax.nn.sigmoid(gated)
        silu_gate = gated * sigma
        hidden[here, :] = (silu_gate * raised).astype(BF16)
        d_gate[here, :] = (d_hidden * raised * sigma * (1.0 + gated * (1.0 - sigma))).astype(BF16)
        d_up[here, :] = (d_hidden * silu_gate).astype(BF16)

    gather_near(gather_two)
    feed(0)
    passed = [gather_pass(gather_two, slot) for slot in (1, 2)]
    passed[0].wait_recv()
    feed(1)
    passed.append(gather_pass(gather_two, 3))
    passed[1].wait_recv()
    feed(2)
    passed[2].wait_recv()
    feed(3)

    def feed_back(here):
        return mm_nt(d_gate[here, :], wg[...]) + mm_nt(d_up[here, :], wu[...])

    first = scatter_start(0, feed_back, {})
    middle = scatter_middle(0, first)

    def line_first(grad, by_rows, out, part, features, columns):
        own, cross, rounded, land, found = grad

        def block_grad(at):
            place = lanes(at * span, span)
            if by_rows:
                return mm_tn(columns[...], features[:, place])
            return mm_tn(features[:, place], columns[...])

        far = near = None
        if lines > 2:
            rounded[0] = block_grad(flip(line, 3)).astype(BF16)
            far = remote(rounded.at[0], land.at[0], at_dp(2))
        if lines > 1:
            rounded[1] = block_grad(flip(line, 1)).astype(BF16)
            near = remote(rounded.at[1], land.at[1], at_dp(2))
        if lines > 2:
            cross[...] = block_grad(flip(line, 2))
        own[...] = block_grad(line)
        return grad, by_rows, out, part, far, near

    def line_second(handles):
        grad, by_rows, out, part, far, near = handles
        own, cross, rounded, land, found = grad
        sent = None
        if far is not None:
            far.wait_recv()
            cross[...] = cross[...] + land[0].astype(F32)
            sent = remote(cross, found, at_dp(4))
        return grad, by_rows, out, part, near, sent

    def line_third(handles):
        grad, by_rows, out, part, near, sent = handles
        own, cross, rounded, land, found = grad
        if near is not None:
            near.wait_recv()
            own[...] = own[...] + land[1].astype(F32)
        if sent is not None:
            sent.wait_recv()
            own[...] = own[...] + found[...]
        near_part = owner_block(own, by_rows, side)
        away_part = owner_block(own, by_rows, 1 - side)
        target = shard_part(out, by_rows, part, mine)
        own_copies.append(local(near_part, target))
        return [
            remote(away_part, target, to_diagonal),
            remote(near_part, target, to_ctx),
            remote(away_part, target, to_pair),
        ]

    grad_q, grad_k, grad_v, grad_o, grad_g, grad_u, grad_d = grads
    line_d = line_first(grad_d, True, d_out, part_f, dy_all, hidden)
    line_g = line_first(grad_g, False, g_out, part_f, h2, d_gate)
    line_u = line_first(grad_u, False, u_out, part_f, h2, d_up)

    middle = scatter_relay(0, middle)
    d_normed = scatter_end(0, middle)
    unit_two = resid[...] * inv_two
    gains[1:2, mine_half] = jnp.sum(d_normed * unit_two, axis=0, keepdims=True)
    scaled = d_normed * mlp_gain_ref[:, mine_half]
    dot = core_sum(1, jnp.sum(scaled * unit_two, axis=-1, keepdims=True))
    d_resid_half = dy_ref[:, mine_half].astype(F32) + inv_two * (scaled - unit_two * (dot / width))
    d_resid[...] = d_resid_half
    drb[rows_of(0), mine_half] = d_resid_half.astype(BF16)
    gather_drb = gather_start(drb, True)
    output_first = scatter_start(1, lambda here: mm(hidden[here, :], wd[...]), {})
    line_d = line_second(line_d)
    line_g = line_second(line_g)

    def d_attend(slot):
        here = rows_of(slot)
        d_attn[here, :] = mm_nt(drb[here, :], wo[...]).astype(BF16)

    gather_near(gather_drb)
    d_attend(0)
    passed = [gather_pass(gather_drb, slot) for slot in (1, 2)]
    passed[0].wait_recv()
    d_attend(1)
    passed.append(gather_pass(gather_drb, 3))

    def attend_back(seq, carry):
        here = pl.ds(pl.multiple_of(seq * length, length), length)
        key, value = kr[here, :], vr[here, :]
        cos, sin = cos_ref[...], sin_ref[...]

        def unturn(d_rot):
            return d_rot * cos - pltpu.roll(d_rot, HD // 2, 1) * sin

        def norm_head(d_scaled, unit, inverse, gain):
            gained = d_scaled * gain
            mean = jnp.mean(gained * unit, axis=-1, keepdims=True)
            return (inverse * (gained - unit * mean)).astype(BF16)

        d_key = jnp.zeros((length, HD), F32)
        d_value = jnp.zeros((length, HD), F32)
        query_part, key_part = carry
        for at in range(group):
            columns = slice(at * HD, (at + 1) * HD)
            query, d_mixed = qr[here, columns], d_attn[here, columns]
            delta = jnp.sum(
                d_mixed.astype(F32) * attn[here, columns].astype(F32), axis=-1, keepdims=True
            )
            probs = jnp.exp(masked_scores(query, key) - lse[at, here, :])
            d_scores = (probs * (mm_nt(d_mixed, value) - delta) * score_scale).astype(BF16)
            d_scaled = unturn(mm(d_scores, key))
            unit = uq[here, columns]
            query_part = query_part + jnp.sum(d_scaled * unit, axis=0, keepdims=True)
            d_qkv[here, columns] = norm_head(
                d_scaled, unit, invq[at, here, :], query_gain_ref[...]
            )
            d_key = d_key + mm_tn(d_scores, query)
            d_value = d_value + mm_tn(probs.astype(BF16), d_mixed)
        d_scaled = unturn(d_key)
        unit = uk[here, :]
        key_part = key_part + jnp.sum(d_scaled * unit, axis=0, keepdims=True)
        d_qkv[here, part_q : part_q + part_k] = norm_head(
            d_scaled, unit, invk[0, here, :], key_gain_ref[...]
        )
        d_qkv[here, part_q + part_k : part_q + 2 * part_k] = d_value.astype(BF16)
        return query_part, key_part

    empty = jnp.zeros((1, HD), F32)
    gain_parts = lax.fori_loop(0, 1, attend_back, (empty, empty))
    line_u = line_second(line_u)
    passed[1].wait_recv()
    d_attend(2)
    passed[2].wait_recv()
    d_attend(3)
    line_o = line_first(grad_o, True, o_out, part_q, drb, attn)
    output_middle = scatter_middle(1, output_first)
    query_part, key_part = lax.fori_loop(1, 2, attend_back, gain_parts)
    output_middle = scatter_relay(1, output_middle)
    gains[2:3, 0:HD] = query_part
    gains[3:4, 0:HD] = key_part

    def columns_of(start, size):
        return d_qkv.at[:, start : start + size]

    line_q = line_first(grad_q, False, q_out, part_q, h1, columns_of(0, part_q))
    line_k = line_first(grad_k, False, k_out, part_k, h1, columns_of(part_q, part_k))
    line_v = line_first(grad_v, False, v_out, part_k, h1, columns_of(part_q + part_k, part_k))

    def d_project(here):
        d_query = d_qkv[here, 0:part_q]
        d_key = d_qkv[here, part_q : part_q + part_k]
        d_value = d_qkv[here, part_q + part_k : part_q + 2 * part_k]
        return mm_nt(d_query, wq[...]) + mm_nt(d_key, wk[...]) + mm_nt(d_value, wv[...])

    first = scatter_start(0, d_project, {})
    middle = scatter_middle(0, first)
    line_o = line_second(line_o)
    out_half = (resid[...] + scatter_end(1, output_middle)).astype(BF16)
    out_ref[:, mine_half] = out_half
    out_copy = remote(out_ref.at[:, mine_half], out_ref.at[:, mine_half], to_core)
    middle = scatter_relay(0, middle)
    line_q = line_second(line_q)
    line_k = line_second(line_k)
    line_v = line_second(line_v)
    spread = line_third(line_d)

    d_normed = scatter_end(0, middle)
    tokens_half = x_ref[:, mine_half].astype(F32)
    unit_one = tokens_half * inv_one
    gains[0:1, mine_half] = jnp.sum(d_normed * unit_one, axis=0, keepdims=True)
    scaled = d_normed * attn_gain_ref[:, mine_half]
    dot = core_sum(2, jnp.sum(scaled * unit_one, axis=-1, keepdims=True))
    d_input_half = d_resid[...] + inv_one * (scaled - unit_one * (dot / width))
    d_input_ref[:, mine_half] = d_input_half.astype(BF16)
    in_copy = remote(d_input_ref.at[:, mine_half], d_input_ref.at[:, mine_half], to_core)

    rounds = [to_core, to_ctx]
    stride = 1
    while stride < dp_size:
        rounds.append(at_dp(stride))
        stride *= 2
    later = [line_g, line_u, line_o, line_q, line_k, line_v]
    for i, device in enumerate(rounds):
        copy = remote(gains, gains_in.at[i], device)
        if len(later) > 3:
            spread += line_third(later.pop(0))
        copy.wait_recv()
        wait_sent(copy)
        gains[...] = gains[...] + gains_in[i]
    gains_ref[...] = gains[...]
    for handles in later:
        spread += line_third(handles)
    for copy in spread + [out_copy, in_copy]:
        copy.wait_recv()
    for copy in own_copies:
        copy.wait()
    for copy in unsent:
        copy.wait_send()


def finish_kernel(share, owned, count, *refs):
    gains_ref, sources = refs[0], refs[1 : 1 + count]
    attn_ref, mlp_ref, query_ref, key_ref = refs[1 + count : 5 + count]
    targets, rooms = refs[5 + count : 5 + 2 * count], refs[5 + 2 * count]
    in_sems, out_sems = refs[6 + 2 * count :]
    places = [(source, room, in_sems.at[i]) for i, (source, room) in enumerate(zip(sources, rooms))]
    moves = [pltpu.make_async_copy(*place) for place in places]
    for move in moves:
        move.start()
    owner = lax.axis_index("dp")
    place = pl.ds(pl.multiple_of(owner * owned, 128), owned)
    attn_ref[...] = gains_ref[0:1, place]
    mlp_ref[...] = gains_ref[1:2, place]
    shift = lax.rem(HD - owner * share, HD)
    query_ref[...] = pltpu.roll(gains_ref[2:3, 0:HD], shift, 1)
    key_ref[...] = pltpu.roll(gains_ref[3:4, 0:HD], shift, 1)
    written = []
    for i, move in enumerate(moves):
        move.wait()
        written.append(pltpu.make_async_copy(rooms[i], targets[i], out_sems.at[i]))
        written[i].start()
    for move in written:
        move.wait()


def fused_device(
    dp_size,
    block_input,
    attn_gain,
    query_weight,
    key_weight,
    value_weight,
    query_gain,
    key_gain,
    output_weight,
    mlp_gain,
    gate_weight,
    up_weight,
    down_weight,
    cotangent,
):
    rows, width = block_input.shape[1:]
    block = lax.axis_index("ctx")
    half = width // 2
    owned = width // dp_size
    part_q = query_weight.shape[1] // 4
    part_k = key_weight.shape[1] // 4
    part_f = gate_weight.shape[1] // 4
    span = 2 * owned
    tokens = 4 * rows
    index = jnp.arange(rows, dtype=jnp.int32)
    positions = jnp.concatenate([block * rows + index, (1 - block) * rows + index])
    cos_table, sin_table = rope_tables(positions, HD)
    sin_table = jnp.concatenate([-sin_table[:, : HD // 2], sin_table[:, HD // 2 :]], axis=1)
    vmem = pl.BlockSpec(memory_space=pltpu.VMEM)
    hbm = pl.BlockSpec(memory_space=pl.ANY)

    def shape(dims, kind):
        return jax.ShapeDtypeStruct(dims, kind)

    def grad_room(by_rows, part):
        dims = (part, span) if by_rows else (span, part)
        return (
            pltpu.VMEM(dims, F32),
            pltpu.VMEM(dims, F32),
            pltpu.VMEM((2,) + dims, BF16),
            pltpu.VMEM((2,) + dims, BF16),
            pltpu.VMEM(dims, F32),
        )

    weights = (
        query_weight,
        key_weight,
        value_weight,
        output_weight,
        gate_weight,
        up_weight,
        down_weight,
    )
    group = part_q // part_k
    sizes = (dp_size, rows, width, part_q, part_k, part_f)
    copies = 3 * (dp_size - 1) + 4 * 4 + 4 * 7 + 4 * 10 + 3 + 7 * 6 + 2 + 8
    results = pl.pallas_call(
        functools.partial(layer_kernel, sizes),
        out_shape=(
            shape((rows, width), BF16),
            shape((rows, width), BF16),
            shape((8, width), F32),
        )
        + tuple(shape(weight.shape, F32) for weight in weights),
        in_specs=[vmem] * 8 + [hbm] * 7,
        out_specs=(vmem,) * 3 + (hbm,) * 7,
        scratch_shapes=[
            pltpu.VMEM((width, part_q), BF16),
            pltpu.VMEM((width, part_k), BF16),
            pltpu.VMEM((width, part_k), BF16),
            pltpu.VMEM((part_q, width), BF16),
            pltpu.VMEM((width, part_f), BF16),
            pltpu.VMEM((width, part_f), BF16),
            pltpu.VMEM((part_f, width), BF16),
            [
                grad_room(False, part_q),
                grad_room(False, part_k),
                grad_room(False, part_k),
                grad_room(True, part_q),
                grad_room(False, part_f),
                grad_room(False, part_f),
                grad_room(True, part_f),
            ],
            pltpu.VMEM((tokens, width), BF16),
            pltpu.VMEM((tokens, width), BF16),
            pltpu.VMEM((tokens, width), BF16),
            pltpu.VMEM((tokens, width), BF16),
            pltpu.VMEM((tokens, part_q), F32),
            pltpu.VMEM((tokens, part_k), F32),
            pltpu.VMEM((group, tokens, 1), F32),
            pltpu.VMEM((1, tokens, 1), F32),
            pltpu.VMEM((tokens, part_q), BF16),
            pltpu.VMEM((tokens, part_k), BF16),
            pltpu.VMEM((tokens, part_k), BF16),
            pltpu.VMEM((tokens, part_q), BF16),
            pltpu.VMEM((group, tokens, 1), F32),
            pltpu.VMEM((tokens, part_f), BF16),
            pltpu.VMEM((tokens, part_f), BF16),
            pltpu.VMEM((tokens, part_f), BF16),
            pltpu.VMEM((tokens, part_q), BF16),
            pltpu.VMEM((tokens, part_q + 2 * part_k), BF16),
            pltpu.VMEM((2, tokens, width), F32),
            pltpu.VMEM((2, tokens, half), F32),
            pltpu.VMEM((2, tokens, half), F32),
            pltpu.VMEM((2, 6, rows, half // 2), F32),
            pltpu.VMEM((rows, half), F32),
            pltpu.VMEM((rows, half), F32),
            pltpu.VMEM((3, rows, HD), F32),
            pltpu.VMEM((3, rows, HD), F32),
            pltpu.VMEM((8, width), F32),
            pltpu.VMEM((8, 8, width), F32),
            pltpu.SemaphoreType.DMA((copies,)),
            pltpu.SemaphoreType.DMA((copies,)),
            pltpu.SemaphoreType.DMA((14,)),
        ],
        compiler_params=pltpu.CompilerParams(
            collective_id=0, has_side_effects=True, vmem_limit_bytes=63 * 1024 * 1024
        ),
        cost_estimate=pl.CostEstimate(
            flops=24 * tokens * width * (part_q + part_k + part_f),
            bytes_accessed=8 * width * width,
            transcendentals=0,
        ),
    )(
        block_input[0],
        cotangent[0],
        attn_gain[None],
        mlp_gain[None],
        query_gain[None],
        key_gain[None],
        cos_table,
        sin_table,
        *weights,
    )
    gains = results[2]
    moved = results[:2] + results[3:]
    share = HD // dp_size
    finished = pl.pallas_call(
        functools.partial(finish_kernel, share, owned, len(moved)),
        out_shape=(
            shape((1, owned), F32),
            shape((1, owned), F32),
            shape((1, HD), F32),
            shape((1, HD), F32),
        )
        + tuple(shape(array.shape, array.dtype) for array in moved),
        in_specs=[vmem] + [hbm] * len(moved),
        out_specs=(vmem,) * 4 + (hbm,) * len(moved),
        scratch_shapes=[
            [pltpu.VMEM(array.shape, array.dtype) for array in moved],
            pltpu.SemaphoreType.DMA((len(moved),)),
            pltpu.SemaphoreType.DMA((len(moved),)),
        ],
        compiler_params=pltpu.CompilerParams(vmem_limit_bytes=32 * 1024 * 1024),
    )(gains, *moved)
    attn_share, mlp_share, query_row, key_row = finished[:4]
    output, d_input, grad_q, grad_k, grad_v, grad_o, grad_g, grad_u, grad_d = finished[4:]
    return (
        output[None],
        d_input[None],
        attn_share[0],
        grad_q,
        grad_k,
        grad_v,
        query_row[0, :share],
        key_row[0, :share],
        grad_o,
        mlp_share[0],
        grad_g,
        grad_u,
        grad_d,
    )


def solution(mesh):
    sizes = dict(mesh.shape)
    body = per_device
    if sizes["ctx"] == 2 and sizes["tensor"] == 2 and sizes["dp"] in (2, 4, 8):
        body = functools.partial(fused_device, sizes["dp"])
    return jax.shard_map(
        body,
        mesh=mesh,
        in_specs=(
            P("dp", "ctx", None),
            P(),
            P("dp", "tensor"),
            P("dp", "tensor"),
            P("dp", "tensor"),
            P(),
            P(),
            P("tensor", "dp"),
            P(),
            P("dp", "tensor"),
            P("dp", "tensor"),
            P("tensor", "dp"),
            P("dp", "ctx", None),
        ),
        out_specs=(
            P("dp", "ctx", None),
            P("dp", "ctx", None),
            P("dp"),
            P("dp", "tensor"),
            P("dp", "tensor"),
            P("dp", "tensor"),
            P("dp"),
            P("dp"),
            P("tensor", "dp"),
            P("dp"),
            P("dp", "tensor"),
            P("dp", "tensor"),
            P("tensor", "dp"),
        ),
        check_vma=False,
    )
```

```python
import functools
import math

import jax
import jax.numpy as jnp
from jax import lax
from jax.experimental import pallas as pl
from jax.experimental.pallas import tpu as pltpu
from jax.sharding import PartitionSpec as P

HD = 128


EPS = 1e-06
THETA = 1000000.0
F32 = jnp.float32
BF16 = jnp.bfloat16


def rms_inverse(value):
    return lax.rsqrt(jnp.mean(value * value, axis=-1, keepdims=True) + EPS)


def norm_back(grad, unit, inverse, gain):
    scaled = grad * gain
    return inverse * (scaled - unit * jnp.mean(scaled * unit, axis=-1, keepdims=True))


def rotate(value):
    half_width = value.shape[-1] // 2
    return jnp.concatenate([-value[..., half_width:], value[..., :half_width]], axis=-1)


def rotate_back(value):
    half_width = value.shape[-1] // 2
    return jnp.concatenate([value[..., half_width:], -value[..., :half_width]], axis=-1)


def rope_tables(positions, width):
    half_width = width // 2
    exponent = jnp.arange(half_width).astype(F32) * (2.0 / width)
    frequency = jnp.power(THETA, -exponent)
    angle = positions.astype(F32)[:, None] * frequency[None, :]
    angle = jnp.concatenate([angle, angle], axis=-1)
    return (jnp.cos(angle), jnp.sin(angle))


def over_heads(partial_value):
    return lax.psum(partial_value, "tensor")


def per_device(
    block_input,
    attn_gain,
    query_weight,
    key_weight,
    value_weight,
    query_gain,
    key_gain,
    output_weight,
    mlp_gain,
    gate_weight,
    up_weight,
    down_weight,
    cotangent,
):
    tokens = block_input[0].astype(F32)
    row_count = tokens.shape[0]
    score_scale = 1.0 / math.sqrt(HD)
    positions = lax.axis_index("ctx") * row_count + jnp.arange(row_count, dtype=jnp.int32)
    cos_table, sin_table = rope_tables(positions, HD)
    cos_heads = cos_table[:, None, :]
    sin_heads = sin_table[:, None, :]
    w_query, w_key, w_value, w_out, w_gate, w_up, w_down = (
        lax.all_gather(query_weight, "dp", axis=0, tiled=True),
        lax.all_gather(key_weight, "dp", axis=0, tiled=True),
        lax.all_gather(value_weight, "dp", axis=0, tiled=True),
        lax.all_gather(output_weight, "dp", axis=1, tiled=True),
        lax.all_gather(gate_weight, "dp", axis=0, tiled=True),
        lax.all_gather(up_weight, "dp", axis=0, tiled=True),
        lax.all_gather(down_weight, "dp", axis=1, tiled=True),
    )
    q_heads = w_query.shape[1] // HD
    kv_heads = w_key.shape[1] // HD
    group_size = q_heads // kv_heads
    inv_one = rms_inverse(tokens)
    unit_one = tokens * inv_one
    normed_one = (unit_one * attn_gain).astype(BF16)
    query = jnp.dot(normed_one, w_query, preferred_element_type=F32).reshape(row_count, q_heads, HD)
    key_raw = jnp.dot(normed_one, w_key, preferred_element_type=F32).reshape(
        row_count, kv_heads, HD
    )
    value = (
        jnp.dot(normed_one, w_value, preferred_element_type=F32)
        .astype(BF16)
        .reshape(row_count, kv_heads, HD)
    )
    query_inv = rms_inverse(query)
    query_unit = query * query_inv
    query_scaled = query_unit * query_gain
    query_rot = (query_scaled * cos_heads + rotate(query_scaled) * sin_heads).astype(BF16)
    key_inv = rms_inverse(key_raw)
    key_unit = key_raw * key_inv
    key_scaled = key_unit * key_gain
    key_rot = (key_scaled * cos_heads + rotate(key_scaled) * sin_heads).astype(BF16)
    grouped_query = query_rot.reshape(row_count, kv_heads, group_size, HD)

    def piece_scores(piece_keys):
        piece_rows = piece_keys.shape[0]
        key_positions = jnp.arange(piece_rows, dtype=jnp.int32)
        allowed = key_positions[None, :] <= positions[:, None]
        scores = (
            jnp.einsum("qkgd,nkd->kgqn", grouped_query, piece_keys, preferred_element_type=F32)
            * score_scale
        )
        return jnp.where(allowed, scores, -jnp.inf)

    peak_old = jnp.full((kv_heads, group_size, row_count), -1e30, F32)
    piece_keys = lax.all_gather(key_rot, "ctx", axis=0, tiled=True)
    piece_values = lax.all_gather(value, "ctx", axis=0, tiled=True)
    scores = piece_scores(piece_keys)
    peak_new = jnp.maximum(peak_old, jnp.max(scores, axis=-1))
    expo = jnp.exp(scores - peak_new[..., None])
    total_new = jnp.sum(expo, axis=-1)
    accum_new = jnp.einsum(
        "kgqn,nkd->kgqd", expo.astype(BF16), piece_values, preferred_element_type=F32
    )
    log_total = peak_new + jnp.log(total_new)
    attn = (
        (accum_new / total_new[..., None])
        .astype(BF16)
        .transpose(2, 0, 1, 3)
        .reshape(row_count, q_heads * HD)
    )
    resid = tokens + over_heads(jnp.dot(attn, w_out, preferred_element_type=F32))
    inv_two = rms_inverse(resid)
    unit_two = resid * inv_two
    normed_two = (unit_two * mlp_gain).astype(BF16)
    gate = jnp.dot(normed_two, w_gate, preferred_element_type=F32)
    up_proj = jnp.dot(normed_two, w_up, preferred_element_type=F32)
    sigma = jax.nn.sigmoid(gate)
    silu_gate = gate * sigma
    hidden = (silu_gate * up_proj).astype(BF16)
    output = (resid + over_heads(jnp.dot(hidden, w_down, preferred_element_type=F32))).astype(BF16)
    w_query, w_key, w_value, w_out, w_gate, w_up, w_down = (
        lax.all_gather(query_weight, "dp", axis=0, tiled=True),
        lax.all_gather(key_weight, "dp", axis=0, tiled=True),
        lax.all_gather(value_weight, "dp", axis=0, tiled=True),
        lax.all_gather(output_weight, "dp", axis=1, tiled=True),
        lax.all_gather(gate_weight, "dp", axis=0, tiled=True),
        lax.all_gather(up_weight, "dp", axis=0, tiled=True),
        lax.all_gather(down_weight, "dp", axis=1, tiled=True),
    )
    d_output = cotangent[0]
    d_hidden = jnp.einsum("td,fd->tf", d_output, w_down, preferred_element_type=F32)
    grad_down = jnp.einsum("tf,td->fd", hidden, d_output, preferred_element_type=F32)
    d_gate = (d_hidden * up_proj * sigma * (1.0 + gate * (1.0 - sigma))).astype(BF16)
    d_up = (d_hidden * silu_gate).astype(BF16)
    grad_gate = jnp.einsum("td,tf->df", normed_two, d_gate, preferred_element_type=F32)
    grad_up = jnp.einsum("td,tf->df", normed_two, d_up, preferred_element_type=F32)
    partial_two = jnp.einsum("tf,df->td", d_gate, w_gate, preferred_element_type=F32) + jnp.einsum(
        "tf,df->td", d_up, w_up, preferred_element_type=F32
    )
    d_normed_two = lax.psum(partial_two, "tensor")
    grad_mlp_gain = jnp.sum(d_normed_two * unit_two, axis=0)
    d_resid = d_output.astype(F32) + norm_back(d_normed_two, unit_two, inv_two, mlp_gain)
    d_resid_b = d_resid.astype(BF16)
    grad_out = jnp.einsum("th,td->hd", attn, d_resid_b, preferred_element_type=F32)
    d_attn = jnp.einsum("td,hd->th", d_resid_b, w_out, preferred_element_type=F32).astype(BF16)
    delta = jnp.sum(
        d_attn.astype(F32).reshape(row_count, q_heads, HD)
        * attn.astype(F32).reshape(row_count, q_heads, HD),
        axis=-1,
    )
    delta_heads = delta.reshape(row_count, kv_heads, group_size).transpose(1, 2, 0)
    grouped_grad = d_attn.reshape(row_count, kv_heads, group_size, HD)
    piece_keys = lax.all_gather(key_rot, "ctx", axis=0, tiled=True)
    piece_values = lax.all_gather(value, "ctx", axis=0, tiled=True)
    piece_rows = piece_keys.shape[0]
    scores = piece_scores(piece_keys)
    probs = jnp.exp(scores - log_total[..., None])
    d_probs = jnp.einsum("qkgd,nkd->kgqn", grouped_grad, piece_values, preferred_element_type=F32)
    d_scores = (probs * (d_probs - delta_heads[..., None]) * score_scale).astype(BF16)
    d_query_acc = jnp.einsum("kgqn,nkd->kgqd", d_scores, piece_keys, preferred_element_type=F32)
    d_key_piece = jnp.einsum("kgqn,qkgd->nkd", d_scores, grouped_query, preferred_element_type=F32)
    d_value_piece = jnp.einsum(
        "kgqn,qkgd->nkd", probs.astype(BF16), grouped_grad, preferred_element_type=F32
    )
    update = jnp.stack([d_key_piece, d_value_piece])
    d_kv_home = lax.psum_scatter(update, "ctx", scatter_dimension=1, tiled=True)
    d_query_rot = d_query_acc.transpose(2, 0, 1, 3).reshape(row_count, q_heads, HD)
    d_key_rot = d_kv_home[0]
    d_value = d_kv_home[1].astype(BF16).reshape(row_count, kv_heads * HD)
    d_query_scaled = d_query_rot * cos_heads + rotate_back(d_query_rot * sin_heads)
    d_key_scaled = d_key_rot * cos_heads + rotate_back(d_key_rot * sin_heads)
    query_gain_part = jnp.sum(d_query_scaled * query_unit, axis=(0, 1))
    key_gain_part = jnp.sum(d_key_scaled * key_unit, axis=(0, 1))
    d_query = (
        norm_back(d_query_scaled, query_unit, query_inv, query_gain)
        .astype(BF16)
        .reshape(row_count, q_heads * HD)
    )
    d_key = (
        norm_back(d_key_scaled, key_unit, key_inv, key_gain)
        .astype(BF16)
        .reshape(row_count, kv_heads * HD)
    )
    grad_query = jnp.einsum("td,th->dh", normed_one, d_query, preferred_element_type=F32)
    grad_key = jnp.einsum("td,th->dh", normed_one, d_key, preferred_element_type=F32)
    grad_value = jnp.einsum("td,th->dh", normed_one, d_value, preferred_element_type=F32)
    partial_one = jnp.einsum("th,dh->td", d_query, w_query, preferred_element_type=F32)
    partial_one = partial_one + jnp.einsum("th,dh->td", d_key, w_key, preferred_element_type=F32)
    partial_one = partial_one + jnp.einsum(
        "th,dh->td", d_value, w_value, preferred_element_type=F32
    )
    d_normed_one, query_gain_heads, key_gain_heads = lax.psum(
        (partial_one, query_gain_part, key_gain_part), "tensor"
    )
    grad_attn_gain = jnp.sum(d_normed_one * unit_one, axis=0)
    d_input = (d_resid + norm_back(d_normed_one, unit_one, inv_one, attn_gain)).astype(BF16)
    (
        share_a,
        share_q,
        share_k,
        share_v,
        share_qg,
        share_kg,
        share_o,
        share_m,
        share_g,
        share_u,
        share_d,
    ) = (
        lax.psum_scatter(grad_attn_gain, "dp", scatter_dimension=0, tiled=True),
        lax.psum_scatter(grad_query, "dp", scatter_dimension=0, tiled=True),
        lax.psum_scatter(grad_key, "dp", scatter_dimension=0, tiled=True),
        lax.psum_scatter(grad_value, "dp", scatter_dimension=0, tiled=True),
        lax.psum_scatter(query_gain_heads, "dp", scatter_dimension=0, tiled=True),
        lax.psum_scatter(key_gain_heads, "dp", scatter_dimension=0, tiled=True),
        lax.psum_scatter(grad_out, "dp", scatter_dimension=1, tiled=True),
        lax.psum_scatter(grad_mlp_gain, "dp", scatter_dimension=0, tiled=True),
        lax.psum_scatter(grad_gate, "dp", scatter_dimension=0, tiled=True),
        lax.psum_scatter(grad_up, "dp", scatter_dimension=0, tiled=True),
        lax.psum_scatter(grad_down, "dp", scatter_dimension=1, tiled=True),
    )
    finals = lax.psum(
        (
            share_a,
            share_q,
            share_k,
            share_v,
            share_qg,
            share_kg,
            share_o,
            share_m,
            share_g,
            share_u,
            share_d,
        ),
        "ctx",
    )
    return (
        output[None],
        d_input[None],
        finals[0],
        finals[1],
        finals[2],
        finals[3],
        finals[4],
        finals[5],
        finals[6],
        finals[7],
        finals[8],
        finals[9],
        finals[10],
    )


MESH = pl.DeviceIdType.MESH


def mm(a, b):
    return lax.dot_general(a, b, (((1,), (0,)), ((), ())), preferred_element_type=F32)


def mm_nt(a, b):
    return lax.dot_general(a, b, (((1,), (1,)), ((), ())), preferred_element_type=F32)


def mm_tn(a, b):
    return lax.dot_general(a, b, (((0,), (0,)), ((), ())), preferred_element_type=F32)


def layer_kernel(
    sizes,
    x_ref,
    dy_ref,
    attn_gain_ref,
    mlp_gain_ref,
    query_gain_ref,
    key_gain_ref,
    cos_ref,
    sin_ref,
    q_in,
    k_in,
    v_in,
    o_in,
    g_in,
    u_in,
    d_in,
    out_ref,
    d_input_ref,
    gains_ref,
    q_out,
    k_out,
    v_out,
    o_out,
    g_out,
    u_out,
    d_out,
    wq,
    wk,
    wv,
    wo,
    wg,
    wu,
    wd,
    grads,
    h1,
    dy_all,
    h2,
    drb,
    uq,
    uk,
    invq,
    invk,
    qr,
    kr,
    vr,
    attn,
    lse,
    hidden,
    d_gate,
    d_up,
    d_attn,
    d_qkv,
    partial,
    landing,
    acc,
    arrived,
    resid,
    d_resid,
    stat,
    stat_in,
    gains,
    gains_in,
    send_sem,
    recv_sem,
    local_sem,
):
    dp_size, rows, width, part_q, part_k, part_f = sizes
    owned = width // dp_size
    half = width // 2
    length = 2 * rows
    group = part_q // part_k
    score_scale = 1.0 / math.sqrt(HD)
    dp = lax.axis_index("dp")
    block = lax.axis_index("ctx")
    core = lax.axis_index("tensor")
    side = lax.rem(dp, 2)
    line = dp // 2
    lines = dp_size // 2
    mine = 2 * block + side

    def flip(value, bits):
        result = value
        bit = 1
        while bit <= bits:
            if bits & bit:
                result = result + bit * (1 - 2 * lax.rem(value // bit, 2))
            bit *= 2
        return result

    def at_dp(bits):
        return {"dp": flip(dp, bits), "ctx": block, "tensor": core}

    to_core = {"dp": dp, "ctx": block, "tensor": 1 - core}
    to_ctx = {"dp": dp, "ctx": 1 - block, "tensor": core}
    to_pair = at_dp(1)
    to_diagonal = {"dp": flip(dp, 1), "ctx": 1 - block, "tensor": core}
    slots = {1: to_ctx, 2: to_pair, 3: to_diagonal}

    barrier = pltpu.get_barrier_semaphore()
    peers = [to_core, to_ctx, to_diagonal] + [at_dp(bits) for bits in range(1, dp_size)]
    for peer in peers:
        pl.semaphore_signal(barrier, inc=1, device_id=peer, device_id_type=MESH)
    pl.semaphore_wait(barrier, len(peers))

    count = {"remote": 0, "local": 0}
    unsent = []
    own_copies = []

    def remote(src, dst, device):
        i = count["remote"]
        count["remote"] += 1
        copy = pltpu.make_async_remote_copy(
            src_ref=src,
            dst_ref=dst,
            send_sem=send_sem.at[i],
            recv_sem=recv_sem.at[i],
            device_id=device,
            device_id_type=MESH,
        )
        copy.start()
        unsent.append(copy)
        return copy

    def wait_sent(copy):
        copy.wait_send()
        unsent[:] = [other for other in unsent if other is not copy]

    def local(src, dst):
        i = count["local"]
        count["local"] += 1
        copy = pltpu.make_async_copy(src, dst, local_sem.at[i])
        copy.start()
        return copy

    def lanes(start, size):
        return pl.ds(pl.multiple_of(start, 128), size)

    def lines_of(start, size):
        return pl.ds(pl.multiple_of(start, 128), size)

    mine_half = lanes(core * half, half)
    other_half = lanes((1 - core) * half, half)

    def rows_of(slot):
        return pl.ds(slot * rows, rows)

    def shard_part(shard, by_rows, part, which):
        if by_rows:
            return shard.at[lines_of(which * part, part), :]
        return shard.at[:, lanes(which * part, part)]

    def owner_block(whole, by_rows, owner):
        if by_rows:
            return whole.at[:, lanes(owner * owned, owned)]
        return whole.at[lines_of(owner * owned, owned), :]

    span = 2 * owned

    def line_block(whole, by_rows, at):
        if by_rows:
            return whole.at[:, lanes(at * span, span)]
        return whole.at[lines_of(at * span, span), :]

    def weight_pair(shard, whole, by_rows, part):
        place = owner_block(whole, by_rows, dp)
        own = local(shard_part(shard, by_rows, part, mine), place)
        pair = remote(shard_part(shard, by_rows, part, 2 * block + 1 - side), place, to_pair)
        return whole, by_rows, own, pair

    def weight_first(handles):
        whole, by_rows, own, pair = handles
        own.wait()
        pair.wait_recv()
        place = line_block(whole, by_rows, line)
        cross = remote(place, place, at_dp(4)) if lines > 2 else None
        near = remote(place, place, at_dp(2)) if lines > 1 else None
        return whole, by_rows, near, cross

    def weight_second(handles):
        whole, by_rows, near, cross = handles
        found = [near] if lines > 1 else []
        if cross is not None:
            cross.wait_recv()
            place = line_block(whole, by_rows, flip(line, 2))
            found.append(remote(place, place, at_dp(2)))
        return found

    def weight_end(found):
        for copy in found:
            copy.wait_recv()

    def gather_start(buffer, with_core):
        own = buffer.at[rows_of(0), mine_half]
        first = remote(own, own, to_core) if with_core else None
        parts = {
            slot: remote(own, buffer.at[rows_of(slot), mine_half], slots[slot])
            for slot in (1, 2, 3)
        }
        return buffer, first, parts

    def gather_near(handles):
        buffer, first, parts = handles
        if first is not None:
            first.wait_recv()

    def gather_pass(handles, slot):
        buffer, first, parts = handles
        parts[slot].wait_recv()
        place = buffer.at[rows_of(slot), mine_half]
        return remote(place, place, to_core)

    def gather_end(handles):
        gather_near(handles)
        for copy in [gather_pass(handles, slot) for slot in (1, 2, 3)]:
            copy.wait_recv()

    order = (3, 2, 1, 0)

    def scatter_start(which, compute, copies, some=order):
        for slot in some:
            partial[which, rows_of(slot), :] = compute(rows_of(slot))
            copies[slot] = remote(
                partial.at[which, rows_of(slot), other_half],
                landing.at[which, rows_of(slot), :],
                to_core,
            )
        return copies

    quad = half // 2
    low, high = slice(0, quad), slice(quad, half)

    def scatter_middle(which, copies):
        def near_sum(slot):
            copies[slot].wait_recv()
            acc[which, rows_of(slot), :] = (
                partial[which, rows_of(slot), mine_half] + landing[which, rows_of(slot), :]
            )

        def forward(slot, part, place, device):
            return remote(acc.at[which, rows_of(slot), part], arrived.at[which, place], device)

        near_sum(3)
        relay_low = forward(3, low, 0, to_ctx)
        relay_high = forward(3, high, 1, to_pair)
        near_sum(2)
        sent = [forward(2, high, 3, to_pair)]
        near_sum(1)
        sent.append(forward(1, low, 2, to_ctx))
        near_sum(0)
        return copies, relay_low, relay_high, sent, forward

    def scatter_relay(which, handles):
        copies, relay_low, relay_high, sent, forward = handles
        relay_low.wait_recv()
        acc[which, rows_of(2), low] = acc[which, rows_of(2), low] + arrived[which, 0]
        sent.append(forward(2, low, 4, to_pair))
        relay_high.wait_recv()
        acc[which, rows_of(1), high] = acc[which, rows_of(1), high] + arrived[which, 1]
        sent.append(forward(1, high, 5, to_ctx))
        return list(copies.values()) + [relay_low, relay_high] + sent, sent

    def scatter_end(which, handles):
        copies, sent = handles
        for copy in sent:
            copy.wait_recv()
        own = acc[which, rows_of(0), :]
        total = jnp.concatenate(
            [
                own[:, low] + (arrived[which, 2] + arrived[which, 4]),
                own[:, high] + (arrived[which, 3] + arrived[which, 5]),
            ],
            axis=1,
        )
        for copy in copies:
            wait_sent(copy)
        return total

    def core_sum(which, value):
        stat[which] = jnp.broadcast_to(value, stat.shape[1:])
        copy = remote(stat.at[which], stat_in.at[which], to_core)
        copy.wait_recv()
        return value + stat_in[which][:, :1]

    firsts = [(q_in, wq, False, part_q), (k_in, wk, False, part_k), (v_in, wv, False, part_k)]
    firsts = [weight_pair(*each) for each in firsts]
    weight_o = weight_pair(o_in, wo, True, part_q)
    weight_g = weight_pair(g_in, wg, False, part_f)
    weight_u = weight_pair(u_in, wu, False, part_f)
    weight_d = weight_pair(d_in, wd, True, part_f)
    tokens = x_ref[...].astype(F32)
    inv_one = lax.rsqrt(jnp.mean(tokens * tokens, axis=-1, keepdims=True) + EPS)
    h1[rows_of(0), :] = (tokens * inv_one * attn_gain_ref[...]).astype(BF16)
    gather_one = gather_start(h1, False)
    firsts = [weight_first(handles) for handles in firsts]
    gains[...] = jnp.zeros_like(gains)
    dy_all[rows_of(0), :] = dy_ref[...]
    firsts = [weight_second(handles) for handles in firsts]
    weight_o = weight_first(weight_o)
    weight_g = weight_first(weight_g)
    weight_u = weight_first(weight_u)
    weight_d = weight_first(weight_d)
    gather_end(gather_one)
    for found in firsts:
        weight_end(found)
    gather_dy = gather_start(dy_all, False)

    def project(slot, carry):
        here = pl.ds(pl.multiple_of(slot * rows, rows), rows)
        table = pl.ds(pl.multiple_of(lax.rem(slot, 2) * rows, rows), rows)
        cos, sin = cos_ref[table, :], sin_ref[table, :]
        normed = h1[here, :]

        def head(raw, gain, unit_ref, inverse_ref, rot_ref, at):
            inverse = lax.rsqrt(jnp.mean(raw * raw, axis=-1, keepdims=True) + EPS)
            unit = raw * inverse
            scaled = unit * gain
            turned = scaled * cos + pltpu.roll(scaled, HD // 2, 1) * sin
            unit_ref[here, at * HD : (at + 1) * HD] = unit
            inverse_ref[at, here, :] = inverse
            rot_ref[here, at * HD : (at + 1) * HD] = turned.astype(BF16)

        query = mm(normed, wq[...])
        for at in range(group):
            raw = query[:, at * HD : (at + 1) * HD]
            head(raw, query_gain_ref[...], uq, invq, qr, at)
        head(mm(normed, wk[...]), key_gain_ref[...], uk, invk, kr, 0)
        vr[here, :] = mm(normed, wv[...]).astype(BF16)
        return carry

    lax.fori_loop(0, 4, project, 0)
    weight_o = weight_second(weight_o)

    def masked_scores(query, key):
        at_row = lax.broadcasted_iota(jnp.int32, (length, length), 0)
        at_column = lax.broadcasted_iota(jnp.int32, (length, length), 1)
        shift = block * rows
        row = jnp.where(at_row < rows, at_row + shift, at_row - shift)
        column = jnp.where(at_column < rows, at_column + shift, at_column - shift)
        return jnp.where(column <= row, mm_nt(query, key) * score_scale, -jnp.inf)

    def attend(seq, carry):
        here = pl.ds(pl.multiple_of(seq * length, length), length)
        key, value = kr[here, :], vr[here, :]
        for at in range(group):
            columns = slice(at * HD, (at + 1) * HD)
            scores = masked_scores(qr[here, columns], key)
            peak = jnp.max(scores, axis=-1, keepdims=True)
            expo = jnp.exp(scores - peak)
            total = jnp.sum(expo, axis=-1, keepdims=True)
            mixed = mm(expo.astype(BF16), value) / total
            attn[here, columns] = mixed.astype(BF16)
            lse[at, here, :] = peak + jnp.log(total)
        return carry

    def attend_once(seq):
        lax.fori_loop(seq, seq + 1, attend, 0)

    attend_once(1)
    weight_g = weight_second(weight_g)
    weight_end(weight_o)
    def project_out(here):
        return mm(attn[here, :], wo[...])

    first = scatter_start(0, project_out, {}, (3, 2))
    attend_once(0)
    first = scatter_start(0, project_out, first, (1, 0))
    middle = scatter_middle(0, first)
    gather_end(gather_dy)
    middle = scatter_relay(0, middle)
    weight_u = weight_second(weight_u)
    resid_half = x_ref[:, mine_half].astype(F32) + scatter_end(0, middle)
    resid[...] = resid_half
    square = core_sum(0, jnp.sum(resid_half * resid_half, axis=-1, keepdims=True))
    inv_two = lax.rsqrt(square / width + EPS)
    unit_two = resid_half * inv_two
    h2[rows_of(0), mine_half] = (unit_two * mlp_gain_ref[:, mine_half]).astype(BF16)
    gather_two = gather_start(h2, True)
    weight_d = weight_second(weight_d)
    weight_end(weight_g)
    weight_end(weight_u)
    weight_end(weight_d)

    def feed(slot):
        here = rows_of(slot)
        normed = h2[here, :]
        gated, raised = mm(normed, wg[...]), mm(normed, wu[...])
        d_hidden = mm_nt(dy_all[here, :], wd[...])
        sigma = jax.nn.sigmoid(gated)
        silu_gate = gated * sigma
        hidden[here, :] = (silu_gate * raised).astype(BF16)
        d_gate[here, :] = (d_hidden * raised * sigma * (1.0 + gated * (1.0 - sigma))).astype(BF16)
        d_up[here, :] = (d_hidden * silu_gate).astype(BF16)

    gather_near(gather_two)
    feed(0)
    passed = [gather_pass(gather_two, slot) for slot in (1, 2)]
    passed[0].wait_recv()
    feed(1)
    passed.append(gather_pass(gather_two, 3))
    passed[1].wait_recv()
    feed(2)
    passed[2].wait_recv()
    feed(3)

    def feed_back(here):
        return mm_nt(d_gate[here, :], wg[...]) + mm_nt(d_up[here, :], wu[...])

    first = scatter_start(0, feed_back, {})
    middle = scatter_middle(0, first)

    def line_far(grad, by_rows, out, part, features, columns):
        own, cross, rounded, land, found = grad

        def block_grad(at):
            place = lanes(at * span, span)
            if by_rows:
                return mm_tn(columns[...], features[:, place])
            return mm_tn(features[:, place], columns[...])

        far = None
        if lines > 2:
            rounded[0] = block_grad(flip(line, 3)).astype(BF16)
            far = remote(rounded.at[0], land.at[0], at_dp(2))
        return grad, by_rows, out, part, far, block_grad

    def line_first(handles):
        grad, by_rows, out, part, far, block_grad = handles
        own, cross, rounded, land, found = grad
        if lines > 2:
            cross[...] = block_grad(flip(line, 2))
        if lines > 1:
            rounded[1] = block_grad(flip(line, 1)).astype(BF16)
        own[...] = block_grad(line)
        return grad, by_rows, out, part, far

    def line_second(handles):
        grad, by_rows, out, part, far = handles
        own, cross, rounded, land, found = grad
        sent = near = None
        if far is not None:
            far.wait_recv()
            cross[...] = cross[...] + land[0].astype(F32)
            sent = remote(cross, found, at_dp(4))
        if lines > 1:
            near = remote(rounded.at[1], land.at[1], at_dp(2))
        return grad, by_rows, out, part, near, sent

    def line_third(handles):
        grad, by_rows, out, part, near, sent = handles
        own, cross, rounded, land, found = grad
        if near is not None:
            near.wait_recv()
            own[...] = own[...] + land[1].astype(F32)
        if sent is not None:
            sent.wait_recv()
            own[...] = own[...] + found[...]
        near_part = owner_block(own, by_rows, side)
        away_part = owner_block(own, by_rows, 1 - side)
        target = shard_part(out, by_rows, part, mine)
        own_copies.append(local(near_part, target))
        return [
            remote(away_part, target, to_diagonal),
            remote(near_part, target, to_ctx),
            remote(away_part, target, to_pair),
        ]

    grad_q, grad_k, grad_v, grad_o, grad_g, grad_u, grad_d = grads
    line_d = line_far(grad_d, True, d_out, part_f, dy_all, hidden)
    line_g = line_far(grad_g, False, g_out, part_f, h2, d_gate)
    line_u = line_far(grad_u, False, u_out, part_f, h2, d_up)

    line_d = line_first(line_d)
    line_g = line_first(line_g)
    line_d = line_second(line_d)
    middle = scatter_relay(0, middle)
    line_u = line_first(line_u)
    line_g = line_second(line_g)
    line_u = line_second(line_u)
    d_normed = scatter_end(0, middle)
    unit_two = resid[...] * inv_two
    gains[1:2, mine_half] = jnp.sum(d_normed * unit_two, axis=0, keepdims=True)
    scaled = d_normed * mlp_gain_ref[:, mine_half]
    dot = core_sum(1, jnp.sum(scaled * unit_two, axis=-1, keepdims=True))
    d_resid_half = dy_ref[:, mine_half].astype(F32) + inv_two * (scaled - unit_two * (dot / width))
    d_resid[...] = d_resid_half
    drb[rows_of(0), mine_half] = d_resid_half.astype(BF16)
    gather_drb = gather_start(drb, True)
    output_first = scatter_start(1, lambda here: mm(hidden[here, :], wd[...]), {})

    def d_attend(slot):
        here = rows_of(slot)
        d_attn[here, :] = mm_nt(drb[here, :], wo[...]).astype(BF16)

    gather_near(gather_drb)
    d_attend(0)
    passed = [gather_pass(gather_drb, slot) for slot in (1, 2)]
    passed[0].wait_recv()
    d_attend(1)
    passed.append(gather_pass(gather_drb, 3))

    def attend_back(seq, carry):
        here = pl.ds(pl.multiple_of(seq * length, length), length)
        key, value = kr[here, :], vr[here, :]
        cos, sin = cos_ref[...], sin_ref[...]

        def unturn(d_rot):
            return d_rot * cos - pltpu.roll(d_rot, HD // 2, 1) * sin

        def norm_head(d_scaled, unit, inverse, gain):
            gained = d_scaled * gain
            mean = jnp.mean(gained * unit, axis=-1, keepdims=True)
            return (inverse * (gained - unit * mean)).astype(BF16)

        d_key = jnp.zeros((length, HD), F32)
        d_value = jnp.zeros((length, HD), F32)
        query_part, key_part = carry
        for at in range(group):
            columns = slice(at * HD, (at + 1) * HD)
            query, d_mixed = qr[here, columns], d_attn[here, columns]
            delta = jnp.sum(
                d_mixed.astype(F32) * attn[here, columns].astype(F32), axis=-1, keepdims=True
            )
            probs = jnp.exp(masked_scores(query, key) - lse[at, here, :])
            d_scores = (probs * (mm_nt(d_mixed, value) - delta) * score_scale).astype(BF16)
            d_scaled = unturn(mm(d_scores, key))
            unit = uq[here, columns]
            query_part = query_part + jnp.sum(d_scaled * unit, axis=0, keepdims=True)
            d_qkv[here, columns] = norm_head(
                d_scaled, unit, invq[at, here, :], query_gain_ref[...]
            )
            d_key = d_key + mm_tn(d_scores, query)
            d_value = d_value + mm_tn(probs.astype(BF16), d_mixed)
        d_scaled = unturn(d_key)
        unit = uk[here, :]
        key_part = key_part + jnp.sum(d_scaled * unit, axis=0, keepdims=True)
        d_qkv[here, part_q : part_q + part_k] = norm_head(
            d_scaled, unit, invk[0, here, :], key_gain_ref[...]
        )
        d_qkv[here, part_q + part_k : part_q + 2 * part_k] = d_value.astype(BF16)
        return query_part, key_part

    empty = jnp.zeros((1, HD), F32)
    gain_parts = lax.fori_loop(0, 1, attend_back, (empty, empty))
    passed[1].wait_recv()
    d_attend(2)
    passed[2].wait_recv()
    d_attend(3)
    line_o = line_far(grad_o, True, o_out, part_q, drb, attn)
    line_o = line_first(line_o)
    output_middle = scatter_middle(1, output_first)
    query_part, key_part = lax.fori_loop(1, 2, attend_back, gain_parts)
    output_middle = scatter_relay(1, output_middle)
    gains[2:3, 0:HD] = query_part
    gains[3:4, 0:HD] = key_part

    def columns_of(start, size):
        return d_qkv.at[:, start : start + size]

    line_q = line_far(grad_q, False, q_out, part_q, h1, columns_of(0, part_q))
    line_k = line_far(grad_k, False, k_out, part_k, h1, columns_of(part_q, part_k))
    line_v = line_far(grad_v, False, v_out, part_k, h1, columns_of(part_q + part_k, part_k))

    line_q = line_first(line_q)
    line_k = line_first(line_k)
    line_v = line_first(line_v)
    line_o = line_second(line_o)

    def d_project(here):
        d_query = d_qkv[here, 0:part_q]
        d_key = d_qkv[here, part_q : part_q + part_k]
        d_value = d_qkv[here, part_q + part_k : part_q + 2 * part_k]
        return mm_nt(d_query, wq[...]) + mm_nt(d_key, wk[...]) + mm_nt(d_value, wv[...])

    first = scatter_start(0, d_project, {})
    middle = scatter_middle(0, first)
    line_q = line_second(line_q)
    line_k = line_second(line_k)
    line_v = line_second(line_v)
    middle = scatter_relay(0, middle)
    spread = line_third(line_d)
    out_half = (resid[...] + scatter_end(1, output_middle)).astype(BF16)
    out_ref[:, mine_half] = out_half
    out_copy = remote(out_ref.at[:, mine_half], out_ref.at[:, mine_half], to_core)
    spread += line_third(line_g)

    d_normed = scatter_end(0, middle)
    tokens_half = x_ref[:, mine_half].astype(F32)
    unit_one = tokens_half * inv_one
    gains[0:1, mine_half] = jnp.sum(d_normed * unit_one, axis=0, keepdims=True)
    scaled = d_normed * attn_gain_ref[:, mine_half]
    dot = core_sum(2, jnp.sum(scaled * unit_one, axis=-1, keepdims=True))
    d_input_half = d_resid[...] + inv_one * (scaled - unit_one * (dot / width))
    d_input_ref[:, mine_half] = d_input_half.astype(BF16)
    in_copy = remote(d_input_ref.at[:, mine_half], d_input_ref.at[:, mine_half], to_core)

    rounds = [to_core, to_ctx]
    stride = 1
    while stride < dp_size:
        rounds.append(at_dp(stride))
        stride *= 2
    later = [line_u, line_o, line_q, line_k, line_v]
    for i, device in enumerate(rounds):
        copy = remote(gains, gains_in.at[i], device)
        if later:
            spread += line_third(later.pop(0))
        copy.wait_recv()
        wait_sent(copy)
        gains[...] = gains[...] + gains_in[i]
    gains_ref[...] = gains[...]
    for handles in later:
        spread += line_third(handles)
    for copy in spread + [out_copy, in_copy]:
        copy.wait_recv()
    for copy in own_copies:
        copy.wait()
    for copy in unsent:
        copy.wait_send()


def finish_kernel(share, owned, count, *refs):
    gains_ref, sources = refs[0], refs[1 : 1 + count]
    attn_ref, mlp_ref, query_ref, key_ref = refs[1 + count : 5 + count]
    targets, rooms = refs[5 + count : 5 + 2 * count], refs[5 + 2 * count]
    in_sems, out_sems = refs[6 + 2 * count :]
    places = [(source, room, in_sems.at[i]) for i, (source, room) in enumerate(zip(sources, rooms))]
    moves = [pltpu.make_async_copy(*place) for place in places]
    for move in moves:
        move.start()
    owner = lax.axis_index("dp")
    place = pl.ds(pl.multiple_of(owner * owned, 128), owned)
    attn_ref[...] = gains_ref[0:1, place]
    mlp_ref[...] = gains_ref[1:2, place]
    shift = lax.rem(HD - owner * share, HD)
    query_ref[...] = pltpu.roll(gains_ref[2:3, 0:HD], shift, 1)[:, :share]
    key_ref[...] = pltpu.roll(gains_ref[3:4, 0:HD], shift, 1)[:, :share]
    written = []
    for i, move in enumerate(moves):
        move.wait()
        written.append(pltpu.make_async_copy(rooms[i], targets[i], out_sems.at[i]))
        written[i].start()
    for move in written:
        move.wait()


def fused_device(
    dp_size,
    block_input,
    attn_gain,
    query_weight,
    key_weight,
    value_weight,
    query_gain,
    key_gain,
    output_weight,
    mlp_gain,
    gate_weight,
    up_weight,
    down_weight,
    cotangent,
):
    rows, width = block_input.shape[1:]
    block = lax.axis_index("ctx")
    half = width // 2
    owned = width // dp_size
    part_q = query_weight.shape[1] // 4
    part_k = key_weight.shape[1] // 4
    part_f = gate_weight.shape[1] // 4
    span = 2 * owned
    tokens = 4 * rows
    index = jnp.arange(rows, dtype=jnp.int32)
    positions = jnp.concatenate([block * rows + index, (1 - block) * rows + index])
    cos_table, sin_table = rope_tables(positions, HD)
    sin_table = jnp.concatenate([-sin_table[:, : HD // 2], sin_table[:, HD // 2 :]], axis=1)
    vmem = pl.BlockSpec(memory_space=pltpu.VMEM)
    hbm = pl.BlockSpec(memory_space=pl.ANY)

    def shape(dims, kind):
        return jax.ShapeDtypeStruct(dims, kind)

    def grad_room(by_rows, part):
        dims = (part, span) if by_rows else (span, part)
        return (
            pltpu.VMEM(dims, F32),
            pltpu.VMEM(dims, F32),
            pltpu.VMEM((2,) + dims, BF16),
            pltpu.VMEM((2,) + dims, BF16),
            pltpu.VMEM(dims, F32),
        )

    weights = (
        query_weight,
        key_weight,
        value_weight,
        output_weight,
        gate_weight,
        up_weight,
        down_weight,
    )
    group = part_q // part_k
    sizes = (dp_size, rows, width, part_q, part_k, part_f)
    copies = 7 * 4 + 4 * 7 + 4 * 10 + 3 + 7 * 6 + 2 + 8
    results = pl.pallas_call(
        functools.partial(layer_kernel, sizes),
        out_shape=(
            shape((rows, width), BF16),
            shape((rows, width), BF16),
            shape((8, width), F32),
        )
        + tuple(shape(weight.shape, F32) for weight in weights),
        in_specs=[vmem] * 8 + [hbm] * 7,
        out_specs=(vmem,) * 3 + (hbm,) * 7,
        scratch_shapes=[
            pltpu.VMEM((width, part_q), BF16),
            pltpu.VMEM((width, part_k), BF16),
            pltpu.VMEM((width, part_k), BF16),
            pltpu.VMEM((part_q, width), BF16),
            pltpu.VMEM((width, part_f), BF16),
            pltpu.VMEM((width, part_f), BF16),
            pltpu.VMEM((part_f, width), BF16),
            [
                grad_room(False, part_q),
                grad_room(False, part_k),
                grad_room(False, part_k),
                grad_room(True, part_q),
                grad_room(False, part_f),
                grad_room(False, part_f),
                grad_room(True, part_f),
            ],
            pltpu.VMEM((tokens, width), BF16),
            pltpu.VMEM((tokens, width), BF16),
            pltpu.VMEM((tokens, width), BF16),
            pltpu.VMEM((tokens, width), BF16),
            pltpu.VMEM((tokens, part_q), F32),
            pltpu.VMEM((tokens, part_k), F32),
            pltpu.VMEM((group, tokens, 1), F32),
            pltpu.VMEM((1, tokens, 1), F32),
            pltpu.VMEM((tokens, part_q), BF16),
            pltpu.VMEM((tokens, part_k), BF16),
            pltpu.VMEM((tokens, part_k), BF16),
            pltpu.VMEM((tokens, part_q), BF16),
            pltpu.VMEM((group, tokens, 1), F32),
            pltpu.VMEM((tokens, part_f), BF16),
            pltpu.VMEM((tokens, part_f), BF16),
            pltpu.VMEM((tokens, part_f), BF16),
            pltpu.VMEM((tokens, part_q), BF16),
            pltpu.VMEM((tokens, part_q + 2 * part_k), BF16),
            pltpu.VMEM((2, tokens, width), F32),
            pltpu.VMEM((2, tokens, half), F32),
            pltpu.VMEM((2, tokens, half), F32),
            pltpu.VMEM((2, 6, rows, half // 2), F32),
            pltpu.VMEM((rows, half), F32),
            pltpu.VMEM((rows, half), F32),
            pltpu.VMEM((3, rows, HD), F32),
            pltpu.VMEM((3, rows, HD), F32),
            pltpu.VMEM((8, width), F32),
            pltpu.VMEM((8, 8, width), F32),
            pltpu.SemaphoreType.DMA((copies,)),
            pltpu.SemaphoreType.DMA((copies,)),
            pltpu.SemaphoreType.DMA((14,)),
        ],
        compiler_params=pltpu.CompilerParams(
            collective_id=0, has_side_effects=True, vmem_limit_bytes=63 * 1024 * 1024
        ),
        cost_estimate=pl.CostEstimate(
            flops=24 * tokens * width * (part_q + part_k + part_f),
            bytes_accessed=8 * width * width,
            transcendentals=0,
        ),
    )(
        block_input[0],
        cotangent[0],
        attn_gain[None],
        mlp_gain[None],
        query_gain[None],
        key_gain[None],
        cos_table,
        sin_table,
        *weights,
    )
    gains = results[2]
    moved = results[:2] + results[3:]
    share = HD // dp_size
    finished = pl.pallas_call(
        functools.partial(finish_kernel, share, owned, len(moved)),
        out_shape=(
            shape((1, owned), F32),
            shape((1, owned), F32),
            shape((1, share), F32),
            shape((1, share), F32),
        )
        + tuple(shape(array.shape, array.dtype) for array in moved),
        in_specs=[vmem] + [hbm] * len(moved),
        out_specs=(vmem,) * 4 + (hbm,) * len(moved),
        scratch_shapes=[
            [pltpu.VMEM(array.shape, array.dtype) for array in moved],
            pltpu.SemaphoreType.DMA((len(moved),)),
            pltpu.SemaphoreType.DMA((len(moved),)),
        ],
        compiler_params=pltpu.CompilerParams(vmem_limit_bytes=63 * 1024 * 1024),
    )(gains, *moved)
    attn_share, mlp_share, query_row, key_row = finished[:4]
    output, d_input, grad_q, grad_k, grad_v, grad_o, grad_g, grad_u, grad_d = finished[4:]
    return (
        output[None],
        d_input[None],
        attn_share[0],
        grad_q,
        grad_k,
        grad_v,
        query_row[0],
        key_row[0],
        grad_o,
        mlp_share[0],
        grad_g,
        grad_u,
        grad_d,
    )


def solution(mesh):
    sizes = dict(mesh.shape)
    body = per_device
    if sizes["ctx"] == 2 and sizes["tensor"] == 2 and sizes["dp"] in (2, 4, 8):
        body = functools.partial(fused_device, sizes["dp"])
    return jax.shard_map(
        body,
        mesh=mesh,
        in_specs=(
            P("dp", "ctx", None),
            P(),
            P("dp", "tensor"),
            P("dp", "tensor"),
            P("dp", "tensor"),
            P(),
            P(),
            P("tensor", "dp"),
            P(),
            P("dp", "tensor"),
            P("dp", "tensor"),
            P("tensor", "dp"),
            P("dp", "ctx", None),
        ),
        out_specs=(
            P("dp", "ctx", None),
            P("dp", "ctx", None),
            P("dp"),
            P("dp", "tensor"),
            P("dp", "tensor"),
            P("dp", "tensor"),
            P("dp"),
            P("dp"),
            P("tensor", "dp"),
            P("dp"),
            P("dp", "tensor"),
            P("dp", "tensor"),
            P("tensor", "dp"),
        ),
        check_vma=False,
    )
```

```python
import functools
import math

import jax
import jax.numpy as jnp
from jax import lax
from jax.experimental import pallas as pl
from jax.experimental.pallas import tpu as pltpu
from jax.sharding import PartitionSpec as P

HD = 128


EPS = 1e-06
THETA = 1000000.0
F32 = jnp.float32
BF16 = jnp.bfloat16


def rms_inverse(value):
    return lax.rsqrt(jnp.mean(value * value, axis=-1, keepdims=True) + EPS)


def norm_back(grad, unit, inverse, gain):
    scaled = grad * gain
    return inverse * (scaled - unit * jnp.mean(scaled * unit, axis=-1, keepdims=True))


def rotate(value):
    half_width = value.shape[-1] // 2
    return jnp.concatenate([-value[..., half_width:], value[..., :half_width]], axis=-1)


def rotate_back(value):
    half_width = value.shape[-1] // 2
    return jnp.concatenate([value[..., half_width:], -value[..., :half_width]], axis=-1)


def rope_tables(positions, width):
    half_width = width // 2
    exponent = jnp.arange(half_width).astype(F32) * (2.0 / width)
    frequency = jnp.power(THETA, -exponent)
    angle = positions.astype(F32)[:, None] * frequency[None, :]
    angle = jnp.concatenate([angle, angle], axis=-1)
    return (jnp.cos(angle), jnp.sin(angle))


def over_heads(partial_value):
    return lax.psum(partial_value, "tensor")


def per_device(
    block_input,
    attn_gain,
    query_weight,
    key_weight,
    value_weight,
    query_gain,
    key_gain,
    output_weight,
    mlp_gain,
    gate_weight,
    up_weight,
    down_weight,
    cotangent,
):
    tokens = block_input[0].astype(F32)
    row_count = tokens.shape[0]
    score_scale = 1.0 / math.sqrt(HD)
    positions = lax.axis_index("ctx") * row_count + jnp.arange(row_count, dtype=jnp.int32)
    cos_table, sin_table = rope_tables(positions, HD)
    cos_heads = cos_table[:, None, :]
    sin_heads = sin_table[:, None, :]
    w_query, w_key, w_value, w_out, w_gate, w_up, w_down = (
        lax.all_gather(query_weight, "dp", axis=0, tiled=True),
        lax.all_gather(key_weight, "dp", axis=0, tiled=True),
        lax.all_gather(value_weight, "dp", axis=0, tiled=True),
        lax.all_gather(output_weight, "dp", axis=1, tiled=True),
        lax.all_gather(gate_weight, "dp", axis=0, tiled=True),
        lax.all_gather(up_weight, "dp", axis=0, tiled=True),
        lax.all_gather(down_weight, "dp", axis=1, tiled=True),
    )
    q_heads = w_query.shape[1] // HD
    kv_heads = w_key.shape[1] // HD
    group_size = q_heads // kv_heads
    inv_one = rms_inverse(tokens)
    unit_one = tokens * inv_one
    normed_one = (unit_one * attn_gain).astype(BF16)
    query = jnp.dot(normed_one, w_query, preferred_element_type=F32).reshape(row_count, q_heads, HD)
    key_raw = jnp.dot(normed_one, w_key, preferred_element_type=F32).reshape(
        row_count, kv_heads, HD
    )
    value = (
        jnp.dot(normed_one, w_value, preferred_element_type=F32)
        .astype(BF16)
        .reshape(row_count, kv_heads, HD)
    )
    query_inv = rms_inverse(query)
    query_unit = query * query_inv
    query_scaled = query_unit * query_gain
    query_rot = (query_scaled * cos_heads + rotate(query_scaled) * sin_heads).astype(BF16)
    key_inv = rms_inverse(key_raw)
    key_unit = key_raw * key_inv
    key_scaled = key_unit * key_gain
    key_rot = (key_scaled * cos_heads + rotate(key_scaled) * sin_heads).astype(BF16)
    grouped_query = query_rot.reshape(row_count, kv_heads, group_size, HD)

    def piece_scores(piece_keys):
        piece_rows = piece_keys.shape[0]
        key_positions = jnp.arange(piece_rows, dtype=jnp.int32)
        allowed = key_positions[None, :] <= positions[:, None]
        scores = (
            jnp.einsum("qkgd,nkd->kgqn", grouped_query, piece_keys, preferred_element_type=F32)
            * score_scale
        )
        return jnp.where(allowed, scores, -jnp.inf)

    peak_old = jnp.full((kv_heads, group_size, row_count), -1e30, F32)
    piece_keys = lax.all_gather(key_rot, "ctx", axis=0, tiled=True)
    piece_values = lax.all_gather(value, "ctx", axis=0, tiled=True)
    scores = piece_scores(piece_keys)
    peak_new = jnp.maximum(peak_old, jnp.max(scores, axis=-1))
    expo = jnp.exp(scores - peak_new[..., None])
    total_new = jnp.sum(expo, axis=-1)
    accum_new = jnp.einsum(
        "kgqn,nkd->kgqd", expo.astype(BF16), piece_values, preferred_element_type=F32
    )
    log_total = peak_new + jnp.log(total_new)
    attn = (
        (accum_new / total_new[..., None])
        .astype(BF16)
        .transpose(2, 0, 1, 3)
        .reshape(row_count, q_heads * HD)
    )
    resid = tokens + over_heads(jnp.dot(attn, w_out, preferred_element_type=F32))
    inv_two = rms_inverse(resid)
    unit_two = resid * inv_two
    normed_two = (unit_two * mlp_gain).astype(BF16)
    gate = jnp.dot(normed_two, w_gate, preferred_element_type=F32)
    up_proj = jnp.dot(normed_two, w_up, preferred_element_type=F32)
    sigma = jax.nn.sigmoid(gate)
    silu_gate = gate * sigma
    hidden = (silu_gate * up_proj).astype(BF16)
    output = (resid + over_heads(jnp.dot(hidden, w_down, preferred_element_type=F32))).astype(BF16)
    w_query, w_key, w_value, w_out, w_gate, w_up, w_down = (
        lax.all_gather(query_weight, "dp", axis=0, tiled=True),
        lax.all_gather(key_weight, "dp", axis=0, tiled=True),
        lax.all_gather(value_weight, "dp", axis=0, tiled=True),
        lax.all_gather(output_weight, "dp", axis=1, tiled=True),
        lax.all_gather(gate_weight, "dp", axis=0, tiled=True),
        lax.all_gather(up_weight, "dp", axis=0, tiled=True),
        lax.all_gather(down_weight, "dp", axis=1, tiled=True),
    )
    d_output = cotangent[0]
    d_hidden = jnp.einsum("td,fd->tf", d_output, w_down, preferred_element_type=F32)
    grad_down = jnp.einsum("tf,td->fd", hidden, d_output, preferred_element_type=F32)
    d_gate = (d_hidden * up_proj * sigma * (1.0 + gate * (1.0 - sigma))).astype(BF16)
    d_up = (d_hidden * silu_gate).astype(BF16)
    grad_gate = jnp.einsum("td,tf->df", normed_two, d_gate, preferred_element_type=F32)
    grad_up = jnp.einsum("td,tf->df", normed_two, d_up, preferred_element_type=F32)
    partial_two = jnp.einsum("tf,df->td", d_gate, w_gate, preferred_element_type=F32) + jnp.einsum(
        "tf,df->td", d_up, w_up, preferred_element_type=F32
    )
    d_normed_two = lax.psum(partial_two, "tensor")
    grad_mlp_gain = jnp.sum(d_normed_two * unit_two, axis=0)
    d_resid = d_output.astype(F32) + norm_back(d_normed_two, unit_two, inv_two, mlp_gain)
    d_resid_b = d_resid.astype(BF16)
    grad_out = jnp.einsum("th,td->hd", attn, d_resid_b, preferred_element_type=F32)
    d_attn = jnp.einsum("td,hd->th", d_resid_b, w_out, preferred_element_type=F32).astype(BF16)
    delta = jnp.sum(
        d_attn.astype(F32).reshape(row_count, q_heads, HD)
        * attn.astype(F32).reshape(row_count, q_heads, HD),
        axis=-1,
    )
    delta_heads = delta.reshape(row_count, kv_heads, group_size).transpose(1, 2, 0)
    grouped_grad = d_attn.reshape(row_count, kv_heads, group_size, HD)
    piece_keys = lax.all_gather(key_rot, "ctx", axis=0, tiled=True)
    piece_values = lax.all_gather(value, "ctx", axis=0, tiled=True)
    piece_rows = piece_keys.shape[0]
    scores = piece_scores(piece_keys)
    probs = jnp.exp(scores - log_total[..., None])
    d_probs = jnp.einsum("qkgd,nkd->kgqn", grouped_grad, piece_values, preferred_element_type=F32)
    d_scores = (probs * (d_probs - delta_heads[..., None]) * score_scale).astype(BF16)
    d_query_acc = jnp.einsum("kgqn,nkd->kgqd", d_scores, piece_keys, preferred_element_type=F32)
    d_key_piece = jnp.einsum("kgqn,qkgd->nkd", d_scores, grouped_query, preferred_element_type=F32)
    d_value_piece = jnp.einsum(
        "kgqn,qkgd->nkd", probs.astype(BF16), grouped_grad, preferred_element_type=F32
    )
    update = jnp.stack([d_key_piece, d_value_piece])
    d_kv_home = lax.psum_scatter(update, "ctx", scatter_dimension=1, tiled=True)
    d_query_rot = d_query_acc.transpose(2, 0, 1, 3).reshape(row_count, q_heads, HD)
    d_key_rot = d_kv_home[0]
    d_value = d_kv_home[1].astype(BF16).reshape(row_count, kv_heads * HD)
    d_query_scaled = d_query_rot * cos_heads + rotate_back(d_query_rot * sin_heads)
    d_key_scaled = d_key_rot * cos_heads + rotate_back(d_key_rot * sin_heads)
    query_gain_part = jnp.sum(d_query_scaled * query_unit, axis=(0, 1))
    key_gain_part = jnp.sum(d_key_scaled * key_unit, axis=(0, 1))
    d_query = (
        norm_back(d_query_scaled, query_unit, query_inv, query_gain)
        .astype(BF16)
        .reshape(row_count, q_heads * HD)
    )
    d_key = (
        norm_back(d_key_scaled, key_unit, key_inv, key_gain)
        .astype(BF16)
        .reshape(row_count, kv_heads * HD)
    )
    grad_query = jnp.einsum("td,th->dh", normed_one, d_query, preferred_element_type=F32)
    grad_key = jnp.einsum("td,th->dh", normed_one, d_key, preferred_element_type=F32)
    grad_value = jnp.einsum("td,th->dh", normed_one, d_value, preferred_element_type=F32)
    partial_one = jnp.einsum("th,dh->td", d_query, w_query, preferred_element_type=F32)
    partial_one = partial_one + jnp.einsum("th,dh->td", d_key, w_key, preferred_element_type=F32)
    partial_one = partial_one + jnp.einsum(
        "th,dh->td", d_value, w_value, preferred_element_type=F32
    )
    d_normed_one, query_gain_heads, key_gain_heads = lax.psum(
        (partial_one, query_gain_part, key_gain_part), "tensor"
    )
    grad_attn_gain = jnp.sum(d_normed_one * unit_one, axis=0)
    d_input = (d_resid + norm_back(d_normed_one, unit_one, inv_one, attn_gain)).astype(BF16)
    (
        share_a,
        share_q,
        share_k,
        share_v,
        share_qg,
        share_kg,
        share_o,
        share_m,
        share_g,
        share_u,
        share_d,
    ) = (
        lax.psum_scatter(grad_attn_gain, "dp", scatter_dimension=0, tiled=True),
        lax.psum_scatter(grad_query, "dp", scatter_dimension=0, tiled=True),
        lax.psum_scatter(grad_key, "dp", scatter_dimension=0, tiled=True),
        lax.psum_scatter(grad_value, "dp", scatter_dimension=0, tiled=True),
        lax.psum_scatter(query_gain_heads, "dp", scatter_dimension=0, tiled=True),
        lax.psum_scatter(key_gain_heads, "dp", scatter_dimension=0, tiled=True),
        lax.psum_scatter(grad_out, "dp", scatter_dimension=1, tiled=True),
        lax.psum_scatter(grad_mlp_gain, "dp", scatter_dimension=0, tiled=True),
        lax.psum_scatter(grad_gate, "dp", scatter_dimension=0, tiled=True),
        lax.psum_scatter(grad_up, "dp", scatter_dimension=0, tiled=True),
        lax.psum_scatter(grad_down, "dp", scatter_dimension=1, tiled=True),
    )
    finals = lax.psum(
        (
            share_a,
            share_q,
            share_k,
            share_v,
            share_qg,
            share_kg,
            share_o,
            share_m,
            share_g,
            share_u,
            share_d,
        ),
        "ctx",
    )
    return (
        output[None],
        d_input[None],
        finals[0],
        finals[1],
        finals[2],
        finals[3],
        finals[4],
        finals[5],
        finals[6],
        finals[7],
        finals[8],
        finals[9],
        finals[10],
    )


MESH = pl.DeviceIdType.MESH


def mm(a, b):
    return lax.dot_general(a, b, (((1,), (0,)), ((), ())), preferred_element_type=F32)


def mm_nt(a, b):
    return lax.dot_general(a, b, (((1,), (1,)), ((), ())), preferred_element_type=F32)


def mm_tn(a, b):
    return lax.dot_general(a, b, (((0,), (0,)), ((), ())), preferred_element_type=F32)


def layer_kernel(
    sizes,
    x_ref,
    dy_ref,
    attn_gain_ref,
    mlp_gain_ref,
    query_gain_ref,
    key_gain_ref,
    cos_ref,
    sin_ref,
    q_in,
    k_in,
    v_in,
    o_in,
    g_in,
    u_in,
    d_in,
    out_ref,
    d_input_ref,
    gains_ref,
    q_out,
    k_out,
    v_out,
    o_out,
    g_out,
    u_out,
    d_out,
    wq,
    wk,
    wv,
    wo,
    wg,
    wu,
    wd,
    grads,
    h1,
    dy_all,
    h2,
    drb,
    uq,
    uk,
    invq,
    invk,
    qr,
    kr,
    vr,
    attn,
    lse,
    hidden,
    d_gate,
    d_up,
    d_attn,
    d_qkv,
    partial,
    landing,
    acc,
    arrived,
    resid,
    d_resid,
    stat,
    stat_in,
    gains,
    gains_in,
    send_sem,
    recv_sem,
    local_sem,
):
    dp_size, rows, width, part_q, part_k, part_f = sizes
    owned = width // dp_size
    half = width // 2
    length = 2 * rows
    group = part_q // part_k
    score_scale = 1.0 / math.sqrt(HD)
    dp = lax.axis_index("dp")
    block = lax.axis_index("ctx")
    core = lax.axis_index("tensor")
    side = lax.rem(dp, 2)
    line = dp // 2
    lines = dp_size // 2
    mine = 2 * block + side

    def flip(value, bits):
        result = value
        bit = 1
        while bit <= bits:
            if bits & bit:
                result = result + bit * (1 - 2 * lax.rem(value // bit, 2))
            bit *= 2
        return result

    def at_dp(bits):
        return {"dp": flip(dp, bits), "ctx": block, "tensor": core}

    to_core = {"dp": dp, "ctx": block, "tensor": 1 - core}
    to_ctx = {"dp": dp, "ctx": 1 - block, "tensor": core}
    to_pair = at_dp(1)
    to_diagonal = {"dp": flip(dp, 1), "ctx": 1 - block, "tensor": core}
    slots = {1: to_ctx, 2: to_pair, 3: to_diagonal}

    barrier = pltpu.get_barrier_semaphore()
    peers = [to_core, to_ctx, to_diagonal] + [at_dp(bits) for bits in range(1, dp_size)]
    for peer in peers:
        pl.semaphore_signal(barrier, inc=1, device_id=peer, device_id_type=MESH)
    pl.semaphore_wait(barrier, len(peers))

    count = {"remote": 0, "local": 0}
    unsent = []
    own_copies = []

    def remote(src, dst, device):
        i = count["remote"]
        count["remote"] += 1
        copy = pltpu.make_async_remote_copy(
            src_ref=src,
            dst_ref=dst,
            send_sem=send_sem.at[i],
            recv_sem=recv_sem.at[i],
            device_id=device,
            device_id_type=MESH,
        )
        copy.start()
        unsent.append(copy)
        return copy

    def wait_sent(copy):
        copy.wait_send()
        unsent[:] = [other for other in unsent if other is not copy]

    def local(src, dst):
        i = count["local"]
        count["local"] += 1
        copy = pltpu.make_async_copy(src, dst, local_sem.at[i])
        copy.start()
        return copy

    def lanes(start, size):
        return pl.ds(pl.multiple_of(start, 128), size)

    def lines_of(start, size):
        return pl.ds(pl.multiple_of(start, 128), size)

    mine_half = lanes(core * half, half)
    other_half = lanes((1 - core) * half, half)

    def rows_of(slot):
        return pl.ds(slot * rows, rows)

    def shard_part(shard, by_rows, part, which):
        if by_rows:
            return shard.at[lines_of(which * part, part), :]
        return shard.at[:, lanes(which * part, part)]

    def owner_block(whole, by_rows, owner):
        if by_rows:
            return whole.at[:, lanes(owner * owned, owned)]
        return whole.at[lines_of(owner * owned, owned), :]

    span = 2 * owned

    def line_block(whole, by_rows, at):
        if by_rows:
            return whole.at[:, lanes(at * span, span)]
        return whole.at[lines_of(at * span, span), :]

    def weight_pair(shard, whole, by_rows, part):
        place = owner_block(whole, by_rows, dp)
        own = local(shard_part(shard, by_rows, part, mine), place)
        pair = remote(shard_part(shard, by_rows, part, 2 * block + 1 - side), place, to_pair)
        return whole, by_rows, own, pair

    def weight_first(handles):
        whole, by_rows, own, pair = handles
        own.wait()
        pair.wait_recv()
        place = line_block(whole, by_rows, line)
        cross = remote(place, place, at_dp(4)) if lines > 2 else None
        near = remote(place, place, at_dp(2)) if lines > 1 else None
        return whole, by_rows, near, cross

    def weight_second(handles):
        whole, by_rows, near, cross = handles
        found = [near] if lines > 1 else []
        if cross is not None:
            cross.wait_recv()
            place = line_block(whole, by_rows, flip(line, 2))
            found.append(remote(place, place, at_dp(2)))
        return found

    def weight_end(found):
        for copy in found:
            copy.wait_recv()

    def gather_start(buffer, with_core):
        own = buffer.at[rows_of(0), mine_half]
        first = remote(own, own, to_core) if with_core else None
        parts = {
            slot: remote(own, buffer.at[rows_of(slot), mine_half], slots[slot])
            for slot in (1, 2, 3)
        }
        return buffer, first, parts

    def gather_near(handles):
        buffer, first, parts = handles
        if first is not None:
            first.wait_recv()

    def gather_pass(handles, slot):
        buffer, first, parts = handles
        parts[slot].wait_recv()
        place = buffer.at[rows_of(slot), mine_half]
        return remote(place, place, to_core)

    def gather_end(handles):
        gather_near(handles)
        for copy in [gather_pass(handles, slot) for slot in (1, 2, 3)]:
            copy.wait_recv()

    order = (3, 2, 1, 0)

    def scatter_start(which, compute, copies, some=order):
        for slot in some:
            partial[which, rows_of(slot), :] = compute(rows_of(slot))
            copies[slot] = remote(
                partial.at[which, rows_of(slot), other_half],
                landing.at[which, rows_of(slot), :],
                to_core,
            )
        return copies

    quad = half // 2
    low, high = slice(0, quad), slice(quad, half)

    def scatter_middle(which, copies):
        def near_sum(slot):
            copies[slot].wait_recv()
            acc[which, rows_of(slot), :] = (
                partial[which, rows_of(slot), mine_half] + landing[which, rows_of(slot), :]
            )

        def forward(slot, part, place, device):
            return remote(acc.at[which, rows_of(slot), part], arrived.at[which, place], device)

        near_sum(3)
        relay_low = forward(3, low, 0, to_ctx)
        relay_high = forward(3, high, 1, to_pair)
        near_sum(2)
        sent = [forward(2, high, 3, to_pair)]
        near_sum(1)
        sent.append(forward(1, low, 2, to_ctx))
        near_sum(0)
        return copies, relay_low, relay_high, sent, forward

    def scatter_relay(which, handles):
        copies, relay_low, relay_high, sent, forward = handles
        relay_low.wait_recv()
        acc[which, rows_of(2), low] = acc[which, rows_of(2), low] + arrived[which, 0]
        sent.append(forward(2, low, 4, to_pair))
        relay_high.wait_recv()
        acc[which, rows_of(1), high] = acc[which, rows_of(1), high] + arrived[which, 1]
        sent.append(forward(1, high, 5, to_ctx))
        return list(copies.values()) + [relay_low, relay_high] + sent, sent

    def scatter_end(which, handles):
        copies, sent = handles
        for copy in sent:
            copy.wait_recv()
        own = acc[which, rows_of(0), :]
        total = jnp.concatenate(
            [
                own[:, low] + (arrived[which, 2] + arrived[which, 4]),
                own[:, high] + (arrived[which, 3] + arrived[which, 5]),
            ],
            axis=1,
        )
        for copy in copies:
            wait_sent(copy)
        return total

    def core_sum(which, value):
        stat[which] = jnp.broadcast_to(value, stat.shape[1:])
        copy = remote(stat.at[which], stat_in.at[which], to_core)
        copy.wait_recv()
        return value + stat_in[which][:, :1]

    firsts = [(q_in, wq, False, part_q), (k_in, wk, False, part_k), (v_in, wv, False, part_k)]
    firsts = [weight_pair(*each) for each in firsts]
    weight_o = weight_pair(o_in, wo, True, part_q)
    weight_g = weight_pair(g_in, wg, False, part_f)
    weight_u = weight_pair(u_in, wu, False, part_f)
    weight_d = weight_pair(d_in, wd, True, part_f)
    tokens = x_ref[...].astype(F32)
    inv_one = lax.rsqrt(jnp.mean(tokens * tokens, axis=-1, keepdims=True) + EPS)
    h1[rows_of(0), :] = (tokens * inv_one * attn_gain_ref[...]).astype(BF16)
    gather_one = gather_start(h1, False)
    firsts = [weight_first(handles) for handles in firsts]
    gains[...] = jnp.zeros_like(gains)
    dy_all[rows_of(0), :] = dy_ref[...]
    firsts = [weight_second(handles) for handles in firsts]
    weight_o = weight_first(weight_o)
    weight_g = weight_first(weight_g)
    weight_u = weight_first(weight_u)
    weight_d = weight_first(weight_d)
    gather_end(gather_one)
    for found in firsts:
        weight_end(found)
    gather_dy = gather_start(dy_all, False)

    def project(slot, carry):
        here = pl.ds(pl.multiple_of(slot * rows, rows), rows)
        table = pl.ds(pl.multiple_of(lax.rem(slot, 2) * rows, rows), rows)
        cos, sin = cos_ref[table, :], sin_ref[table, :]
        normed = h1[here, :]

        def head(raw, gain, unit_ref, inverse_ref, rot_ref, at):
            inverse = lax.rsqrt(jnp.mean(raw * raw, axis=-1, keepdims=True) + EPS)
            unit = raw * inverse
            scaled = unit * gain
            turned = scaled * cos + pltpu.roll(scaled, HD // 2, 1) * sin
            unit_ref[here, at * HD : (at + 1) * HD] = unit
            inverse_ref[at, here, :] = inverse
            rot_ref[here, at * HD : (at + 1) * HD] = turned.astype(BF16)

        query = mm(normed, wq[...])
        for at in range(group):
            raw = query[:, at * HD : (at + 1) * HD]
            head(raw, query_gain_ref[...], uq, invq, qr, at)
        head(mm(normed, wk[...]), key_gain_ref[...], uk, invk, kr, 0)
        vr[here, :] = mm(normed, wv[...]).astype(BF16)
        return carry

    lax.fori_loop(0, 4, project, 0)
    weight_o = weight_second(weight_o)

    def masked_scores(query, key):
        at_row = lax.broadcasted_iota(jnp.int32, (length, length), 0)
        at_column = lax.broadcasted_iota(jnp.int32, (length, length), 1)
        shift = block * rows
        row = jnp.where(at_row < rows, at_row + shift, at_row - shift)
        column = jnp.where(at_column < rows, at_column + shift, at_column - shift)
        return jnp.where(column <= row, mm_nt(query, key) * score_scale, -jnp.inf)

    def attend(seq, carry):
        here = pl.ds(pl.multiple_of(seq * length, length), length)
        key, value = kr[here, :], vr[here, :]
        for at in range(group):
            columns = slice(at * HD, (at + 1) * HD)
            scores = masked_scores(qr[here, columns], key)
            peak = jnp.max(scores, axis=-1, keepdims=True)
            expo = jnp.exp(scores - peak)
            total = jnp.sum(expo, axis=-1, keepdims=True)
            mixed = mm(expo.astype(BF16), value) / total
            attn[here, columns] = mixed.astype(BF16)
            lse[at, here, :] = peak + jnp.log(total)
        return carry

    def attend_once(seq):
        lax.fori_loop(seq, seq + 1, attend, 0)

    attend_once(1)
    weight_g = weight_second(weight_g)
    weight_end(weight_o)
    def project_out(here):
        return mm(attn[here, :], wo[...])

    first = scatter_start(0, project_out, {}, (3, 2))
    attend_once(0)
    first = scatter_start(0, project_out, first, (1, 0))
    middle = scatter_middle(0, first)
    gather_end(gather_dy)
    middle = scatter_relay(0, middle)
    weight_u = weight_second(weight_u)
    resid_half = x_ref[:, mine_half].astype(F32) + scatter_end(0, middle)
    resid[...] = resid_half
    square = core_sum(0, jnp.sum(resid_half * resid_half, axis=-1, keepdims=True))
    inv_two = lax.rsqrt(square / width + EPS)
    unit_two = resid_half * inv_two
    h2[rows_of(0), mine_half] = (unit_two * mlp_gain_ref[:, mine_half]).astype(BF16)
    gather_two = gather_start(h2, True)
    weight_d = weight_second(weight_d)
    weight_end(weight_g)
    weight_end(weight_u)
    weight_end(weight_d)

    def feed(slot):
        here = rows_of(slot)
        normed = h2[here, :]
        gated, raised = mm(normed, wg[...]), mm(normed, wu[...])
        d_hidden = mm_nt(dy_all[here, :], wd[...])
        sigma = jax.nn.sigmoid(gated)
        silu_gate = gated * sigma
        hidden[here, :] = (silu_gate * raised).astype(BF16)
        d_gate[here, :] = (d_hidden * raised * sigma * (1.0 + gated * (1.0 - sigma))).astype(BF16)
        d_up[here, :] = (d_hidden * silu_gate).astype(BF16)

    gather_near(gather_two)
    feed(0)
    passed = [gather_pass(gather_two, slot) for slot in (1, 2)]
    passed[0].wait_recv()
    feed(1)
    passed.append(gather_pass(gather_two, 3))
    passed[1].wait_recv()
    feed(2)
    passed[2].wait_recv()
    feed(3)

    def feed_back(here):
        return mm_nt(d_gate[here, :], wg[...]) + mm_nt(d_up[here, :], wu[...])

    first = scatter_start(0, feed_back, {})
    middle = scatter_middle(0, first)

    def line_far(grad, by_rows, out, part, features, columns):
        own, cross, rounded, land, found, leaving = grad

        def block_grad(at):
            place = lanes(at * span, span)
            if by_rows:
                return mm_tn(columns[...], features[:, place])
            return mm_tn(features[:, place], columns[...])

        far = None
        if lines > 2:
            rounded[0] = block_grad(flip(line, 3)).astype(rounded.dtype)
            far = remote(rounded.at[0], land.at[0], at_dp(2))
        return grad, by_rows, out, part, far, block_grad

    def line_first(handles):
        grad, by_rows, out, part, far, block_grad = handles
        own, cross, rounded, land, found, leaving = grad
        if lines > 2:
            cross[...] = block_grad(flip(line, 2))
        if lines > 1:
            rounded[1] = block_grad(flip(line, 1)).astype(rounded.dtype)
        own[...] = block_grad(line)
        return grad, by_rows, out, part, far

    def line_second(handles):
        grad, by_rows, out, part, far = handles
        own, cross, rounded, land, found, leaving = grad
        sent = near = None
        if far is not None:
            far.wait_recv()
            leaving[...] = (cross[...] + land[0].astype(F32)).astype(leaving.dtype)
            sent = remote(leaving, found, at_dp(4))
        if lines > 1:
            near = remote(rounded.at[1], land.at[1], at_dp(2))
        return grad, by_rows, out, part, near, sent

    def line_third(handles):
        grad, by_rows, out, part, near, sent = handles
        own, cross, rounded, land, found, leaving = grad
        if near is not None:
            near.wait_recv()
            own[...] = own[...] + land[1].astype(F32)
        if sent is not None:
            sent.wait_recv()
            own[...] = own[...] + found[...].astype(F32)
        near_part = owner_block(own, by_rows, side)
        away_part = owner_block(own, by_rows, 1 - side)
        target = shard_part(out, by_rows, part, mine)
        own_copies.append(local(near_part, target))
        return [
            remote(away_part, target, to_diagonal),
            remote(near_part, target, to_ctx),
            remote(away_part, target, to_pair),
        ]

    grad_q, grad_k, grad_v, grad_o, grad_g, grad_u, grad_d = grads
    line_d = line_far(grad_d, True, d_out, part_f, dy_all, hidden)
    line_g = line_far(grad_g, False, g_out, part_f, h2, d_gate)
    line_u = line_far(grad_u, False, u_out, part_f, h2, d_up)

    line_d = line_first(line_d)
    line_g = line_first(line_g)
    line_d = line_second(line_d)
    middle = scatter_relay(0, middle)
    line_u = line_first(line_u)
    line_g = line_second(line_g)
    line_u = line_second(line_u)
    d_normed = scatter_end(0, middle)
    unit_two = resid[...] * inv_two
    gains[1:2, mine_half] = jnp.sum(d_normed * unit_two, axis=0, keepdims=True)
    scaled = d_normed * mlp_gain_ref[:, mine_half]
    dot = core_sum(1, jnp.sum(scaled * unit_two, axis=-1, keepdims=True))
    d_resid_half = dy_ref[:, mine_half].astype(F32) + inv_two * (scaled - unit_two * (dot / width))
    d_resid[...] = d_resid_half
    drb[rows_of(0), mine_half] = d_resid_half.astype(BF16)
    gather_drb = gather_start(drb, True)
    output_first = scatter_start(1, lambda here: mm(hidden[here, :], wd[...]), {})

    def d_attend(slot):
        here = rows_of(slot)
        d_attn[here, :] = mm_nt(drb[here, :], wo[...]).astype(BF16)

    gather_near(gather_drb)
    d_attend(0)
    passed = [gather_pass(gather_drb, slot) for slot in (1, 2)]
    passed[0].wait_recv()
    d_attend(1)
    passed.append(gather_pass(gather_drb, 3))

    def attend_back(seq, carry):
        here = pl.ds(pl.multiple_of(seq * length, length), length)
        key, value = kr[here, :], vr[here, :]
        cos, sin = cos_ref[...], sin_ref[...]

        def unturn(d_rot):
            return d_rot * cos - pltpu.roll(d_rot, HD // 2, 1) * sin

        def norm_head(d_scaled, unit, inverse, gain):
            gained = d_scaled * gain
            mean = jnp.mean(gained * unit, axis=-1, keepdims=True)
            return (inverse * (gained - unit * mean)).astype(BF16)

        d_key = jnp.zeros((length, HD), F32)
        d_value = jnp.zeros((length, HD), F32)
        query_part, key_part = carry
        for at in range(group):
            columns = slice(at * HD, (at + 1) * HD)
            query, d_mixed = qr[here, columns], d_attn[here, columns]
            delta = jnp.sum(
                d_mixed.astype(F32) * attn[here, columns].astype(F32), axis=-1, keepdims=True
            )
            probs = jnp.exp(masked_scores(query, key) - lse[at, here, :])
            d_scores = (probs * (mm_nt(d_mixed, value) - delta) * score_scale).astype(BF16)
            d_scaled = unturn(mm(d_scores, key))
            unit = uq[here, columns]
            query_part = query_part + jnp.sum(d_scaled * unit, axis=0, keepdims=True)
            d_qkv[here, columns] = norm_head(
                d_scaled, unit, invq[at, here, :], query_gain_ref[...]
            )
            d_key = d_key + mm_tn(d_scores, query)
            d_value = d_value + mm_tn(probs.astype(BF16), d_mixed)
        d_scaled = unturn(d_key)
        unit = uk[here, :]
        key_part = key_part + jnp.sum(d_scaled * unit, axis=0, keepdims=True)
        d_qkv[here, part_q : part_q + part_k] = norm_head(
            d_scaled, unit, invk[0, here, :], key_gain_ref[...]
        )
        d_qkv[here, part_q + part_k : part_q + 2 * part_k] = d_value.astype(BF16)
        return query_part, key_part

    empty = jnp.zeros((1, HD), F32)
    gain_parts = lax.fori_loop(0, 1, attend_back, (empty, empty))
    passed[1].wait_recv()
    d_attend(2)
    passed[2].wait_recv()
    d_attend(3)
    line_o = line_far(grad_o, True, o_out, part_q, drb, attn)
    line_o = line_first(line_o)
    output_middle = scatter_middle(1, output_first)
    query_part, key_part = lax.fori_loop(1, 2, attend_back, gain_parts)
    output_middle = scatter_relay(1, output_middle)
    gains[2:3, 0:HD] = query_part
    gains[3:4, 0:HD] = key_part

    def columns_of(start, size):
        return d_qkv.at[:, start : start + size]

    line_q = line_far(grad_q, False, q_out, part_q, h1, columns_of(0, part_q))
    line_k = line_far(grad_k, False, k_out, part_k, h1, columns_of(part_q, part_k))
    line_v = line_far(grad_v, False, v_out, part_k, h1, columns_of(part_q + part_k, part_k))

    line_q = line_first(line_q)
    line_k = line_first(line_k)
    line_v = line_first(line_v)
    line_o = line_second(line_o)

    def d_project(here):
        d_query = d_qkv[here, 0:part_q]
        d_key = d_qkv[here, part_q : part_q + part_k]
        d_value = d_qkv[here, part_q + part_k : part_q + 2 * part_k]
        return mm_nt(d_query, wq[...]) + mm_nt(d_key, wk[...]) + mm_nt(d_value, wv[...])

    first = scatter_start(0, d_project, {})
    middle = scatter_middle(0, first)
    line_q = line_second(line_q)
    line_k = line_second(line_k)
    line_v = line_second(line_v)
    middle = scatter_relay(0, middle)
    spread = line_third(line_d)
    out_half = (resid[...] + scatter_end(1, output_middle)).astype(BF16)
    out_ref[:, mine_half] = out_half
    out_copy = remote(out_ref.at[:, mine_half], out_ref.at[:, mine_half], to_core)
    spread += line_third(line_g)

    d_normed = scatter_end(0, middle)
    tokens_half = x_ref[:, mine_half].astype(F32)
    unit_one = tokens_half * inv_one
    gains[0:1, mine_half] = jnp.sum(d_normed * unit_one, axis=0, keepdims=True)
    scaled = d_normed * attn_gain_ref[:, mine_half]
    dot = core_sum(2, jnp.sum(scaled * unit_one, axis=-1, keepdims=True))
    d_input_half = d_resid[...] + inv_one * (scaled - unit_one * (dot / width))
    d_input_ref[:, mine_half] = d_input_half.astype(BF16)
    in_copy = remote(d_input_ref.at[:, mine_half], d_input_ref.at[:, mine_half], to_core)

    rounds = [to_core, to_ctx]
    stride = 1
    while stride < dp_size:
        rounds.append(at_dp(stride))
        stride *= 2
    later = [line_u, line_o, line_q, line_k, line_v]
    for i, device in enumerate(rounds):
        copy = remote(gains, gains_in.at[i], device)
        if later:
            spread += line_third(later.pop(0))
        copy.wait_recv()
        wait_sent(copy)
        gains[...] = gains[...] + gains_in[i]
    gains_ref[...] = gains[...]
    for handles in later:
        spread += line_third(handles)
    for copy in spread + [out_copy, in_copy]:
        copy.wait_recv()
    for copy in own_copies:
        copy.wait()
    for copy in unsent:
        copy.wait_send()


def finish_kernel(share, owned, count, *refs):
    gains_ref, sources = refs[0], refs[1 : 1 + count]
    attn_ref, mlp_ref, query_ref, key_ref = refs[1 + count : 5 + count]
    targets, rooms = refs[5 + count : 5 + 2 * count], refs[5 + 2 * count]
    in_sems, out_sems = refs[6 + 2 * count :]
    places = [(source, room, in_sems.at[i]) for i, (source, room) in enumerate(zip(sources, rooms))]
    moves = [pltpu.make_async_copy(*place) for place in places]
    for move in moves:
        move.start()
    owner = lax.axis_index("dp")
    place = pl.ds(pl.multiple_of(owner * owned, 128), owned)
    attn_ref[...] = gains_ref[0:1, place]
    mlp_ref[...] = gains_ref[1:2, place]
    shift = lax.rem(HD - owner * share, HD)
    query_ref[...] = pltpu.roll(gains_ref[2:3, 0:HD], shift, 1)[:, :share]
    key_ref[...] = pltpu.roll(gains_ref[3:4, 0:HD], shift, 1)[:, :share]
    written = []
    for i, move in enumerate(moves):
        move.wait()
        written.append(pltpu.make_async_copy(rooms[i], targets[i], out_sems.at[i]))
        written[i].start()
    for move in written:
        move.wait()


def fused_device(
    dp_size,
    block_input,
    attn_gain,
    query_weight,
    key_weight,
    value_weight,
    query_gain,
    key_gain,
    output_weight,
    mlp_gain,
    gate_weight,
    up_weight,
    down_weight,
    cotangent,
):
    rows, width = block_input.shape[1:]
    block = lax.axis_index("ctx")
    half = width // 2
    owned = width // dp_size
    part_q = query_weight.shape[1] // 4
    part_k = key_weight.shape[1] // 4
    part_f = gate_weight.shape[1] // 4
    span = 2 * owned
    tokens = 4 * rows
    index = jnp.arange(rows, dtype=jnp.int32)
    positions = jnp.concatenate([block * rows + index, (1 - block) * rows + index])
    cos_table, sin_table = rope_tables(positions, HD)
    sin_table = jnp.concatenate([-sin_table[:, : HD // 2], sin_table[:, HD // 2 :]], axis=1)
    vmem = pl.BlockSpec(memory_space=pltpu.VMEM)
    hbm = pl.BlockSpec(memory_space=pl.ANY)

    def shape(dims, kind):
        return jax.ShapeDtypeStruct(dims, kind)

    def grad_room(by_rows, part, wide=False):
        dims = (part, span) if by_rows else (span, part)
        early, late = (F32, BF16) if wide else (BF16, F32)
        return (
            pltpu.VMEM(dims, F32),
            pltpu.VMEM(dims, F32),
            pltpu.VMEM((2,) + dims, early),
            pltpu.VMEM((2,) + dims, early),
            pltpu.VMEM(dims, late),
            pltpu.VMEM(dims, late),
        )

    weights = (
        query_weight,
        key_weight,
        value_weight,
        output_weight,
        gate_weight,
        up_weight,
        down_weight,
    )
    group = part_q // part_k
    sizes = (dp_size, rows, width, part_q, part_k, part_f)
    copies = 7 * 4 + 4 * 7 + 4 * 10 + 3 + 7 * 6 + 2 + 8
    results = pl.pallas_call(
        functools.partial(layer_kernel, sizes),
        out_shape=(
            shape((rows, width), BF16),
            shape((rows, width), BF16),
            shape((8, width), F32),
        )
        + tuple(shape(weight.shape, F32) for weight in weights),
        in_specs=[vmem] * 8 + [hbm] * 7,
        out_specs=(vmem,) * 3 + (hbm,) * 7,
        scratch_shapes=[
            pltpu.VMEM((width, part_q), BF16),
            pltpu.VMEM((width, part_k), BF16),
            pltpu.VMEM((width, part_k), BF16),
            pltpu.VMEM((part_q, width), BF16),
            pltpu.VMEM((width, part_f), BF16),
            pltpu.VMEM((width, part_f), BF16),
            pltpu.VMEM((part_f, width), BF16),
            [
                grad_room(False, part_q),
                grad_room(False, part_k),
                grad_room(False, part_k),
                grad_room(True, part_q, True),
                grad_room(False, part_f),
                grad_room(False, part_f),
                grad_room(True, part_f),
            ],
            pltpu.VMEM((tokens, width), BF16),
            pltpu.VMEM((tokens, width), BF16),
            pltpu.VMEM((tokens, width), BF16),
            pltpu.VMEM((tokens, width), BF16),
            pltpu.VMEM((tokens, part_q), F32),
            pltpu.VMEM((tokens, part_k), F32),
            pltpu.VMEM((group, tokens, 1), F32),
            pltpu.VMEM((1, tokens, 1), F32),
            pltpu.VMEM((tokens, part_q), BF16),
            pltpu.VMEM((tokens, part_k), BF16),
            pltpu.VMEM((tokens, part_k), BF16),
            pltpu.VMEM((tokens, part_q), BF16),
            pltpu.VMEM((group, tokens, 1), F32),
            pltpu.VMEM((tokens, part_f), BF16),
            pltpu.VMEM((tokens, part_f), BF16),
            pltpu.VMEM((tokens, part_f), BF16),
            pltpu.VMEM((tokens, part_q), BF16),
            pltpu.VMEM((tokens, part_q + 2 * part_k), BF16),
            pltpu.VMEM((2, tokens, width), F32),
            pltpu.VMEM((2, tokens, half), F32),
            pltpu.VMEM((2, tokens, half), F32),
            pltpu.VMEM((2, 6, rows, half // 2), F32),
            pltpu.VMEM((rows, half), F32),
            pltpu.VMEM((rows, half), F32),
            pltpu.VMEM((3, rows, HD), F32),
            pltpu.VMEM((3, rows, HD), F32),
            pltpu.VMEM((8, width), F32),
            pltpu.VMEM((8, 8, width), F32),
            pltpu.SemaphoreType.DMA((copies,)),
            pltpu.SemaphoreType.DMA((copies,)),
            pltpu.SemaphoreType.DMA((14,)),
        ],
        compiler_params=pltpu.CompilerParams(
            collective_id=0, has_side_effects=True, vmem_limit_bytes=63 * 1024 * 1024
        ),
        cost_estimate=pl.CostEstimate(
            flops=24 * tokens * width * (part_q + part_k + part_f),
            bytes_accessed=8 * width * width,
            transcendentals=0,
        ),
    )(
        block_input[0],
        cotangent[0],
        attn_gain[None],
        mlp_gain[None],
        query_gain[None],
        key_gain[None],
        cos_table,
        sin_table,
        *weights,
    )
    gains = results[2]
    moved = results[:2] + results[3:]
    share = HD // dp_size
    finished = pl.pallas_call(
        functools.partial(finish_kernel, share, owned, len(moved)),
        out_shape=(
            shape((1, owned), F32),
            shape((1, owned), F32),
            shape((1, share), F32),
            shape((1, share), F32),
        )
        + tuple(shape(array.shape, array.dtype) for array in moved),
        in_specs=[vmem] + [hbm] * len(moved),
        out_specs=(vmem,) * 4 + (hbm,) * len(moved),
        scratch_shapes=[
            [pltpu.VMEM(array.shape, array.dtype) for array in moved],
            pltpu.SemaphoreType.DMA((len(moved),)),
            pltpu.SemaphoreType.DMA((len(moved),)),
        ],
        compiler_params=pltpu.CompilerParams(vmem_limit_bytes=63 * 1024 * 1024),
    )(gains, *moved)
    attn_share, mlp_share, query_row, key_row = finished[:4]
    output, d_input, grad_q, grad_k, grad_v, grad_o, grad_g, grad_u, grad_d = finished[4:]
    return (
        output[None],
        d_input[None],
        attn_share[0],
        grad_q,
        grad_k,
        grad_v,
        query_row[0],
        key_row[0],
        grad_o,
        mlp_share[0],
        grad_g,
        grad_u,
        grad_d,
    )


def solution(mesh):
    sizes = dict(mesh.shape)
    body = per_device
    if sizes["ctx"] == 2 and sizes["tensor"] == 2 and sizes["dp"] in (2, 4, 8):
        body = functools.partial(fused_device, sizes["dp"])
    return jax.shard_map(
        body,
        mesh=mesh,
        in_specs=(
            P("dp", "ctx", None),
            P(),
            P("dp", "tensor"),
            P("dp", "tensor"),
            P("dp", "tensor"),
            P(),
            P(),
            P("tensor", "dp"),
            P(),
            P("dp", "tensor"),
            P("dp", "tensor"),
            P("tensor", "dp"),
            P("dp", "ctx", None),
        ),
        out_specs=(
            P("dp", "ctx", None),
            P("dp", "ctx", None),
            P("dp"),
            P("dp", "tensor"),
            P("dp", "tensor"),
            P("dp", "tensor"),
            P("dp"),
            P("dp"),
            P("tensor", "dp"),
            P("dp"),
            P("dp", "tensor"),
            P("dp", "tensor"),
            P("tensor", "dp"),
        ),
        check_vma=False,
    )
```
